32 devices in a mesh: dp: 8 (over z, y), tensor: 4 (over x, core).
Axes of the slice: x: 2, y: 2, z: 4, core: 2. Of those that a mesh axis runs over, the one named last changes fastest.
Arguments:
- query_act: bfloat16 [8, 1024, 1024], P('dp', None, 'tensor'), may hold values from -6 to 6
- rotated_keys: bfloat16 [8, 1024, 256], P('dp'), may hold values from -6 to 6
- value_input: bfloat16 [8, 1024, 256], P('dp'), may hold values from -6 to 6
- grad_out: bfloat16 [8, 1024, 8192], P('dp', 'tensor'), may hold values from -6 to 6
- out_weight: bfloat16 [1024, 8192], P('tensor', 'dp'), may hold values from -0.1875 to 0.1875
- doc_lengths: int32 [8, 4], P('dp'), may hold values from 1 to 512, 1024 in all within a row
Outputs:
- query_grad: bfloat16 [8, 1024, 1024], P('dp', None, 'tensor')
- key_gradient: bfloat16 [8, 4, 512, 128], P('dp', 'tensor')
- value_gradient: bfloat16 [8, 4, 512, 128], P('dp', 'tensor')
- weight_grad: float32 [1024, 8192], P('tensor', 'dp')
The draws below stay inside these ranges and needn't reach their ends.
All inputs are finite; a program needn't handle non-finite values.
Results may differ from the reference program's by a relative error of at most 0.015.
The reference program's roundings to bfloat16 on the way count: a program that leaves them out, or rounds other values in their place, can miss the bound.
Values may be sent and summed in bfloat16 or wider, within the bound.
A program may use at most 128 MiB of HBM per device.

```python
import math
import jax
import jax.numpy as jnp
import numpy as np
from jax import lax

D = 8192
HEAD_SIZE = 128
SEQUENCE_TOKENS = 1024
NDOCS = 4
SEQUENCE_COUNT = 8
QUERY_HEADS = 8
KEY_VALUE_HEADS = 2


def draw_query_act(key, part):
    array_shape = (SEQUENCE_COUNT, SEQUENCE_TOKENS, QUERY_HEADS * HEAD_SIZE)
    drawn = jnp.clip(jax.random.normal(jax.random.fold_in(key, 1), array_shape, jnp.float32), -6.0, 6.0)
    return drawn.astype(jnp.bfloat16)


def draw_rotated_keys(key, part):
    array_shape = (SEQUENCE_COUNT, SEQUENCE_TOKENS, KEY_VALUE_HEADS * HEAD_SIZE)
    drawn = jnp.clip(jax.random.normal(jax.random.fold_in(key, 3), array_shape, jnp.float32), -6.0, 6.0)
    return drawn.astype(jnp.bfloat16)


def raised(values, key, source, target, parts, factor):
    def block_of(position):
        return (jnp.arange(values.shape[position]) // (values.shape[position] // parts)).reshape((-1,) + (1,) * (values.ndim - 1 - position))

    first = jax.random.permutation(key, parts)[block_of(target)]
    far = (block_of(target) + parts // 2) % parts
    return jnp.where((block_of(source) == first) | (block_of(source) == far), factor * values, values)


def shard_levels(own_key, dims, split, low, high):
    level, own = 1.0, jax.random.fold_in(own_key, 6)
    for dim, parts in split:
        draws = jnp.exp(jax.random.uniform(jax.random.fold_in(own, dim), (parts,), jnp.float32, low / len(split), high / len(split)))
        level = level * jnp.repeat(draws, dims[dim] // parts).reshape([-1 if axis == dim else 1 for axis in range(len(dims))])
    return level


def profile(number_of, total, bound, skew):
    weights = [(1 << 20) // math.isqrt(standing ** skew) + 1 for standing in range(2, number_of + 1)]
    rest, holding = total - bound - (number_of - 1), [1] * (number_of - 1)
    while rest > 0:
        candidates = [i for i in range(number_of - 1) if holding[i] < bound]
        mass, budget = sum([weights[i] for i in candidates]), rest
        for i in candidates:
            extra = min(bound - holding[i], max(1, budget * weights[i] // mass), rest)
            holding[i] = holding[i] + extra
            rest = rest - extra
    return np.array([bound] + holding)


def uneven(key, number_of, total, reach, slope):
    if number_of == 2:
        one = jax.random.randint(key, (), max(1, total - reach), min(reach, total - 1) + 1)
        return jnp.stack([one, total - one])
    tallies = jnp.asarray(profile(number_of, total, reach, slope), jnp.int32)
    pairs = (number_of - 1) // 2
    giver, taker = tallies[1:1 + 2 * pairs:2], tallies[2:2 + 2 * pairs:2]
    margin = jnp.minimum(giver - 1, reach - taker)
    shifted = jax.random.randint(jax.random.fold_in(key, 1), (pairs,), 0, 1 << 20) % (margin + 1)
    tallies = tallies.at[1:1 + 2 * pairs:2].set(giver - shifted).at[2:2 + 2 * pairs:2].set(taker + shifted)
    return tallies[jax.random.permutation(jax.random.fold_in(key, 2), number_of)]


def bell_draw(own_key, shape, deviation, limit, pieces=(), held_as=jnp.bfloat16):
    loudness = shard_levels(own_key, shape, pieces, -0.22, 0.18) if pieces else 1.0
    array = jax.random.normal(own_key, shape, jnp.float32) * deviation * loudness
    return jnp.minimum(jnp.maximum(array, -limit), limit).astype(held_as)


def gaussian_with(stream_key, dims, scale, bound, shards, heavy, kind=jnp.bfloat16):
    array = scale * jax.random.normal(stream_key, dims, jnp.float32)
    if shards:
        array = array * shard_levels(stream_key, dims, shards, -0.22, 0.18)
    return jnp.clip(raised(array, jax.random.fold_in(stream_key, 3), *heavy), -bound, bound).astype(kind)


def setup_inputs(seed: int = 0) -> dict:
    keys = jax.random.split(jax.random.key(seed), 7)
    query_act = draw_query_act(jax.random.fold_in(keys[6], 71), 0)
    rotated_keys = draw_rotated_keys(jax.random.fold_in(keys[6], 71), 0)
    value_input = bell_draw(keys[2], (SEQUENCE_COUNT, SEQUENCE_TOKENS, KEY_VALUE_HEADS * HEAD_SIZE), 1.0, 6.0, ((0, 8),))
    grad_out = gaussian_with(keys[3], (SEQUENCE_COUNT, SEQUENCE_TOKENS, D), 1.0, 6.0, ((0, 8), (1, 4)), (0, 2, 8, 2.0))
    out_weight = bell_draw(keys[4], (QUERY_HEADS * HEAD_SIZE, D), (QUERY_HEADS * HEAD_SIZE) ** -0.5, 0.1875, ((0, 4), (1, 8)))
    doc_lengths = jax.vmap(lambda own: uneven(own, NDOCS, SEQUENCE_TOKENS, SEQUENCE_TOKENS // 2, 2))(jax.random.split(keys[5], SEQUENCE_COUNT)).reshape((SEQUENCE_COUNT, NDOCS)).astype(jnp.int32)
    return dict(query_act=query_act, rotated_keys=rotated_keys, value_input=value_input, grad_out=grad_out, out_weight=out_weight, doc_lengths=doc_lengths)


def doc_mask(lengths):
    doc_ends = jnp.cumsum(lengths).astype(jnp.int32)
    positions = jnp.arange(SEQUENCE_TOKENS, dtype=jnp.int32)
    doc_ids = jnp.sum((positions[:, None] >= doc_ends[None, :]).astype(jnp.int32), axis=1)
    return (positions[None, :] <= positions[:, None]) & (doc_ids[:, None] == doc_ids[None, :])


def one_sequence(out_weight, sequence):
    query_act, rotated_keys, value_input, grad_out, lengths = sequence
    score_scale = HEAD_SIZE ** -0.5
    query_group_width = QUERY_HEADS // KEY_VALUE_HEADS
    allowed = doc_mask(lengths)
    query_float32 = query_act.astype(jnp.float32).reshape(SEQUENCE_TOKENS, QUERY_HEADS, HEAD_SIZE).transpose(1, 0, 2)
    key_float32 = jnp.repeat(rotated_keys.astype(jnp.float32).reshape(SEQUENCE_TOKENS, KEY_VALUE_HEADS, HEAD_SIZE).transpose(1, 0, 2), query_group_width, axis=0)
    value_float32 = jnp.repeat(value_input.astype(jnp.float32).reshape(SEQUENCE_TOKENS, KEY_VALUE_HEADS, HEAD_SIZE).transpose(1, 0, 2), query_group_width, axis=0)
    scores = jnp.einsum('hqd,hkd->hqk', query_float32, key_float32) * score_scale
    scores = jnp.where(allowed[None], scores, -jnp.inf)
    row_max = jnp.max(scores, axis=-1, keepdims=True)
    log_total = row_max + jnp.log(jnp.sum(jnp.exp(scores - row_max), axis=-1, keepdims=True))
    probs = jnp.exp(scores - log_total)
    probability_narrow = lax.optimization_barrier(probs.astype(jnp.bfloat16)).astype(jnp.float32)
    attn_out = jnp.einsum('hqk,hkd->hqd', probability_narrow, value_float32).astype(jnp.bfloat16)
    out_flat = attn_out.transpose(1, 0, 2).reshape(SEQUENCE_TOKENS, QUERY_HEADS * HEAD_SIZE)
    out_grad = jnp.dot(grad_out, out_weight.T, preferred_element_type=jnp.float32).astype(jnp.bfloat16)
    weight_part = jnp.dot(out_flat.T, grad_out, preferred_element_type=jnp.float32)
    gradient_float32 = lax.optimization_barrier(out_grad).astype(jnp.float32).reshape(SEQUENCE_TOKENS, QUERY_HEADS, HEAD_SIZE).transpose(1, 0, 2)
    out_f32 = lax.optimization_barrier(attn_out).astype(jnp.float32)
    dprobs = jnp.einsum('hqd,hkd->hqk', gradient_float32, value_float32)
    row_delta = jnp.sum(gradient_float32 * out_f32, axis=-1, keepdims=True)
    score_gradient = lax.optimization_barrier((probs * (dprobs - row_delta) * score_scale).astype(jnp.bfloat16)).astype(jnp.float32)
    query_grad = jnp.einsum('hqk,hkd->hqd', score_gradient, key_float32).astype(jnp.bfloat16)
    query_grad = query_grad.transpose(1, 0, 2).reshape(SEQUENCE_TOKENS, QUERY_HEADS * HEAD_SIZE)
    key_head_rows = jnp.einsum('auf,aur->afr', score_gradient, query_float32).reshape(KEY_VALUE_HEADS, query_group_width, SEQUENCE_TOKENS, HEAD_SIZE)
    value_head_rows = jnp.einsum('auf,aur->afr', probability_narrow, gradient_float32).reshape(KEY_VALUE_HEADS, query_group_width, SEQUENCE_TOKENS, HEAD_SIZE)
    key_gradient = jnp.sum(key_head_rows, axis=1).astype(jnp.bfloat16).reshape(2 * KEY_VALUE_HEADS, SEQUENCE_TOKENS // 2, HEAD_SIZE)
    value_gradient = jnp.sum(value_head_rows, axis=1).astype(jnp.bfloat16).reshape(2 * KEY_VALUE_HEADS, SEQUENCE_TOKENS // 2, HEAD_SIZE)
    return weight_part, (query_grad, key_gradient, value_gradient)


def reference(query_act, rotated_keys, value_input, grad_out, out_weight, doc_lengths):
    def scan_step(grad_sum, sequence):
        weight_part, others = one_sequence(out_weight, sequence)
        return grad_sum + weight_part, others

    initial = jnp.zeros((QUERY_HEADS * HEAD_SIZE, D), jnp.float32)
    weight_grad, stacked = lax.scan(scan_step, initial, (query_act, rotated_keys, value_input, grad_out, doc_lengths))
    query_grad, key_gradient, value_gradient = stacked
    return query_grad, key_gradient, value_gradient, weight_grad
```

```python
import functools

import jax
import jax.numpy as jnp
from jax import lax
from jax.experimental import pallas as pl
from jax.experimental.pallas import tpu as pltpu
from jax.sharding import PartitionSpec as P

HEAD_SIZE = 128


MESH = pl.DeviceIdType.MESH


def ring_place(index, count):
    odd = index % 2
    return (1 - odd) * (index // 2) + odd * (count - 1 - index // 2)


def ring_index(place, count):
    back = place // (count // 2)
    return (1 - back) * (2 * place) + back * (2 * (count - 1 - place) + 1)


def block_sizes(seq_len, tensor_count):
    forward_rows = min(256, seq_len)
    backward_rows = min(forward_rows, 2 * seq_len // tensor_count)
    return forward_rows, backward_rows, seq_len // 2 + forward_rows


def exchange_kernel(
    dp_count,
    tensor_count,
    grad_ref,
    weight_ref,
    query_full,
    key_full,
    value_full,
    lengths_ref,
    query_grad_out,
    key_grad_ref,
    value_grad_ref,
    weight_grad_out,
    grads,
    weights,
    sums_out,
    sums_in,
    accum,
    query_ref,
    key_ref,
    value_ref,
    query_grad_ref,
    weight_grad_ref,
    probs,
    probs_t,
    outs,
    outs_t,
    share_out,
    share_in,
    back_out,
    back_in,
    kv_grads,
    kv_in,
    own_sem,
    own_weight_sem,
    near_send,
    near_recv,
    far_send,
    far_recv,
    pass_send,
    pass_recv,
    mate_send,
    mate_recv,
    weight_send,
    weight_recv,
    sum_send,
    sum_recv,
    outs_send,
    outs_recv,
    share_send,
    share_recv,
    back_send,
    back_recv,
    kv_send,
    kv_recv,
    load_sem,
    query_sem,
    put_sem,
):
    dp_index = lax.axis_index("dp")
    tensor_index = lax.axis_index("tensor")
    chip_count = tensor_count // 2
    chip, core = tensor_index // 2, tensor_index % 2
    parity = chip % 2
    mate_chip = chip + 1 - 2 * parity
    mate = mate_chip * 2 + core
    partner = chip * 2 + 1 - core
    place = ring_place(dp_index, dp_count)
    ring = (
        ring_index((place + 1) % dp_count, dp_count),
        ring_index((place + dp_count - 1) % dp_count, dp_count),
    )
    rows = grad_ref.shape[0]
    depth, width = weight_ref.shape
    half, quarter = width // 2, width // 4
    last = dp_count - 1
    seq_len = query_full.shape[0]
    heads = depth // HEAD_SIZE
    half_rows = seq_len // 2
    score_scale = HEAD_SIZE ** (-0.5)
    lead = min(3, dp_count - 2)
    forward_rows, backward_rows, window = block_sizes(seq_len, tensor_count)
    chip_blocks = 2 * rows // backward_rows
    kv_columns = pl.ds(pl.multiple_of(tensor_index // 2 * HEAD_SIZE, HEAD_SIZE), HEAD_SIZE)
    far_chips = [(chip + away) % chip_count for away in range(1, chip_count)]
    slots = (slice(0, depth), slice(depth, 2 * depth))

    def place_rows(index):
        return pl.ds(pl.multiple_of(index * rows, rows), rows)

    def own_columns(whose, side):
        return pl.ds(pl.multiple_of(whose * half + side * quarter, quarter), quarter)

    def columns(side, step, whose):
        if side == 0:
            owner = ring_index((place + 2 * dp_count - 1 - step) % dp_count, dp_count)
        else:
            owner = ring_index((place + 1 + step) % dp_count, dp_count)
        return pl.ds(
            pl.multiple_of(owner * width + whose * half + side * quarter, quarter), quarter
        )

    def remote(source, target, send, recv, dp_to, tensor_to):
        return pltpu.make_async_remote_copy(
            source, target, send, recv, device_id=(dp_to, tensor_to), device_id_type=MESH
        )

    def own_copy(side, step):
        return pltpu.make_async_copy(
            grad_ref.at[:, columns(side, step, parity)],
            grads.at[side, step, place_rows(tensor_index)],
            own_sem.at[side, step],
        )

    def own_weight(side):
        return pltpu.make_async_copy(
            weight_ref.at[:, own_columns(parity, side)],
            weights.at[side, last, slots[0]],
            own_weight_sem.at[side],
        )

    def mate_weight(side):
        return remote(
            weight_ref.at[:, own_columns(1 - parity, side)],
            weights.at[side, last, slots[1]],
            mate_send.at[side],
            mate_recv.at[side],
            dp_index,
            mate,
        )

    def near_copy(side, step):
        return remote(
            grad_ref.at[:, columns(side, step, parity)],
            grads.at[side, step, place_rows(tensor_index)],
            near_send.at[side, step],
            near_recv.at[side, step],
            dp_index,
            partner,
        )

    def far_copy(away, side, step):
        return remote(
            grad_ref.at[:, columns(side, step, far_chips[away] % 2)],
            grads.at[side, step, place_rows(tensor_index)],
            far_send.at[away, side, step],
            far_recv.at[away, side, step],
            dp_index,
            far_chips[away] * 2 + core,
        )

    def pass_copy(away, side, step):
        source = (chip + chip_count - 1 - away) % chip_count * 2 + core
        block = grads.at[side, step, place_rows(source)]
        return remote(
            block,
            block,
            pass_send.at[away, side, step],
            pass_recv.at[away, side, step],
            dp_index,
            partner,
        )

    def weight_copy(side, hop, slot):
        if isinstance(hop, int) and hop == 0:
            if slot == 0:
                source = weight_ref.at[:, own_columns(parity, side)]
            else:
                source = weights.at[side, last, slots[1]]
        else:
            source = weights.at[side, hop - 1, slots[slot]]
        return remote(
            source,
            weights.at[side, hop, slots[slot]],
            weight_send.at[side, hop, slot],
            weight_recv.at[side, hop, slot],
            ring[side],
            tensor_index,
        )

    def sum_copy(side, step, slot):
        return remote(
            sums_out.at[side, step, slots[slot]],
            sums_in.at[side, step, slots[slot]],
            sum_send.at[side, step, slot],
            sum_recv.at[side, step, slot],
            ring[side],
            tensor_index,
        )

    def block_of(owner_chip, part):
        return owner_chip * chip_blocks + part

    def block_rows(block):
        return pl.ds(pl.multiple_of(block * backward_rows, backward_rows), backward_rows)

    def share_copy(block):
        return remote(
            share_out.at[block_rows(block)],
            share_in.at[block_rows(block)],
            share_send.at[block],
            share_recv.at[block],
            dp_index,
            mate,
        )

    def back_copy(side):
        return remote(
            back_out.at[side],
            back_in.at[side],
            back_send.at[side],
            back_recv.at[side],
            dp_index,
            mate,
        )

    outs_copy = remote(outs_t.at[0], outs_t.at[1], outs_send, outs_recv, dp_index, mate)
    kv_copy = remote(
        kv_grads.at[:, pl.ds(pl.multiple_of((1 - core) * half_rows, half_rows), half_rows)],
        kv_in,
        kv_send,
        kv_recv,
        dp_index,
        partner,
    )

    loads = [
        pltpu.make_async_copy(query_full, query_ref, load_sem.at[0]),
        pltpu.make_async_copy(key_full.at[:, kv_columns], key_ref, load_sem.at[1]),
        pltpu.make_async_copy(value_full.at[:, kv_columns], value_ref, load_sem.at[2]),
    ]
    for load in loads:
        load.start()

    targets = [(dp_index, partner), (ring[0], tensor_index), (ring[1], tensor_index)]
    targets += [(dp_index, other * 2 + core) for other in far_chips]
    barrier = pltpu.get_barrier_semaphore()
    for target in targets:
        pl.semaphore_signal(barrier, inc=1, device_id=target, device_id_type=MESH)
    pl.semaphore_wait(barrier, len(targets))

    def far_start(step):
        for side in (0, 1):
            for away in range(chip_count - 1):
                far_copy(away, side, step).start()

    for side in (0, 1):
        mate_weight(side).start()
        weight_copy(side, 0, 0).start()
        own_weight(side).start()
    far_start(0)
    far_start(1)

    @pl.loop(0, dp_count)
    def _(step):
        for side in (0, 1):
            near_copy(side, step).start()
            own_copy(side, step).start()

    accum[...] = jnp.zeros_like(accum)
    kv_grads[...] = jnp.zeros_like(kv_grads)
    nt = (((1,), (1,)), ((), ()))
    tn = (((0,), (0,)), ((), ()))

    def dot(left, right, dims):
        return lax.dot_general(left, right, dims, preferred_element_type=jnp.float32)

    def window_start(index):
        skip, total = half_rows // forward_rows, seq_len // forward_rows
        past = (index + total - skip) // total
        return past * (index - skip) * forward_rows

    def window_keys(index):
        return pl.ds(pl.multiple_of(window_start(index), forward_rows), window)

    def forward(index):
        here = pl.ds(pl.multiple_of(index * forward_rows, forward_rows), forward_rows)
        query_places = index * forward_rows + lax.broadcasted_iota(jnp.int32, (forward_rows, 1), 0)
        key_places = window_start(index) + lax.broadcasted_iota(
            jnp.int32, (forward_rows, window), 1
        )
        doc_start = jnp.zeros((forward_rows, 1), jnp.int32)
        doc_end = jnp.int32(0)
        for doc in range(lengths_ref.shape[1]):
            doc_end = doc_end + lengths_ref[0, doc]
            doc_start = jnp.where(query_places >= doc_end, doc_end, doc_start)
        allowed = (key_places >= doc_start) & (key_places <= query_places)
        keys, values = key_ref[window_keys(index)], value_ref[window_keys(index)]
        for head in range(heads):
            lanes = slice(head * HEAD_SIZE, (head + 1) * HEAD_SIZE)
            scores = dot(query_ref[here, lanes], keys, nt) * score_scale
            scores = jnp.where(allowed, scores, -jnp.inf)
            row_max = jnp.max(scores, axis=1, keepdims=True)
            total = jnp.sum(jnp.exp(scores - row_max), axis=1, keepdims=True)
            prob = jnp.exp(scores - (row_max + jnp.log(total)))
            probs[head, here] = prob
            out = jnp.dot(prob.astype(jnp.bfloat16), values, preferred_element_type=jnp.float32)
            outs[here, lanes] = out.astype(jnp.bfloat16)
            outs_t[0, lanes, here] = out.T.astype(jnp.bfloat16)
            for part in range(forward_rows // backward_rows):
                piece = prob[part * backward_rows : (part + 1) * backward_rows]
                block = index * (forward_rows // backward_rows) + part
                probs_t[head, block] = piece.T.astype(jnp.bfloat16)

    def query_put(block):
        here = block_rows(block)
        return pltpu.make_async_copy(
            query_grad_ref.at[here], query_grad_out.at[here], query_sem.at[block]
        )

    def backward(block):
        here = block_rows(block)
        index = block // (forward_rows // backward_rows)
        seen = window_keys(index)
        keys, values = key_ref[seen], value_ref[seen]
        share_copy(block).wait_recv()
        key_total, value_total = kv_grads[0, seen], kv_grads[1, seen]
        for head in range(heads):
            lanes = slice(head * HEAD_SIZE, (head + 1) * HEAD_SIZE)
            grad = (accum[here, lanes] + share_in[here, lanes].astype(jnp.float32)).astype(
                jnp.bfloat16
            )
            delta = jnp.sum(
                grad.astype(jnp.float32) * outs[here, lanes].astype(jnp.float32), axis=1, keepdims=True
            )
            dscore = probs[head, here] * (dot(grad, values, nt) - delta) * score_scale
            dscore = dscore.astype(jnp.bfloat16)
            query_grad_ref[here, lanes] = jnp.dot(
                dscore, keys, preferred_element_type=jnp.float32
            ).astype(jnp.bfloat16)
            key_total += dot(dscore, query_ref[here, lanes], tn)
            value_total += jnp.dot(probs_t[head, block], grad, preferred_element_type=jnp.float32)
        kv_grads[0, seen] = key_total
        kv_grads[1, seen] = value_total
        query_put(block).start()

    def chip_rows(owner_chip):
        return pl.ds(pl.multiple_of(owner_chip * (2 * rows), 2 * rows), 2 * rows)

    def project(owner_chip, steps):
        here = chip_rows(owner_chip)
        total = accum[here]
        for step in steps:
            for side in (0, 1):
                total += dot(grads[side, step, here], weights[side, step], nt)
        accum[here] = total

    def share(owner_chip):
        for part in range(chip_blocks):
            block = block_of(owner_chip, part)
            here = block_rows(block)
            share_out[here] = accum[here, slots[1]].astype(jnp.bfloat16)
            share_copy(block).start()

    def local_wait(step):
        for side in (0, 1):
            own_copy(side, step).wait()
            near_copy(side, step).wait_recv()

    def weight_step(hop, slot, send):
        for side in (0, 1):
            weight_copy(side, hop, slot).wait_recv()
            if send:
                weight_copy(side, hop + 1, slot).start()

    def far_pass(step):
        for side in (0, 1):
            for away in range(chip_count - 1):
                far_copy(away, side, step).wait_recv()
                pass_copy(away, side, step).start()

    def pass_wait(step):
        for side in (0, 1):
            for away in range(chip_count - 1):
                pass_copy(away, side, step).wait_recv()

    def sum_part(slot, side, step):
        return jnp.dot(outs_t[slot], grads[side, step], preferred_element_type=jnp.float32)

    def sum_step(slot, step, first=False):
        for side in (0, 1):
            part = sum_part(slot, side, step)
            if not first:
                sum_copy(side, step - 1, slot).wait_recv()
                part = part + sums_in[side, step - 1, slots[slot]].astype(jnp.float32)
            sums_out[side, step, slots[slot]] = part.astype(jnp.bfloat16)
            sum_copy(side, step, slot).start()

    def sum_final(slot):
        for side in (0, 1):
            part = sum_part(slot, side, last)
            sum_copy(side, last - 1, slot).wait_recv()
            part = part + sums_in[side, last - 1, slots[slot]].astype(jnp.float32)
            if slot == 0:
                weight_grad_ref[0, :, side * quarter : (side + 1) * quarter] = part
            else:
                back_out[side] = part.astype(jnp.bfloat16)
                back_copy(side).start()

    def weight_put(which):
        whose = parity if which == 0 else 1 - parity
        to = pl.ds(pl.multiple_of(whose * half, half), half)
        return pltpu.make_async_copy(
            weight_grad_ref.at[which], weight_grad_out.at[:, to], put_sem.at[which]
        )

    for load in loads:
        load.wait()
    blocks = seq_len // forward_rows
    events = [
        lambda: weight_step(0, 0, True),
        lambda: [mate_weight(side).wait_recv() for side in (0, 1)]
        + [weight_copy(side, 0, 1).start() for side in (0, 1)],
        lambda: weight_step(1, 0, True),
    ]
    for index in range(blocks):
        forward(index)
        if index < len(events):
            events[index]()
    for event in events[blocks:]:
        event()
    outs_copy.start()

    @pl.loop(2, dp_count)
    def _(step):
        far_start(step)

    for side in (0, 1):
        own_weight(side).wait()
    weight_step(0, 1, True)
    local_wait(last)
    project(chip, [last])
    weight_step(1, 1, True)
    for step in range(2):
        local_wait(step)
    project(chip, [0, 1])
    for hop in range(2, lead):
        weight_step(hop, 0, hop < last - 1)
        weight_step(hop, 1, hop < last - 1)
        local_wait(hop)
        project(chip, [hop])
    far_pass(0)
    far_pass(1)
    outs_copy.wait_recv()
    pass_wait(0)
    sum_step(1, 0, True)

    def main_step(step, send):
        weight_step(step + lead, 0, send)
        weight_step(step + lead, 1, send)
        pass_wait(step + 1)
        sum_step(1, step + 1)
        if isinstance(step, int) and step == 0:
            sum_step(0, step, True)
        else:
            sum_step(0, step)
        local_wait(step + lead)
        project(chip, [step + lead])
        for other in far_chips:
            project(other, [step])
        far_pass(step + 2)

    steps = last - lead
    main_step(0, lead < last - 1)

    @pl.loop(1, steps - 1)
    def _(step):
        main_step(step, True)

    tail = steps - 1
    weight_step(last - 1, 0, False)
    weight_step(last - 1, 1, False)
    local_wait(last - 1)
    project(chip, [last - 1])
    share(chip)
    pass_wait(tail + 1)
    sum_step(1, tail + 1)
    sum_step(0, tail)
    for step in range(tail + 2, dp_count):
        far_pass(step)
    for other in far_chips:
        project(other, [tail, tail + 1])
    for step in range(tail + 2, dp_count):
        pass_wait(step)
    for other in far_chips:
        project(other, list(range(tail + 2, dp_count)))
        share(other)

    rest = list(range(tail + 2, last))
    order = [(mate_chip + away) % chip_count for away in range(chip_count)]
    pieces = [block_of(owner, part) for owner in order for part in range(chip_blocks)]
    per = -(-len(pieces) // max(len(rest), 1))
    for place_in, step in enumerate(rest):
        sum_step(1, step)
        sum_step(0, step - 1)
        for block in pieces[place_in * per : (place_in + 1) * per]:
            backward(block)
    for block in pieces[len(rest) * per :]:
        backward(block)
    kv_copy.start()
    sum_final(1)
    sum_step(0, last - 1)
    mine = pl.ds(pl.multiple_of(core * half_rows, half_rows), half_rows)
    kv_copy.wait()
    key_grad_ref[...] = (kv_grads[0, mine] + kv_in[0]).astype(jnp.bfloat16)
    value_grad_ref[...] = (kv_grads[1, mine] + kv_in[1]).astype(jnp.bfloat16)

    for side in (0, 1):
        mate_weight(side).wait_send()

    @pl.loop(0, dp_count)
    def _(step):
        for side in (0, 1):
            near_copy(side, step).wait_send()
            for away in range(chip_count - 1):
                far_copy(away, side, step).wait_send()
                pass_copy(away, side, step).wait_send()

    @pl.loop(0, tensor_count // 2 * chip_blocks)
    def _(block):
        share_copy(block).wait_send()
        query_put(block).wait()

    outs_copy.wait_send()
    sum_final(0)
    weight_put(0).start()
    for side in (0, 1):
        back_copy(side).wait_recv()
        weight_grad_ref[1, :, side * quarter : (side + 1) * quarter] = back_in[side].astype(
            jnp.float32
        )
    weight_put(1).start()

    for slot in (0, 1):
        for side in (0, 1):
            weight_copy(side, 0, slot).wait_send()
            sum_copy(side, 0, slot).wait_send()

    @pl.loop(1, dp_count - 1)
    def _(step):
        for slot in (0, 1):
            for side in (0, 1):
                weight_copy(side, step, slot).wait_send()
                sum_copy(side, step, slot).wait_send()

    for side in (0, 1):
        back_copy(side).wait_send()
    for which in (0, 1):
        weight_put(which).wait()


def finish_kernel(*refs):
    count = (len(refs) - 2) // 3
    sources, results, held = refs[:count], refs[count : 2 * count], refs[2 * count : 3 * count]
    in_sem, out_sem = refs[3 * count :]
    takes = [pltpu.make_async_copy(sources[i], held[i], in_sem.at[i]) for i in range(count)]
    puts = [pltpu.make_async_copy(held[i], results[i], out_sem.at[i]) for i in range(count)]
    for take in takes:
        take.start()
    for take, put in zip(takes, puts):
        take.wait()
        put.start()
    for put in puts:
        put.wait()


def finish(*values):
    anywhere = pl.BlockSpec(memory_space=pl.ANY)
    dma = pltpu.SemaphoreType.DMA
    return pl.pallas_call(
        finish_kernel,
        out_shape=tuple(jax.ShapeDtypeStruct(value.shape, value.dtype) for value in values),
        in_specs=[anywhere] * len(values),
        out_specs=(anywhere,) * len(values),
        scratch_shapes=[pltpu.VMEM(value.shape, value.dtype) for value in values]
        + [dma((len(values),)), dma((len(values),))],
        compiler_params=pltpu.CompilerParams(vmem_limit_bytes=62 * 1024 * 1024),
        name="finish",
    )(*values)


def shards(query_act, rotated_keys, value_input, grad_out, out_weight, doc_lengths):
    dp_count, tensor_count = lax.axis_size("dp"), lax.axis_size("tensor")
    chip_count = tensor_count // 2
    far = chip_count - 1
    seq_len = query_act.shape[1]
    depth, width = out_weight.shape
    half, quarter = width // 2, width // 4
    heads = depth // HEAD_SIZE
    forward_rows, backward_rows, window = block_sizes(seq_len, tensor_count)
    blocks = seq_len // backward_rows
    dma = pltpu.SemaphoreType.DMA
    vmem = pl.BlockSpec(memory_space=pltpu.VMEM)
    anywhere = pl.BlockSpec(memory_space=pl.ANY)
    kv_shape = jax.ShapeDtypeStruct((seq_len // 2, HEAD_SIZE), jnp.bfloat16)
    low, full = jnp.bfloat16, jnp.float32
    query_grad, key_grad, value_grad, weight_grad = pl.pallas_call(
        functools.partial(exchange_kernel, dp_count, tensor_count),
        out_shape=(
            jax.ShapeDtypeStruct((seq_len, depth), low),
            kv_shape,
            kv_shape,
            jax.ShapeDtypeStruct((depth, width), full),
        ),
        in_specs=[anywhere] * 5 + [pl.BlockSpec(memory_space=pltpu.SMEM)],
        out_specs=(anywhere, vmem, vmem, anywhere),
        scratch_shapes=[
            pltpu.VMEM((2, dp_count, seq_len, quarter), low),
            pltpu.VMEM((2, dp_count, 2 * depth, quarter), low),
            pltpu.VMEM((2, dp_count - 1, 2 * depth, quarter), low),
            pltpu.VMEM((2, dp_count - 1, 2 * depth, quarter), low),
            pltpu.VMEM((seq_len, 2 * depth), full),
            pltpu.VMEM((seq_len, depth), low),
            pltpu.VMEM((seq_len, HEAD_SIZE), low),
            pltpu.VMEM((seq_len, HEAD_SIZE), low),
            pltpu.VMEM((seq_len, depth), low),
            pltpu.VMEM((2, depth, half), full),
            pltpu.VMEM((heads, seq_len, window), full),
            pltpu.VMEM((heads, blocks, window, backward_rows), low),
            pltpu.VMEM((seq_len, depth), low),
            pltpu.VMEM((2, depth, seq_len), low),
            pltpu.VMEM((seq_len, depth), low),
            pltpu.VMEM((seq_len, depth), low),
            pltpu.VMEM((2, depth, quarter), low),
            pltpu.VMEM((2, depth, quarter), low),
            pltpu.VMEM((2, seq_len, HEAD_SIZE), full),
            pltpu.VMEM((2, seq_len // 2, HEAD_SIZE), full),
            dma((2, dp_count)),
            dma((2,)),
            dma((2, dp_count)),
            dma((2, dp_count)),
            dma((far, 2, dp_count)),
            dma((far, 2, dp_count)),
            dma((far, 2, dp_count)),
            dma((far, 2, dp_count)),
            dma((2,)),
            dma((2,)),
            dma((2, dp_count - 1, 2)),
            dma((2, dp_count - 1, 2)),
            dma((2, dp_count - 1, 2)),
            dma((2, dp_count - 1, 2)),
            dma,
            dma,
            dma((blocks,)),
            dma((blocks,)),
            dma((2,)),
            dma((2,)),
            dma,
            dma,
            dma((3,)),
            dma((blocks,)),
            dma((2,)),
        ],
        compiler_params=pltpu.CompilerParams(
            collective_id=0, has_side_effects=True, vmem_limit_bytes=60 * 1024 * 1024
        ),
        name="exchange",
    )(grad_out[0], out_weight, query_act[0], rotated_keys[0], value_input[0], doc_lengths)
    query_grad, key_grad, value_grad, weight_grad = finish(
        query_grad, key_grad, value_grad, weight_grad
    )
    return (query_grad[None], key_grad[None, None], value_grad[None, None], weight_grad)


def solution(mesh):
    placed = (
        P("dp", None, "tensor"),
        P("dp", None, None),
        P("dp", None, None),
        P("dp", "tensor", None),
        P("tensor", "dp"),
        P("dp", None),
    )
    return jax.shard_map(
        shards,
        mesh=mesh,
        in_specs=placed,
        out_specs=(
            P("dp", None, "tensor"),
            P("dp", "tensor", None, None),
            P("dp", "tensor", None, None),
            P("tensor", "dp"),
        ),
        check_vma=False,
    )
```

```python
import functools

import jax
import jax.numpy as jnp
from jax import lax
from jax.experimental import pallas as pl
from jax.experimental.pallas import tpu as pltpu
from jax.sharding import PartitionSpec as P

HEAD_SIZE = 128


MESH = pl.DeviceIdType.MESH


def ring_place(index, count):
    odd = index % 2
    return (1 - odd) * (index // 2) + odd * (count - 1 - index // 2)


def ring_index(place, count):
    back = place // (count // 2)
    return (1 - back) * (2 * place) + back * (2 * (count - 1 - place) + 1)


def block_sizes(seq_len, tensor_count):
    forward_rows = min(256, seq_len)
    backward_rows = min(forward_rows, 2 * seq_len // tensor_count)
    return forward_rows, backward_rows, seq_len // 2 + forward_rows


def exchange_kernel(
    dp_count,
    tensor_count,
    grad_ref,
    weight_ref,
    query_full,
    key_full,
    value_full,
    lengths_ref,
    query_grad_out,
    key_grad_out,
    value_grad_out,
    weight_grad_out,
    grads,
    weights,
    sums_out,
    sums_in,
    accum,
    query_ref,
    key_ref,
    value_ref,
    query_grad_ref,
    weight_grad_ref,
    probs,
    probs_t,
    outs,
    outs_t,
    share_out,
    share_in,
    back_out,
    back_in,
    kv_grads,
    kv_in,
    kv_done,
    own_sem,
    own_weight_sem,
    near_send,
    near_recv,
    far_send,
    far_recv,
    pass_send,
    pass_recv,
    mate_send,
    mate_recv,
    weight_send,
    weight_recv,
    sum_send,
    sum_recv,
    outs_send,
    outs_recv,
    share_send,
    share_recv,
    back_send,
    back_recv,
    kv_send,
    kv_recv,
    load_sem,
    query_sem,
    put_sem,
    kv_sem,
):
    dp_index = lax.axis_index("dp")
    tensor_index = lax.axis_index("tensor")
    chip_count = tensor_count // 2
    chip, core = tensor_index // 2, tensor_index % 2
    parity = chip % 2
    mate_chip = chip + 1 - 2 * parity
    mate = mate_chip * 2 + core
    partner = chip * 2 + 1 - core
    place = ring_place(dp_index, dp_count)
    ring = (
        ring_index((place + 1) % dp_count, dp_count),
        ring_index((place + dp_count - 1) % dp_count, dp_count),
    )
    rows = grad_ref.shape[0]
    depth, width = weight_ref.shape
    half, quarter = width // 2, width // 4
    last = dp_count - 1
    seq_len = query_full.shape[0]
    heads = depth // HEAD_SIZE
    half_rows = seq_len // 2
    score_scale = HEAD_SIZE ** (-0.5)
    lead = min(3, dp_count - 2)
    forward_rows, backward_rows, window = block_sizes(seq_len, tensor_count)
    chip_blocks = 2 * rows // backward_rows
    kv_columns = pl.ds(pl.multiple_of(tensor_index // 2 * HEAD_SIZE, HEAD_SIZE), HEAD_SIZE)
    far_chips = [(chip + away) % chip_count for away in range(1, chip_count)]
    slots = (slice(0, depth), slice(depth, 2 * depth))

    def place_rows(index):
        return pl.ds(pl.multiple_of(index * rows, rows), rows)

    def own_columns(whose, side):
        return pl.ds(pl.multiple_of(whose * half + side * quarter, quarter), quarter)

    def columns(side, step, whose):
        if side == 0:
            owner = ring_index((place + 2 * dp_count - 1 - step) % dp_count, dp_count)
        else:
            owner = ring_index((place + 1 + step) % dp_count, dp_count)
        return pl.ds(
            pl.multiple_of(owner * width + whose * half + side * quarter, quarter), quarter
        )

    def remote(source, target, send, recv, dp_to, tensor_to):
        return pltpu.make_async_remote_copy(
            source, target, send, recv, device_id=(dp_to, tensor_to), device_id_type=MESH
        )

    def own_copy(side, step):
        return pltpu.make_async_copy(
            grad_ref.at[:, columns(side, step, parity)],
            grads.at[side, step, place_rows(tensor_index)],
            own_sem,
        )

    def own_weight(side):
        return pltpu.make_async_copy(
            weight_ref.at[:, own_columns(parity, side)],
            weights.at[side, last, slots[0]],
            own_weight_sem,
        )

    def mate_weight(side):
        return remote(
            weight_ref.at[:, own_columns(1 - parity, side)],
            weights.at[side, last, slots[1]],
            mate_send,
            mate_recv.at[side],
            dp_index,
            mate,
        )

    def near_copy(side, step):
        return remote(
            grad_ref.at[:, columns(side, step, parity)],
            grads.at[side, step, place_rows(tensor_index)],
            near_send,
            near_recv,
            dp_index,
            partner,
        )

    def far_copy(away, side, step):
        return remote(
            grad_ref.at[:, columns(side, step, far_chips[away] % 2)],
            grads.at[side, step, place_rows(tensor_index)],
            far_send.at[away],
            far_recv.at[away, step],
            dp_index,
            far_chips[away] * 2 + core,
        )

    def pass_copy(away, side, step):
        source = (chip + chip_count - 1 - away) % chip_count * 2 + core
        block = grads.at[side, step, place_rows(source)]
        return remote(
            block,
            block,
            pass_send.at[away],
            pass_recv.at[away, step],
            dp_index,
            partner,
        )

    def weight_copy(side, hop, slot):
        if isinstance(hop, int) and hop == 0:
            if slot == 0:
                source = weight_ref.at[:, own_columns(parity, side)]
            else:
                source = weights.at[side, last, slots[1]]
        else:
            source = weights.at[side, hop - 1, slots[slot]]
        return remote(
            source,
            weights.at[side, hop, slots[slot]],
            weight_send,
            weight_recv.at[side, hop, slot],
            ring[side],
            tensor_index,
        )

    def sum_copy(side, step, slot):
        return remote(
            sums_out.at[side, step, slots[slot]],
            sums_in.at[side, step, slots[slot]],
            sum_send,
            sum_recv.at[side, step, slot],
            ring[side],
            tensor_index,
        )

    def block_of(owner_chip, part):
        return owner_chip * chip_blocks + part

    def block_rows(block):
        return pl.ds(pl.multiple_of(block * backward_rows, backward_rows), backward_rows)

    def share_copy(block):
        return remote(
            share_out.at[block_rows(block)],
            share_in.at[block_rows(block)],
            share_send,
            share_recv.at[block],
            dp_index,
            mate,
        )

    def back_copy(side):
        return remote(
            back_out.at[side],
            back_in.at[side],
            back_send,
            back_recv.at[side],
            dp_index,
            mate,
        )

    outs_copy = remote(outs_t.at[0], outs_t.at[1], outs_send, outs_recv, dp_index, mate)
    kv_copy = remote(
        kv_grads.at[:, pl.ds(pl.multiple_of((1 - core) * half_rows, half_rows), half_rows)],
        kv_in,
        kv_send,
        kv_recv,
        dp_index,
        partner,
    )

    loads = [
        pltpu.make_async_copy(query_full, query_ref, load_sem.at[0]),
        pltpu.make_async_copy(key_full.at[:, kv_columns], key_ref, load_sem.at[1]),
        pltpu.make_async_copy(value_full.at[:, kv_columns], value_ref, load_sem.at[2]),
    ]
    for load in loads:
        load.start()

    targets = [(dp_index, partner), (ring[0], tensor_index), (ring[1], tensor_index)]
    targets += [(dp_index, other * 2 + core) for other in far_chips]
    barrier = pltpu.get_barrier_semaphore()
    for target in targets:
        pl.semaphore_signal(barrier, inc=1, device_id=target, device_id_type=MESH)
    pl.semaphore_wait(barrier, len(targets))

    def far_start(step):
        for side in (0, 1):
            for away in range(chip_count - 1):
                far_copy(away, side, step).start()

    for side in (0, 1):
        weight_copy(side, 0, 0).start()
        mate_weight(side).start()
    far_start(0)
    for side in (0, 1):
        own_weight(side).start()

    @pl.loop(0, dp_count)
    def _(step):
        for side in (0, 1):
            near_copy(side, step).start()
            own_copy(side, step).start()

    accum[...] = jnp.zeros_like(accum)
    kv_grads[...] = jnp.zeros_like(kv_grads)
    nt = (((1,), (1,)), ((), ()))
    tn = (((0,), (0,)), ((), ()))

    def dot(left, right, dims):
        return lax.dot_general(left, right, dims, preferred_element_type=jnp.float32)

    def window_start(index):
        skip, total = half_rows // forward_rows, seq_len // forward_rows
        past = (index + total - skip) // total
        return past * (index - skip) * forward_rows

    def window_keys(index):
        return pl.ds(pl.multiple_of(window_start(index), forward_rows), window)

    def forward(index):
        here = pl.ds(pl.multiple_of(index * forward_rows, forward_rows), forward_rows)
        query_places = index * forward_rows + lax.broadcasted_iota(jnp.int32, (forward_rows, 1), 0)
        key_places = window_start(index) + lax.broadcasted_iota(
            jnp.int32, (forward_rows, window), 1
        )
        doc_start = jnp.zeros((forward_rows, 1), jnp.int32)
        doc_end = jnp.int32(0)
        for doc in range(lengths_ref.shape[1]):
            doc_end = doc_end + lengths_ref[0, doc]
            doc_start = jnp.where(query_places >= doc_end, doc_end, doc_start)
        allowed = (key_places >= doc_start) & (key_places <= query_places)
        keys, values = key_ref[window_keys(index)], value_ref[window_keys(index)]
        for head in range(heads):
            lanes = slice(head * HEAD_SIZE, (head + 1) * HEAD_SIZE)
            scores = dot(query_ref[here, lanes], keys, nt) * score_scale
            scores = jnp.where(allowed, scores, -jnp.inf)
            row_max = jnp.max(scores, axis=1, keepdims=True)
            total = jnp.sum(jnp.exp(scores - row_max), axis=1, keepdims=True)
            prob = jnp.exp(scores - (row_max + jnp.log(total)))
            probs[head, here] = prob
            out = jnp.dot(prob.astype(jnp.bfloat16), values, preferred_element_type=jnp.float32)
            outs[here, lanes] = out.astype(jnp.bfloat16)
            outs_t[0, lanes, here] = out.T.astype(jnp.bfloat16)
            for part in range(forward_rows // backward_rows):
                piece = prob[part * backward_rows : (part + 1) * backward_rows]
                block = index * (forward_rows // backward_rows) + part
                probs_t[head, block] = piece.T.astype(jnp.bfloat16)

    def query_put(block):
        here = block_rows(block)
        return pltpu.make_async_copy(
            query_grad_ref.at[here], query_grad_out.at[here], query_sem
        )

    def backward(block):
        here = block_rows(block)
        index = block // (forward_rows // backward_rows)
        seen = window_keys(index)
        keys, values = key_ref[seen], value_ref[seen]
        share_copy(block).wait_recv()
        key_total, value_total = kv_grads[0, seen], kv_grads[1, seen]
        for head in range(heads):
            lanes = slice(head * HEAD_SIZE, (head + 1) * HEAD_SIZE)
            grad = (accum[here, lanes] + share_in[here, lanes].astype(jnp.float32)).astype(
                jnp.bfloat16
            )
            delta = jnp.sum(
                grad.astype(jnp.float32) * outs[here, lanes].astype(jnp.float32), axis=1, keepdims=True
            )
            dscore = probs[head, here] * (dot(grad, values, nt) - delta) * score_scale
            dscore = dscore.astype(jnp.bfloat16)
            query_grad_ref[here, lanes] = jnp.dot(
                dscore, keys, preferred_element_type=jnp.float32
            ).astype(jnp.bfloat16)
            key_total += dot(dscore, query_ref[here, lanes], tn)
            value_total += jnp.dot(probs_t[head, block], grad, preferred_element_type=jnp.float32)
        kv_grads[0, seen] = key_total
        kv_grads[1, seen] = value_total
        query_put(block).start()

    def chip_rows(owner_chip):
        return pl.ds(pl.multiple_of(owner_chip * (2 * rows), 2 * rows), 2 * rows)

    def project(owner_chip, steps):
        here = chip_rows(owner_chip)
        total = accum[here]
        for step in steps:
            for side in (0, 1):
                total += dot(grads[side, step, here], weights[side, step], nt)
        accum[here] = total

    def share(owner_chip):
        for part in range(chip_blocks):
            block = block_of(owner_chip, part)
            here = block_rows(block)
            share_out[here] = accum[here, slots[1]].astype(jnp.bfloat16)
            share_copy(block).start()

    def drain(ref, sem):
        pltpu.make_async_copy(ref, ref, sem).wait()

    def local_wait():
        drain(grads.at[:, :, place_rows(tensor_index)], own_sem)
        drain(grads.at[:, :, place_rows(partner)], near_recv)
        drain(weights.at[:, last, slots[0]], own_weight_sem)

    def weight_step(hop, slot, send):
        for side in (0, 1):
            weight_copy(side, hop, slot).wait_recv()
            if send:
                weight_copy(side, hop + 1, slot).start()

    def far_pass(step):
        for away in range(chip_count - 1):
            source = (chip + chip_count - 1 - away) % chip_count * 2 + core
            drain(grads.at[:, step, place_rows(source)], far_recv.at[away, step])
            for side in (0, 1):
                pass_copy(away, side, step).start()

    def pass_wait(step):
        for away in range(chip_count - 1):
            source = (chip + chip_count - 1 - away) % chip_count * 2 + 1 - core
            drain(grads.at[:, step, place_rows(source)], pass_recv.at[away, step])

    def sum_part(slot, side, step):
        return jnp.dot(outs_t[slot], grads[side, step], preferred_element_type=jnp.float32)

    def sum_step(slot, step, first=False):
        for side in (0, 1):
            part = sum_part(slot, side, step)
            if not first:
                sum_copy(side, step - 1, slot).wait_recv()
                part = part + sums_in[side, step - 1, slots[slot]].astype(jnp.float32)
            sums_out[side, step, slots[slot]] = part.astype(jnp.bfloat16)
            sum_copy(side, step, slot).start()

    def weight_put(which, side):
        return pltpu.make_async_copy(
            weight_grad_ref.at[which, side],
            weight_grad_out.at[:, own_columns(parity if which == 0 else 1 - parity, side)],
            put_sem,
        )

    def sum_final(slot):
        for side in (0, 1):
            part = sum_part(slot, side, last)
            sum_copy(side, last - 1, slot).wait_recv()
            part = part + sums_in[side, last - 1, slots[slot]].astype(jnp.float32)
            if slot == 0:
                weight_grad_ref[0, side] = part
                weight_put(0, side).start()
            else:
                back_out[side] = part.astype(jnp.bfloat16)
                back_copy(side).start()

    for load in loads:
        load.wait()
    blocks = seq_len // forward_rows
    for index in range(blocks - 1):
        forward(index)
    weight_step(0, 0, True)
    forward(blocks - 1)
    outs_copy.start()

    @pl.loop(1, dp_count)
    def _(step):
        far_start(step)

    for side in (0, 1):
        mate_weight(side).wait_recv()
        weight_copy(side, 0, 1).start()
    local_wait()
    project(chip, [last])
    weight_step(1, 0, True)
    weight_step(0, 1, True)
    far_pass(0)
    project(chip, [0])
    weight_step(2, 0, True)
    pass_wait(0)
    sum_step(0, 0, True)
    weight_step(1, 1, True)
    project(chip, [1])
    for other in far_chips:
        project(other, [0])
    weight_step(2, 1, True)
    project(chip, [2])
    outs_copy.wait_recv()
    sum_step(1, 0, True)
    weight_step(3, 0, True)
    weight_step(3, 1, True)
    project(chip, [3])
    far_pass(1)
    pass_wait(1)
    sum_step(1, 1)
    far_pass(2)

    def main_step(step, send):
        weight_step(step + lead, 0, send)
        weight_step(step + lead, 1, send)
        pass_wait(step + 1)
        sum_step(1, step + 1)
        sum_step(0, step)
        project(chip, [step + lead])
        for other in far_chips:
            project(other, [step])
        far_pass(step + 2)

    tail = last - lead - 1

    @pl.loop(1, tail)
    def _(step):
        main_step(step, True)

    weight_step(last - 1, 0, False)
    weight_step(last - 1, 1, False)
    project(chip, [last - 1])
    share(chip)
    pass_wait(tail + 1)
    sum_step(1, tail + 1)
    for step in range(tail + 2, last):
        far_pass(step)
    for other in far_chips:
        project(other, [tail, tail + 1])
    sum_step(0, tail)
    far_pass(last)
    for step in range(tail + 2, dp_count):
        pass_wait(step)
    for other in far_chips:
        project(other, list(range(tail + 2, dp_count)))
        share(other)

    rest = list(range(tail + 2, last))
    order = [(mate_chip + away) % chip_count for away in range(chip_count)]
    pieces = [block_of(owner, part) for owner in order for part in range(chip_blocks)]
    per = -(-len(pieces) // max(len(rest), 1))
    for place_in, step in enumerate(rest):
        sum_step(1, step)
        sum_step(0, step - 1)
        for block in pieces[place_in * per : (place_in + 1) * per]:
            backward(block)
    for block in pieces[len(rest) * per :]:
        backward(block)
    kv_copy.start()
    sum_final(1)
    sum_step(0, last - 1)
    mine = pl.ds(pl.multiple_of(core * half_rows, half_rows), half_rows)
    kv_copy.wait()
    kv_done[...] = (kv_grads[:, mine] + kv_in[...]).astype(jnp.bfloat16)
    kv_puts = [
        pltpu.make_async_copy(kv_done.at[which], to, kv_sem.at[which])
        for which, to in enumerate((key_grad_out, value_grad_out))
    ]
    for put in kv_puts:
        put.start()

    drain(weights.at[:, last, slots[1]], mate_send)
    drain(grads.at[:, :, place_rows(tensor_index)], near_send)
    for away in range(chip_count - 1):
        drain(grads.at[:, :, place_rows(tensor_index)], far_send.at[away])
        drain(grads.at[:, :, place_rows(tensor_index)], pass_send.at[away])
    drain(weights.at[:, pl.ds(0, last)], weight_send)
    outs_copy.wait_send()
    drain(share_out, share_send)
    drain(query_grad_ref, query_sem)
    for put in kv_puts:
        put.wait()
    sum_final(0)
    for side in (0, 1):
        back_copy(side).wait_recv()
        weight_grad_ref[1, side] = back_in[side].astype(jnp.float32)
        weight_put(1, side).start()
    drain(back_out, back_send)
    drain(sums_out, sum_send)
    drain(weight_grad_ref, put_sem)


def finish_kernel(*refs):
    count = (len(refs) - 1) // 2
    puts = [
        pltpu.make_async_copy(refs[i], refs[count + i], refs[2 * count].at[i]) for i in range(count)
    ]
    for put in puts:
        put.start()
    for put in puts:
        put.wait()


def finish(*values):
    anywhere = pl.BlockSpec(memory_space=pl.ANY)
    return pl.pallas_call(
        finish_kernel,
        out_shape=tuple(pltpu.HBM(value.shape, value.dtype) for value in values),
        in_specs=[anywhere] * len(values),
        out_specs=(anywhere,) * len(values),
        scratch_shapes=[pltpu.SemaphoreType.DMA((len(values),))],
        compiler_params=pltpu.CompilerParams(vmem_limit_bytes=8 * 1024 * 1024),
        name="finish",
    )(*values)


def shards(query_act, rotated_keys, value_input, grad_out, out_weight, doc_lengths):
    dp_count, tensor_count = lax.axis_size("dp"), lax.axis_size("tensor")
    chip_count = tensor_count // 2
    far = chip_count - 1
    seq_len = query_act.shape[1]
    depth, width = out_weight.shape
    quarter = width // 4
    heads = depth // HEAD_SIZE
    forward_rows, backward_rows, window = block_sizes(seq_len, tensor_count)
    blocks = seq_len // backward_rows
    dma = pltpu.SemaphoreType.DMA
    anywhere = pl.BlockSpec(memory_space=pl.ANY)
    low, full = jnp.bfloat16, jnp.float32
    kv_shape = pltpu.VMEM((seq_len // 2, HEAD_SIZE), low)
    query_grad, key_grad, value_grad, weight_grad = pl.pallas_call(
        functools.partial(exchange_kernel, dp_count, tensor_count),
        out_shape=(
            pltpu.VMEM((seq_len, depth), low),
            kv_shape,
            kv_shape,
            pltpu.VMEM((depth, width), full),
        ),
        in_specs=[pl.BlockSpec(memory_space=pltpu.HBM)] * 5
        + [pl.BlockSpec(memory_space=pltpu.SMEM)],
        out_specs=(anywhere,) * 4,
        scratch_shapes=[
            pltpu.VMEM((2, dp_count, seq_len, quarter), low),
            pltpu.VMEM((2, dp_count, 2 * depth, quarter), low),
            pltpu.VMEM((2, dp_count - 1, 2 * depth, quarter), low),
            pltpu.VMEM((2, dp_count - 1, 2 * depth, quarter), low),
            pltpu.VMEM((seq_len, 2 * depth), full),
            pltpu.VMEM((seq_len, depth), low),
            pltpu.VMEM((seq_len, HEAD_SIZE), low),
            pltpu.VMEM((seq_len, HEAD_SIZE), low),
            pltpu.VMEM((seq_len, depth), low),
            pltpu.VMEM((2, 2, depth, quarter), full),
            pltpu.VMEM((heads, seq_len, window), full),
            pltpu.VMEM((heads, blocks, window, backward_rows), low),
            pltpu.VMEM((seq_len, depth), low),
            pltpu.VMEM((2, depth, seq_len), low),
            pltpu.VMEM((seq_len, depth), low),
            pltpu.VMEM((seq_len, depth), low),
            pltpu.VMEM((2, depth, quarter), low),
            pltpu.VMEM((2, depth, quarter), low),
            pltpu.VMEM((2, seq_len, HEAD_SIZE), full),
            pltpu.VMEM((2, seq_len // 2, HEAD_SIZE), full),
            pltpu.VMEM((2, seq_len // 2, HEAD_SIZE), low),
            dma,
            dma,
            dma,
            dma,
            dma((far,)),
            dma((far, dp_count)),
            dma((far,)),
            dma((far, dp_count)),
            dma,
            dma((2,)),
            dma,
            dma((2, dp_count - 1, 2)),
            dma,
            dma((2, dp_count - 1, 2)),
            dma,
            dma,
            dma,
            dma((blocks,)),
            dma,
            dma((2,)),
            dma,
            dma,
            dma((3,)),
            dma,
            dma,
            dma((2,)),
        ],
        compiler_params=pltpu.CompilerParams(
            collective_id=0, has_side_effects=True, vmem_limit_bytes=54 * 1024 * 1024
        ),
        name="exchange",
    )(grad_out[0], out_weight, query_act[0], rotated_keys[0], value_input[0], doc_lengths)
    query_grad, key_grad, value_grad, weight_grad = finish(
        query_grad, key_grad, value_grad, weight_grad
    )
    return (query_grad[None], key_grad[None, None], value_grad[None, None], weight_grad)


def solution(mesh):
    placed = (
        P("dp", None, "tensor"),
        P("dp", None, None),
        P("dp", None, None),
        P("dp", "tensor", None),
        P("tensor", "dp"),
        P("dp", None),
    )
    return jax.shard_map(
        shards,
        mesh=mesh,
        in_specs=placed,
        out_specs=(
            P("dp", None, "tensor"),
            P("dp", "tensor", None, None),
            P("dp", "tensor", None, None),
            P("tensor", "dp"),
        ),
        check_vma=False,
    )
```

```python
import functools

import jax
import jax.numpy as jnp
from jax import lax
from jax.experimental import pallas as pl
from jax.experimental.pallas import tpu as pltpu
from jax.sharding import PartitionSpec as P

HEAD_SIZE = 128


MESH = pl.DeviceIdType.MESH


def ring_place(index, count):
    odd = index % 2
    return (1 - odd) * (index // 2) + odd * (count - 1 - index // 2)


def ring_index(place, count):
    back = place // (count // 2)
    return (1 - back) * (2 * place) + back * (2 * (count - 1 - place) + 1)


def block_sizes(seq_len, tensor_count):
    forward_rows = min(256, seq_len)
    backward_rows = min(forward_rows, 2 * seq_len // tensor_count)
    return forward_rows, backward_rows, seq_len // 2 + forward_rows


def exchange_kernel(
    dp_count,
    tensor_count,
    grad_ref,
    weight_ref,
    query_full,
    key_full,
    value_full,
    lengths_ref,
    query_grad_out,
    key_grad_out,
    value_grad_out,
    weight_grad_out,
    grads,
    weights,
    sums_out,
    sums_in,
    accum,
    query_ref,
    key_ref,
    value_ref,
    query_grad_ref,
    weight_grad_ref,
    probs,
    probs_t,
    outs,
    outs_t,
    share_out,
    share_in,
    back_out,
    back_in,
    kv_grads,
    kv_in,
    kv_done,
    own_sem,
    own_weight_sem,
    near_send,
    near_recv,
    far_send,
    far_recv,
    pass_send,
    pass_recv,
    mate_send,
    mate_recv,
    weight_send,
    weight_recv,
    sum_send,
    sum_recv,
    outs_send,
    outs_recv,
    share_send,
    share_recv,
    back_send,
    back_recv,
    kv_send,
    kv_recv,
    load_sem,
    query_sem,
    put_sem,
    kv_sem,
):
    dp_index = lax.axis_index("dp")
    tensor_index = lax.axis_index("tensor")
    chip_count = tensor_count // 2
    chip, core = tensor_index // 2, tensor_index % 2
    parity = chip % 2
    mate_chip = chip + 1 - 2 * parity
    mate = mate_chip * 2 + core
    partner = chip * 2 + 1 - core
    place = ring_place(dp_index, dp_count)
    ring = (
        ring_index((place + 1) % dp_count, dp_count),
        ring_index((place + dp_count - 1) % dp_count, dp_count),
    )
    rows = grad_ref.shape[0]
    depth, width = weight_ref.shape
    half, quarter = width // 2, width // 4
    last = dp_count - 1
    seq_len = query_full.shape[0]
    heads = depth // HEAD_SIZE
    half_rows = seq_len // 2
    score_scale = HEAD_SIZE ** (-0.5)
    middle = dp_count // 2
    forward_rows, backward_rows, window = block_sizes(seq_len, tensor_count)
    chip_blocks = 2 * rows // backward_rows
    kv_columns = pl.ds(pl.multiple_of(tensor_index // 2 * HEAD_SIZE, HEAD_SIZE), HEAD_SIZE)
    far_chips = [(chip + away) % chip_count for away in range(1, chip_count)]
    slots = (slice(0, depth), slice(depth, 2 * depth))

    def place_rows(index):
        return pl.ds(pl.multiple_of(index * rows, rows), rows)

    def own_columns(whose, side):
        return pl.ds(pl.multiple_of(whose * half + side * quarter, quarter), quarter)

    def columns(side, step, whose):
        if side == 0:
            owner = ring_index((place + 2 * dp_count - 1 - step) % dp_count, dp_count)
        else:
            owner = ring_index((place + 1 + step) % dp_count, dp_count)
        return pl.ds(
            pl.multiple_of(owner * width + whose * half + side * quarter, quarter), quarter
        )

    def remote(source, target, send, recv, dp_to, tensor_to):
        return pltpu.make_async_remote_copy(
            source, target, send, recv, device_id=(dp_to, tensor_to), device_id_type=MESH
        )

    def own_copy(side, step):
        return pltpu.make_async_copy(
            grad_ref.at[:, columns(side, step, parity)],
            grads.at[side, step, place_rows(tensor_index)],
            own_sem,
        )

    def own_weight(side):
        return pltpu.make_async_copy(
            weight_ref.at[:, own_columns(parity, side)],
            weights.at[side, last, slots[0]],
            own_weight_sem,
        )

    def mate_weight(side):
        return remote(
            weight_ref.at[:, own_columns(1 - parity, side)],
            weights.at[side, last, slots[1]],
            mate_send,
            mate_recv.at[side],
            dp_index,
            mate,
        )

    def near_copy(side, step):
        return remote(
            grad_ref.at[:, columns(side, step, parity)],
            grads.at[side, step, place_rows(tensor_index)],
            near_send,
            near_recv,
            dp_index,
            partner,
        )

    def far_copy(away, side, step):
        return remote(
            grad_ref.at[:, columns(side, step, far_chips[away] % 2)],
            grads.at[side, step, place_rows(tensor_index)],
            far_send.at[away],
            far_recv.at[away, step],
            dp_index,
            far_chips[away] * 2 + core,
        )

    def pass_copy(away, side, step):
        source = (chip + chip_count - 1 - away) % chip_count * 2 + core
        block = grads.at[side, step, place_rows(source)]
        return remote(
            block,
            block,
            pass_send.at[away],
            pass_recv.at[away, step],
            dp_index,
            partner,
        )

    def hop_step(hop, minor):
        return last - hop if minor else hop - 1

    def weight_copy(side, hop, minor, slot):
        if hop > 1:
            source = weights.at[side, hop_step(hop - 1, minor), slots[slot]]
        elif slot == 0:
            source = weight_ref.at[:, own_columns(parity, side)]
        else:
            source = weights.at[side, last, slots[1]]
        step = hop_step(hop, minor)
        return remote(
            source,
            weights.at[side, step, slots[slot]],
            weight_send,
            weight_recv.at[side, step, slot],
            ring[1 - side if minor else side],
            tensor_index,
        )

    def sum_copy(side, step, slot):
        return remote(
            sums_out.at[side, step, slots[slot]],
            sums_in.at[side, step, slots[slot]],
            sum_send,
            sum_recv.at[side, step, slot],
            ring[side if step >= middle - 1 else 1 - side],
            tensor_index,
        )

    def block_of(owner_chip, part):
        return owner_chip * chip_blocks + part

    def block_rows(block):
        return pl.ds(pl.multiple_of(block * backward_rows, backward_rows), backward_rows)

    def share_copy(block):
        return remote(
            share_out.at[block_rows(block)],
            share_in.at[block_rows(block)],
            share_send,
            share_recv.at[block],
            dp_index,
            mate,
        )

    def back_copy(side):
        return remote(
            back_out.at[side],
            back_in.at[side],
            back_send,
            back_recv.at[side],
            dp_index,
            mate,
        )

    outs_copy = remote(outs_t.at[0], outs_t.at[1], outs_send, outs_recv, dp_index, mate)
    kv_copy = remote(
        kv_grads.at[:, pl.ds(pl.multiple_of((1 - core) * half_rows, half_rows), half_rows)],
        kv_in,
        kv_send,
        kv_recv,
        dp_index,
        partner,
    )

    loads = [
        pltpu.make_async_copy(query_full, query_ref, load_sem.at[0]),
        pltpu.make_async_copy(key_full.at[:, kv_columns], key_ref, load_sem.at[1]),
        pltpu.make_async_copy(value_full.at[:, kv_columns], value_ref, load_sem.at[2]),
    ]
    for load in loads:
        load.start()

    targets = [(dp_index, partner), (ring[0], tensor_index), (ring[1], tensor_index)]
    targets += [(dp_index, other * 2 + core) for other in far_chips]
    barrier = pltpu.get_barrier_semaphore()
    for target in targets:
        pl.semaphore_signal(barrier, inc=1, device_id=target, device_id_type=MESH)
    pl.semaphore_wait(barrier, len(targets))

    def far_start(step):
        for side in (0, 1):
            for away in range(chip_count - 1):
                far_copy(away, side, step).start()

    grad_order = []
    for turn in range(middle):
        grad_order += [middle - 1 + turn] + ([middle - 2 - turn] if turn < middle - 1 else [])
    grad_order.append(last)
    for side in (0, 1):
        weight_copy(side, 1, 0, 0).start()
        mate_weight(side).start()
    for side in (0, 1):
        weight_copy(side, 1, 1, 0).start()
    far_start(grad_order[0])
    for side in (0, 1):
        own_weight(side).start()

    @pl.loop(0, dp_count)
    def _(step):
        for side in (0, 1):
            near_copy(side, step).start()
            own_copy(side, step).start()

    nt = (((1,), (1,)), ((), ()))
    tn = (((0,), (0,)), ((), ()))

    def dot(left, right, dims):
        return lax.dot_general(left, right, dims, preferred_element_type=jnp.float32)

    def window_start(index):
        skip, total = half_rows // forward_rows, seq_len // forward_rows
        past = (index + total - skip) // total
        return past * (index - skip) * forward_rows

    def window_keys(index):
        return pl.ds(pl.multiple_of(window_start(index), forward_rows), window)

    def forward(index):
        here = pl.ds(pl.multiple_of(index * forward_rows, forward_rows), forward_rows)
        query_places = index * forward_rows + lax.broadcasted_iota(jnp.int32, (forward_rows, 1), 0)
        key_places = window_start(index) + lax.broadcasted_iota(
            jnp.int32, (forward_rows, window), 1
        )
        doc_start = jnp.zeros((forward_rows, 1), jnp.int32)
        doc_end = jnp.int32(0)
        for doc in range(lengths_ref.shape[1]):
            doc_end = doc_end + lengths_ref[0, doc]
            doc_start = jnp.where(query_places >= doc_end, doc_end, doc_start)
        allowed = (key_places >= doc_start) & (key_places <= query_places)
        keys, values = key_ref[window_keys(index)], value_ref[window_keys(index)]
        for head in range(heads):
            lanes = slice(head * HEAD_SIZE, (head + 1) * HEAD_SIZE)
            scores = dot(query_ref[here, lanes], keys, nt) * score_scale
            scores = jnp.where(allowed, scores, -jnp.inf)
            row_max = jnp.max(scores, axis=1, keepdims=True)
            total = jnp.sum(jnp.exp(scores - row_max), axis=1, keepdims=True)
            prob = jnp.exp(scores - (row_max + jnp.log(total)))
            probs[head, here] = prob
            out = jnp.dot(prob.astype(jnp.bfloat16), values, preferred_element_type=jnp.float32)
            outs[here, lanes] = out.astype(jnp.bfloat16)
            outs_t[0, lanes, here] = out.T.astype(jnp.bfloat16)
            for part in range(forward_rows // backward_rows):
                piece = prob[part * backward_rows : (part + 1) * backward_rows]
                block = index * (forward_rows // backward_rows) + part
                probs_t[head, block] = piece.T.astype(jnp.bfloat16)

    def query_put(block):
        here = block_rows(block)
        return pltpu.make_async_copy(
            query_grad_ref.at[here], query_grad_out.at[here], query_sem
        )

    def backward(block):
        here = block_rows(block)
        index = block // (forward_rows // backward_rows)
        seen = window_keys(index)
        keys, values = key_ref[seen], value_ref[seen]
        share_copy(block).wait_recv()
        key_total, value_total = kv_grads[0, seen], kv_grads[1, seen]
        for head in range(heads):
            lanes = slice(head * HEAD_SIZE, (head + 1) * HEAD_SIZE)
            grad = (accum[here, lanes] + share_in[here, lanes].astype(jnp.float32)).astype(
                jnp.bfloat16
            )
            delta = jnp.sum(
                grad.astype(jnp.float32) * outs[here, lanes].astype(jnp.float32), axis=1, keepdims=True
            )
            dscore = probs[head, here] * (dot(grad, values, nt) - delta) * score_scale
            dscore = dscore.astype(jnp.bfloat16)
            query_grad_ref[here, lanes] = jnp.dot(
                dscore, keys, preferred_element_type=jnp.float32
            ).astype(jnp.bfloat16)
            key_total += dot(dscore, query_ref[here, lanes], tn)
            value_total += jnp.dot(probs_t[head, block], grad, preferred_element_type=jnp.float32)
        kv_grads[0, seen] = key_total
        kv_grads[1, seen] = value_total
        query_put(block).start()

    def chip_rows(owner_chip):
        return pl.ds(pl.multiple_of(owner_chip * (2 * rows), 2 * rows), 2 * rows)

    def project(owner_chip, steps):
        here = chip_rows(owner_chip)
        total = accum[here]
        for step in steps:
            for side in (0, 1):
                total += dot(grads[side, step, here], weights[side, step], nt)
        accum[here] = total

    def share(owner_chip):
        for part in range(chip_blocks):
            block = block_of(owner_chip, part)
            here = block_rows(block)
            share_out[here] = accum[here, slots[1]].astype(jnp.bfloat16)
            share_copy(block).start()

    def drain(ref, sem):
        pltpu.make_async_copy(ref, ref, sem).wait()

    def local_wait():
        drain(grads.at[:, :, place_rows(tensor_index)], own_sem)
        drain(grads.at[:, :, place_rows(partner)], near_recv)
        drain(weights.at[:, last, slots[0]], own_weight_sem)

    def weight_step(hop, minor, slot):
        for side in (0, 1):
            weight_copy(side, hop, minor, slot).wait_recv()
            if hop + minor < middle:
                weight_copy(side, hop + 1, minor, slot).start()

    def far_pass(step):
        for away in range(chip_count - 1):
            source = (chip + chip_count - 1 - away) % chip_count * 2 + core
            drain(grads.at[:, step, place_rows(source)], far_recv.at[away, step])
            for side in (0, 1):
                pass_copy(away, side, step).start()

    def pass_wait(step):
        for away in range(chip_count - 1):
            source = (chip + chip_count - 1 - away) % chip_count * 2 + 1 - core
            drain(grads.at[:, step, place_rows(source)], pass_recv.at[away, step])

    passed = set()

    def pass_wait_once(step):
        if step not in passed:
            passed.add(step)
            pass_wait(step)

    def sum_part(slot, side, step):
        return jnp.dot(outs_t[slot], grads[side, step], preferred_element_type=jnp.float32)

    def sum_step(slot, step):
        pass_wait_once(step)
        before = step - 1 if step >= middle - 1 else step + 1
        first = step in (middle - 2, middle - 1)
        for side in (0, 1):
            part = sum_part(slot, side, step)
            if not first:
                sum_copy(side, before, slot).wait_recv()
                part = part + sums_in[side, before, slots[slot]].astype(jnp.float32)
            sums_out[side, step, slots[slot]] = part.astype(jnp.bfloat16)
            sum_copy(side, step, slot).start()

    def weight_put(which, side):
        return pltpu.make_async_copy(
            weight_grad_ref.at[which, side],
            weight_grad_out.at[:, own_columns(parity if which == 0 else 1 - parity, side)],
            put_sem,
        )

    def sum_final(slot):
        for side in (0, 1):
            part = sum_part(slot, side, last)
            for before in (0, last - 1):
                sum_copy(side, before, slot).wait_recv()
                part = part + sums_in[side, before, slots[slot]].astype(jnp.float32)
            if slot == 0:
                weight_grad_ref[0, side] = part
                weight_put(0, side).start()
            else:
                back_out[side] = part.astype(jnp.bfloat16)
                back_copy(side).start()

    for load in loads:
        load.wait()
    blocks = seq_len // forward_rows
    for index in range(blocks - 1):
        forward(index)
    weight_step(1, 0, 0)
    forward(blocks - 1)
    outs_copy.start()
    for step in grad_order[1:]:
        far_start(step)
    for side in (0, 1):
        mate_weight(side).wait_recv()
        for minor in (0, 1):
            weight_copy(side, 1, minor, 1).start()
    weight_step(1, 1, 0)
    accum[...] = jnp.zeros_like(accum)
    kv_grads[...] = jnp.zeros_like(kv_grads)
    local_wait()
    project(chip, [last])
    passing = list(grad_order)

    def pass_next():
        far_pass(passing.pop(0))

    for hop in range(2, middle + 1):
        weight_step(hop, 0, 0)
        weight_step(hop - 1, 0, 1)
        weight_step(hop - 1, 1, 1)
        if hop < middle:
            weight_step(hop, 1, 0)
        if hop == middle - 2:
            pass_next()
        project(chip, [hop - 2, last + 1 - hop])
        if hop == middle - 2:
            sum_step(0, middle - 1)
        if hop == middle - 1:
            outs_copy.wait_recv()
            sum_step(1, middle - 1)
            pass_next()
    sum_step(0, middle - 2)
    weight_step(middle, 0, 1)
    sum_step(1, middle - 2)
    pass_next()
    pass_next()
    project(chip, [middle - 1])
    share(chip)
    for other in far_chips:
        project(other, [middle - 1, middle - 2])

    turns = grad_order[2:last]
    ops = [(1, turns[0]), (1, turns[1])]
    for number in range(2, len(turns)):
        ops += [(0, turns[number - 2]), (1, turns[number])]
    ops[-2], ops[-1] = ops[-1], ops[-2]
    ops += [(0, turns[-2]), (0, turns[-1])]
    ops_left = len(ops)
    order = [(mate_chip + away) % chip_count for away in range(chip_count)]
    pending = []
    for slot, step in ops:
        sum_step(slot, step)
        ops_left -= 1
        if slot == 1:
            pending.append(step)
            if passing and not (ops_left > 2 and len(passing) == 2 and len(pending) == 1):
                pass_next()
        if len(pending) > 1 and ops_left > 2:
            for other in far_chips:
                project(other, pending)
            pending = []
        if ops_left == 2:
            pass_wait_once(last)
            for other in far_chips:
                project(other, pending + [last])
                share(other)
        if ops_left == 1:
            for part in range(chip_blocks):
                backward(block_of(order[0], part))
            sum_final(1)
    for owner in order[1:]:
        for part in range(chip_blocks):
            backward(block_of(owner, part))
    kv_copy.start()
    mine = pl.ds(pl.multiple_of(core * half_rows, half_rows), half_rows)
    kv_copy.wait()
    kv_done[...] = (kv_grads[:, mine] + kv_in[...]).astype(jnp.bfloat16)
    kv_puts = [
        pltpu.make_async_copy(kv_done.at[which], to, kv_sem.at[which])
        for which, to in enumerate((key_grad_out, value_grad_out))
    ]
    for put in kv_puts:
        put.start()

    drain(weights.at[:, last, slots[1]], mate_send)
    drain(grads.at[:, :, place_rows(tensor_index)], near_send)
    for away in range(chip_count - 1):
        drain(grads.at[:, :, place_rows(tensor_index)], far_send.at[away])
        drain(grads.at[:, :, place_rows(tensor_index)], pass_send.at[away])
    drain(weights.at[:, pl.ds(0, last)], weight_send)
    outs_copy.wait_send()
    drain(share_out, share_send)
    drain(query_grad_ref, query_sem)
    for put in kv_puts:
        put.wait()
    sum_final(0)
    for side in (0, 1):
        back_copy(side).wait_recv()
        weight_grad_ref[1, side] = back_in[side].astype(jnp.float32)
        weight_put(1, side).start()
    drain(back_out, back_send)
    drain(sums_out, sum_send)
    drain(weight_grad_ref, put_sem)


def finish_kernel(*refs):
    count = (len(refs) - 1) // 2
    puts = [
        pltpu.make_async_copy(refs[i], refs[count + i], refs[2 * count].at[i]) for i in range(count)
    ]
    for put in puts:
        put.start()
    for put in puts:
        put.wait()


def finish(*values):
    anywhere = pl.BlockSpec(memory_space=pl.ANY)
    return pl.pallas_call(
        finish_kernel,
        out_shape=tuple(pltpu.HBM(value.shape, value.dtype) for value in values),
        in_specs=[anywhere] * len(values),
        out_specs=(anywhere,) * len(values),
        scratch_shapes=[pltpu.SemaphoreType.DMA((len(values),))],
        compiler_params=pltpu.CompilerParams(vmem_limit_bytes=8 * 1024 * 1024),
        name="finish",
    )(*values)


def shards(query_act, rotated_keys, value_input, grad_out, out_weight, doc_lengths):
    dp_count, tensor_count = lax.axis_size("dp"), lax.axis_size("tensor")
    chip_count = tensor_count // 2
    far = chip_count - 1
    seq_len = query_act.shape[1]
    depth, width = out_weight.shape
    quarter = width // 4
    heads = depth // HEAD_SIZE
    forward_rows, backward_rows, window = block_sizes(seq_len, tensor_count)
    blocks = seq_len // backward_rows
    dma = pltpu.SemaphoreType.DMA
    anywhere = pl.BlockSpec(memory_space=pl.ANY)
    low, full = jnp.bfloat16, jnp.float32
    kv_shape = pltpu.VMEM((seq_len // 2, HEAD_SIZE), low)
    query_grad, key_grad, value_grad, weight_grad = pl.pallas_call(
        functools.partial(exchange_kernel, dp_count, tensor_count),
        out_shape=(
            pltpu.VMEM((seq_len, depth), low),
            kv_shape,
            kv_shape,
            pltpu.VMEM((depth, width), full),
        ),
        in_specs=[pl.BlockSpec(memory_space=pltpu.HBM)] * 5
        + [pl.BlockSpec(memory_space=pltpu.SMEM)],
        out_specs=(anywhere,) * 4,
        scratch_shapes=[
            pltpu.VMEM((2, dp_count, seq_len, quarter), low),
            pltpu.VMEM((2, dp_count, 2 * depth, quarter), low),
            pltpu.VMEM((2, dp_count - 1, 2 * depth, quarter), low),
            pltpu.VMEM((2, dp_count - 1, 2 * depth, quarter), low),
            pltpu.VMEM((seq_len, 2 * depth), full),
            pltpu.VMEM((seq_len, depth), low),
            pltpu.VMEM((seq_len, HEAD_SIZE), low),
            pltpu.VMEM((seq_len, HEAD_SIZE), low),
            pltpu.VMEM((seq_len, depth), low),
            pltpu.VMEM((2, 2, depth, quarter), full),
            pltpu.VMEM((heads, seq_len, window), full),
            pltpu.VMEM((heads, blocks, window, backward_rows), low),
            pltpu.VMEM((seq_len, depth), low),
            pltpu.VMEM((2, depth, seq_len), low),
            pltpu.VMEM((seq_len, depth), low),
            pltpu.VMEM((seq_len, depth), low),
            pltpu.VMEM((2, depth, quarter), low),
            pltpu.VMEM((2, depth, quarter), low),
            pltpu.VMEM((2, seq_len, HEAD_SIZE), full),
            pltpu.VMEM((2, seq_len // 2, HEAD_SIZE), full),
            pltpu.VMEM((2, seq_len // 2, HEAD_SIZE), low),
            dma,
            dma,
            dma,
            dma,
            dma((far,)),
            dma((far, dp_count)),
            dma((far,)),
            dma((far, dp_count)),
            dma,
            dma((2,)),
            dma,
            dma((2, dp_count - 1, 2)),
            dma,
            dma((2, dp_count - 1, 2)),
            dma,
            dma,
            dma,
            dma((blocks,)),
            dma,
            dma((2,)),
            dma,
            dma,
            dma((3,)),
            dma,
            dma,
            dma((2,)),
        ],
        compiler_params=pltpu.CompilerParams(
            collective_id=0, has_side_effects=True, vmem_limit_bytes=54 * 1024 * 1024
        ),
        name="exchange",
    )(grad_out[0], out_weight, query_act[0], rotated_keys[0], value_input[0], doc_lengths)
    query_grad, key_grad, value_grad, weight_grad = finish(
        query_grad, key_grad, value_grad, weight_grad
    )
    return (query_grad[None], key_grad[None, None], value_grad[None, None], weight_grad)


def solution(mesh):
    placed = (
        P("dp", None, "tensor"),
        P("dp", None, None),
        P("dp", None, None),
        P("dp", "tensor", None),
        P("tensor", "dp"),
        P("dp", None),
    )
    return jax.shard_map(
        shards,
        mesh=mesh,
        in_specs=placed,
        out_specs=(
            P("dp", None, "tensor"),
            P("dp", "tensor", None, None),
            P("dp", "tensor", None, None),
            P("tensor", "dp"),
        ),
        check_vma=False,
    )
```

```python
import functools

import jax
import jax.numpy as jnp
from jax import lax
from jax.experimental import pallas as pl
from jax.experimental.pallas import tpu as pltpu
from jax.sharding import PartitionSpec as P

HEAD_SIZE = 128


MESH = pl.DeviceIdType.MESH


def ring_place(index, count):
    odd = index % 2
    return (1 - odd) * (index // 2) + odd * (count - 1 - index // 2)


def ring_index(place, count):
    back = place // (count // 2)
    return (1 - back) * (2 * place) + back * (2 * (count - 1 - place) + 1)


def block_sizes(seq_len, tensor_count):
    forward_rows = min(256, seq_len)
    backward_rows = min(forward_rows, 2 * seq_len // tensor_count)
    return forward_rows, backward_rows, seq_len // 2 + forward_rows


def exchange_kernel(
    dp_count,
    tensor_count,
    grad_ref,
    weight_ref,
    query_full,
    key_full,
    value_full,
    lengths_full,
    query_grad_out,
    key_grad_out,
    value_grad_out,
    weight_grad_out,
    grads,
    weights,
    sums_out,
    sums_in,
    accum,
    query_ref,
    key_ref,
    value_ref,
    query_grad_ref,
    weight_grad_ref,
    probs,
    probs_t,
    outs,
    outs_t,
    share_out,
    share_in,
    back_out,
    back_in,
    kv_grads,
    kv_in,
    kv_done,
    lengths_ref,
    own_sem,
    own_weight_sem,
    near_send,
    near_recv,
    far_send,
    far_recv,
    pass_send,
    pass_recv,
    mate_send,
    mate_recv,
    weight_send,
    weight_recv,
    sum_send,
    sum_recv,
    outs_send,
    outs_recv,
    share_send,
    share_recv,
    back_send,
    back_recv,
    kv_send,
    kv_recv,
    load_sem,
    query_sem,
    put_sem,
    kv_sem,
):
    dp_index = lax.axis_index("dp")
    tensor_index = lax.axis_index("tensor")
    chip_count = tensor_count // 2
    chip, core = tensor_index // 2, tensor_index % 2
    parity = chip % 2
    mate_chip = chip + 1 - 2 * parity
    mate = mate_chip * 2 + core
    partner = chip * 2 + 1 - core
    place = ring_place(dp_index, dp_count)
    ring = (
        ring_index((place + 1) % dp_count, dp_count),
        ring_index((place + dp_count - 1) % dp_count, dp_count),
    )
    rows = grad_ref.shape[0]
    depth, width = weight_ref.shape
    half, quarter = width // 2, width // 4
    last = dp_count - 1
    seq_len = query_full.shape[0]
    heads = depth // HEAD_SIZE
    half_rows = seq_len // 2
    score_scale = HEAD_SIZE ** (-0.5)
    middle = dp_count // 2
    forward_rows, backward_rows, window = block_sizes(seq_len, tensor_count)
    chip_blocks = 2 * rows // backward_rows
    kv_columns = pl.ds(pl.multiple_of(tensor_index // 2 * HEAD_SIZE, HEAD_SIZE), HEAD_SIZE)
    far_chips = [(chip + away) % chip_count for away in range(1, chip_count)]
    slots = (slice(0, depth), slice(depth, 2 * depth))

    def place_rows(index):
        return pl.ds(pl.multiple_of(index * rows, rows), rows)

    def own_columns(whose, side):
        return pl.ds(pl.multiple_of(whose * half + side * quarter, quarter), quarter)

    def columns(side, step, whose):
        if side == 0:
            owner = ring_index((place + 2 * dp_count - 1 - step) % dp_count, dp_count)
        else:
            owner = ring_index((place + 1 + step) % dp_count, dp_count)
        return pl.ds(
            pl.multiple_of(owner * width + whose * half + side * quarter, quarter), quarter
        )

    def remote(source, target, send, recv, dp_to, tensor_to):
        return pltpu.make_async_remote_copy(
            source, target, send, recv, device_id=(dp_to, tensor_to), device_id_type=MESH
        )

    def own_copy(side, step):
        return pltpu.make_async_copy(
            grad_ref.at[:, columns(side, step, parity)],
            grads.at[side, step, place_rows(tensor_index)],
            own_sem,
        )

    def own_weight(side):
        return pltpu.make_async_copy(
            weight_ref.at[:, own_columns(parity, side)],
            weights.at[side, last, slots[0]],
            own_weight_sem,
        )

    def mate_weight(side):
        return remote(
            weight_ref.at[:, own_columns(1 - parity, side)],
            weights.at[side, last, slots[1]],
            mate_send,
            mate_recv.at[side],
            dp_index,
            mate,
        )

    def near_copy(side, step):
        return remote(
            grad_ref.at[:, columns(side, step, parity)],
            grads.at[side, step, place_rows(tensor_index)],
            near_send,
            near_recv,
            dp_index,
            partner,
        )

    def far_copy(away, side, step):
        return remote(
            grad_ref.at[:, columns(side, step, far_chips[away] % 2)],
            grads.at[side, step, place_rows(tensor_index)],
            far_send.at[away],
            far_recv.at[away, step],
            dp_index,
            far_chips[away] * 2 + core,
        )

    def pass_copy(away, side, step):
        source = (chip + chip_count - 1 - away) % chip_count * 2 + core
        block = grads.at[side, step, place_rows(source)]
        return remote(
            block,
            block,
            pass_send.at[away],
            pass_recv.at[away, step],
            dp_index,
            partner,
        )

    def hop_step(hop, minor):
        return last - hop if minor else hop - 1

    def weight_copy(side, hop, minor, slot):
        if hop > 1:
            source = weights.at[side, hop_step(hop - 1, minor), slots[slot]]
        elif slot == 0:
            source = weight_ref.at[:, own_columns(parity, side)]
        else:
            source = weights.at[side, last, slots[1]]
        step = hop_step(hop, minor)
        return remote(
            source,
            weights.at[side, step, slots[slot]],
            weight_send,
            weight_recv.at[hop_step(hop, minor), slot],
            ring[1 - side if minor else side],
            tensor_index,
        )

    def sum_copy(side, step, slot):
        return remote(
            sums_out.at[side, step, slots[slot]],
            sums_in.at[side, step, slots[slot]],
            sum_send,
            sum_recv.at[step, slot],
            ring[side if step >= middle - 1 else 1 - side],
            tensor_index,
        )

    def block_of(owner_chip, part):
        return owner_chip * chip_blocks + part

    def block_rows(block):
        return pl.ds(pl.multiple_of(block * backward_rows, backward_rows), backward_rows)

    def share_copy(block):
        return remote(
            share_out.at[block_rows(block)],
            share_in.at[block_rows(block)],
            share_send,
            share_recv.at[block],
            dp_index,
            mate,
        )

    def back_copy(side):
        return remote(
            back_out.at[side],
            back_in.at[side],
            back_send,
            back_recv.at[side],
            dp_index,
            mate,
        )

    outs_copy = remote(outs_t.at[0], outs_t.at[1], outs_send, outs_recv, dp_index, mate)
    kv_copy = remote(
        kv_grads.at[:, pl.ds(pl.multiple_of((1 - core) * half_rows, half_rows), half_rows)],
        kv_in,
        kv_send,
        kv_recv,
        dp_index,
        partner,
    )

    targets = [(dp_index, partner), (ring[0], tensor_index), (ring[1], tensor_index)]
    targets += [(dp_index, other * 2 + core) for other in far_chips]
    barrier = pltpu.get_barrier_semaphore()
    for target in targets:
        pl.semaphore_signal(barrier, inc=1, device_id=target, device_id_type=MESH)
    loads = [
        pltpu.make_async_copy(query_full, query_ref, load_sem.at[0]),
        pltpu.make_async_copy(key_full.at[:, kv_columns], key_ref, load_sem.at[1]),
        pltpu.make_async_copy(value_full.at[:, kv_columns], value_ref, load_sem.at[2]),
        pltpu.make_async_copy(lengths_full, lengths_ref, load_sem.at[3]),
    ]
    for load in loads:
        load.start()
    pl.semaphore_wait(barrier, len(targets))

    def far_start(step):
        for side in (0, 1):
            for away in range(chip_count - 1):
                far_copy(away, side, step).start()

    grad_order = []
    for turn in range(middle):
        grad_order += [middle - 1 + turn] + ([middle - 2 - turn] if turn < middle - 1 else [])
    grad_order.append(last)
    for side in (0, 1):
        weight_copy(side, 1, 0, 0).start()
        mate_weight(side).start()
    for side in (0, 1):
        weight_copy(side, 1, 1, 0).start()
    far_start(grad_order[0])
    nt = (((1,), (1,)), ((), ()))
    tn = (((0,), (0,)), ((), ()))

    def dot(left, right, dims):
        return lax.dot_general(left, right, dims, preferred_element_type=jnp.float32)

    def window_start(index):
        skip, total = half_rows // forward_rows, seq_len // forward_rows
        past = (index + total - skip) // total
        return past * (index - skip) * forward_rows

    def window_keys(index):
        return pl.ds(pl.multiple_of(window_start(index), forward_rows), window)

    def forward(index):
        here = pl.ds(pl.multiple_of(index * forward_rows, forward_rows), forward_rows)
        query_places = index * forward_rows + lax.broadcasted_iota(jnp.int32, (forward_rows, 1), 0)
        key_places = window_start(index) + lax.broadcasted_iota(
            jnp.int32, (forward_rows, window), 1
        )
        doc_start = jnp.zeros((forward_rows, 1), jnp.int32)
        doc_end = jnp.int32(0)
        for doc in range(lengths_ref.shape[1]):
            doc_end = doc_end + lengths_ref[0, doc]
            doc_start = jnp.where(query_places >= doc_end, doc_end, doc_start)
        allowed = (key_places >= doc_start) & (key_places <= query_places)
        keys, values = key_ref[window_keys(index)], value_ref[window_keys(index)]
        for head in range(heads):
            lanes = slice(head * HEAD_SIZE, (head + 1) * HEAD_SIZE)
            scores = dot(query_ref[here, lanes], keys, nt) * score_scale
            scores = jnp.where(allowed, scores, -jnp.inf)
            row_max = jnp.max(scores, axis=1, keepdims=True)
            total = jnp.sum(jnp.exp(scores - row_max), axis=1, keepdims=True)
            prob = jnp.exp(scores - (row_max + jnp.log(total)))
            probs[head, here] = prob
            out = jnp.dot(prob.astype(jnp.bfloat16), values, preferred_element_type=jnp.float32)
            outs[here, lanes] = out.astype(jnp.bfloat16)
            outs_t[0, lanes, here] = out.T.astype(jnp.bfloat16)
            for part in range(forward_rows // backward_rows):
                piece = prob[part * backward_rows : (part + 1) * backward_rows]
                block = index * (forward_rows // backward_rows) + part
                probs_t[head, block] = piece.T.astype(jnp.bfloat16)

    def query_put(block):
        here = block_rows(block)
        return pltpu.make_async_copy(
            query_grad_ref.at[here], query_grad_out.at[here], query_sem
        )

    def backward(block):
        here = block_rows(block)
        index = block // (forward_rows // backward_rows)
        seen = window_keys(index)
        keys, values = key_ref[seen], value_ref[seen]
        share_copy(block).wait_recv()
        key_total, value_total = kv_grads[0, seen], kv_grads[1, seen]
        for head in range(heads):
            lanes = slice(head * HEAD_SIZE, (head + 1) * HEAD_SIZE)
            grad = (accum[here, lanes] + share_in[here, lanes].astype(jnp.float32)).astype(
                jnp.bfloat16
            )
            delta = jnp.sum(
                grad.astype(jnp.float32) * outs[here, lanes].astype(jnp.float32), axis=1, keepdims=True
            )
            dscore = probs[head, here] * (dot(grad, values, nt) - delta) * score_scale
            dscore = dscore.astype(jnp.bfloat16)
            query_grad_ref[here, lanes] = jnp.dot(
                dscore, keys, preferred_element_type=jnp.float32
            ).astype(jnp.bfloat16)
            key_total += dot(dscore, query_ref[here, lanes], tn)
            value_total += jnp.dot(probs_t[head, block], grad, preferred_element_type=jnp.float32)
        kv_grads[0, seen] = key_total
        kv_grads[1, seen] = value_total
        query_put(block).start()

    def chip_rows(owner_chip):
        return pl.ds(pl.multiple_of(owner_chip * (2 * rows), 2 * rows), 2 * rows)

    def project(owner_chip, steps):
        here = chip_rows(owner_chip)
        total = accum[here]
        for step in steps:
            for side in (0, 1):
                total += dot(grads[side, step, here], weights[side, step], nt)
        accum[here] = total

    def share(owner_chip):
        for part in range(chip_blocks):
            block = block_of(owner_chip, part)
            here = block_rows(block)
            share_out[here] = accum[here, slots[1]].astype(jnp.bfloat16)
            share_copy(block).start()

    def drain(ref, sem):
        pltpu.make_async_copy(ref, ref, sem).wait()

    def local_wait():
        drain(grads.at[:, :, place_rows(tensor_index)], own_sem)
        drain(grads.at[:, :, place_rows(partner)], near_recv)
        drain(weights.at[:, last, slots[0]], own_weight_sem)

    def weight_step(hop, minor, slot):
        step = hop_step(hop, minor)
        drain(weights.at[:, step, slots[slot]], weight_recv.at[step, slot])
        if hop + minor < middle:
            for side in (0, 1):
                weight_copy(side, hop + 1, minor, slot).start()

    def far_pass(step):
        for away in range(chip_count - 1):
            source = (chip + chip_count - 1 - away) % chip_count * 2 + core
            drain(grads.at[:, step, place_rows(source)], far_recv.at[away, step])
            for side in (0, 1):
                pass_copy(away, side, step).start()

    def pass_wait(step):
        for away in range(chip_count - 1):
            source = (chip + chip_count - 1 - away) % chip_count * 2 + 1 - core
            drain(grads.at[:, step, place_rows(source)], pass_recv.at[away, step])

    passed = set()

    def pass_wait_once(step):
        if step not in passed:
            passed.add(step)
            waiting.append(step)
            pass_wait(step)

    def sum_part(slot, side, step):
        return jnp.dot(outs_t[slot], grads[side, step], preferred_element_type=jnp.float32)

    def sum_step(slot, step):
        pass_wait_once(step)
        before = step - 1 if step >= middle - 1 else step + 1
        first = step in (middle - 2, middle - 1)
        for side in (0, 1):
            part = sum_part(slot, side, step)
            if not first:
                if side == 0:
                    drain(sums_in.at[:, before, slots[slot]], sum_recv.at[before, slot])
                part = part + sums_in[side, before, slots[slot]].astype(jnp.float32)
            sums_out[side, step, slots[slot]] = part.astype(jnp.bfloat16)
            sum_copy(side, step, slot).start()

    def weight_put(which, side):
        return pltpu.make_async_copy(
            weight_grad_ref.at[which, side],
            weight_grad_out.at[:, own_columns(parity if which == 0 else 1 - parity, side)],
            put_sem,
        )

    def sum_final(slot):
        for side in (0, 1):
            part = sum_part(slot, side, last)
            for before in (0, last - 1):
                if side == 0:
                    drain(sums_in.at[:, before, slots[slot]], sum_recv.at[before, slot])
                part = part + sums_in[side, before, slots[slot]].astype(jnp.float32)
            if slot == 0:
                weight_grad_ref[0, side] = part
                weight_put(0, side).start()
            else:
                back_out[side] = part.astype(jnp.bfloat16)
                back_copy(side).start()

    for load in loads:
        load.wait()
    blocks = seq_len // forward_rows
    forward(0)

    @pl.loop(0, dp_count)
    def _(step):
        for side in (0, 1):
            near_copy(side, step).start()
            own_copy(side, step).start()

    for side in (0, 1):
        own_weight(side).start()
    for index in range(1, blocks - 1):
        forward(index)
    weight_step(1, 0, 0)
    forward(blocks - 1)
    outs_copy.start()
    for step in grad_order[1:]:
        far_start(step)
    for side in (0, 1):
        mate_weight(side).wait_recv()
        for minor in (0, 1):
            weight_copy(side, 1, minor, 1).start()
    weight_step(1, 1, 0)
    accum[...] = jnp.zeros_like(accum)
    kv_grads[...] = jnp.zeros_like(kv_grads)
    local_wait()
    project(chip, [last])
    passing = list(grad_order)
    waiting = []

    def pass_next():
        far_pass(passing.pop(0))

    def far_project(steps):
        for other in far_chips:
            project(other, steps)
        waiting[:] = [step for step in waiting if step not in steps]

    for hop in range(2, middle):
        weight_step(hop, 0, 0)
        if hop == middle - 1:
            outs_copy.wait_recv()
            sum_step(1, grad_order[0])
        weight_step(hop - 1, 0, 1)
        if hop == middle - 1:
            pass_next()
            sum_step(0, grad_order[1])
            sum_step(1, grad_order[1])
        weight_step(hop - 1, 1, 1)
        weight_step(hop, 1, 0)
        if hop == middle - 2:
            pass_next()
        project(chip, [hop - 2, last + 1 - hop])
        if hop == middle - 2:
            sum_step(0, grad_order[0])
    pass_next()
    sum_step(1, grad_order[2])
    weight_step(middle, 0, 0)
    pass_next()
    sum_step(1, grad_order[3])
    weight_step(middle - 1, 0, 1)
    pass_next()
    weight_step(middle - 1, 1, 1)
    project(chip, [middle - 2, middle])
    far_project(grad_order[1:4])

    order = [(mate_chip + away) % chip_count for away in range(chip_count)]
    for number in range(4, last):
        if number == 6:
            weight_step(middle, 0, 1)
            project(chip, [middle - 1])
            share(chip)
            pass_next()
            far_project(list(waiting))
        sum_step(1, grad_order[number])
        if number != 5:
            pass_next()
        sum_step(0, grad_order[number - 2])
    pass_wait_once(last)
    far_project(list(waiting))
    for other in far_chips:
        share(other)
    sum_step(0, grad_order[last - 2])
    for part in range(chip_blocks):
        backward(block_of(order[0], part))
    sum_final(1)
    sum_step(0, grad_order[last - 1])
    for owner in order[1:]:
        for part in range(chip_blocks):
            backward(block_of(owner, part))
    kv_copy.start()
    mine = pl.ds(pl.multiple_of(core * half_rows, half_rows), half_rows)
    kv_copy.wait()
    kv_done[...] = (kv_grads[:, mine] + kv_in[...]).astype(jnp.bfloat16)
    kv_puts = [
        pltpu.make_async_copy(kv_done.at[which], to, kv_sem.at[which])
        for which, to in enumerate((key_grad_out, value_grad_out))
    ]
    for put in kv_puts:
        put.start()

    drain(weights.at[:, last, slots[1]], mate_send)
    drain(grads.at[:, :, place_rows(tensor_index)], near_send)
    for away in range(chip_count - 1):
        drain(grads.at[:, :, place_rows(tensor_index)], far_send.at[away])
        drain(grads.at[:, :, place_rows(tensor_index)], pass_send.at[away])
    drain(weights.at[:, pl.ds(0, last)], weight_send)
    outs_copy.wait_send()
    drain(share_out, share_send)
    drain(query_grad_ref, query_sem)
    for put in kv_puts:
        put.wait()
    sum_final(0)
    for side in (0, 1):
        back_copy(side).wait_recv()
        weight_grad_ref[1, side] = back_in[side].astype(jnp.float32)
        weight_put(1, side).start()
    drain(back_out, back_send)
    drain(sums_out, sum_send)
    drain(weight_grad_ref, put_sem)


def finish_kernel(*refs):
    count = (len(refs) - 1) // 2
    puts = [
        pltpu.make_async_copy(refs[i], refs[count + i], refs[2 * count].at[i]) for i in range(count)
    ]
    for put in puts:
        put.start()
    for put in puts:
        put.wait()


def finish(*values):
    anywhere = pl.BlockSpec(memory_space=pl.ANY)
    return pl.pallas_call(
        finish_kernel,
        out_shape=tuple(pltpu.HBM(value.shape, value.dtype) for value in values),
        in_specs=[anywhere] * len(values),
        out_specs=(anywhere,) * len(values),
        scratch_shapes=[pltpu.SemaphoreType.DMA((len(values),))],
        compiler_params=pltpu.CompilerParams(vmem_limit_bytes=8 * 1024 * 1024),
        name="finish",
    )(*values)


def shards(query_act, rotated_keys, value_input, grad_out, out_weight, doc_lengths):
    dp_count, tensor_count = lax.axis_size("dp"), lax.axis_size("tensor")
    chip_count = tensor_count // 2
    far = chip_count - 1
    seq_len = query_act.shape[1]
    depth, width = out_weight.shape
    quarter = width // 4
    heads = depth // HEAD_SIZE
    forward_rows, backward_rows, window = block_sizes(seq_len, tensor_count)
    blocks = seq_len // backward_rows
    dma = pltpu.SemaphoreType.DMA
    anywhere = pl.BlockSpec(memory_space=pl.ANY)
    low, full = jnp.bfloat16, jnp.float32
    kv_shape = pltpu.VMEM((seq_len // 2, HEAD_SIZE), low)
    query_grad, key_grad, value_grad, weight_grad = pl.pallas_call(
        functools.partial(exchange_kernel, dp_count, tensor_count),
        out_shape=(
            pltpu.VMEM((seq_len, depth), low),
            kv_shape,
            kv_shape,
            pltpu.VMEM((depth, width), full),
        ),
        in_specs=[pl.BlockSpec(memory_space=pltpu.HBM)] * 6,
        out_specs=(anywhere,) * 4,
        scratch_shapes=[
            pltpu.VMEM((2, dp_count, seq_len, quarter), low),
            pltpu.VMEM((2, dp_count, 2 * depth, quarter), low),
            pltpu.VMEM((2, dp_count - 1, 2 * depth, quarter), low),
            pltpu.VMEM((2, dp_count - 1, 2 * depth, quarter), low),
            pltpu.VMEM((seq_len, 2 * depth), full),
            pltpu.VMEM((seq_len, depth), low),
            pltpu.VMEM((seq_len, HEAD_SIZE), low),
            pltpu.VMEM((seq_len, HEAD_SIZE), low),
            pltpu.VMEM((seq_len, depth), low),
            pltpu.VMEM((2, 2, depth, quarter), full),
            pltpu.VMEM((heads, seq_len, window), full),
            pltpu.VMEM((heads, blocks, window, backward_rows), low),
            pltpu.VMEM((seq_len, depth), low),
            pltpu.VMEM((2, depth, seq_len), low),
            pltpu.VMEM((seq_len, depth), low),
            pltpu.VMEM((seq_len, depth), low),
            pltpu.VMEM((2, depth, quarter), low),
            pltpu.VMEM((2, depth, quarter), low),
            pltpu.VMEM((2, seq_len, HEAD_SIZE), full),
            pltpu.VMEM((2, seq_len // 2, HEAD_SIZE), full),
            pltpu.VMEM((2, seq_len // 2, HEAD_SIZE), low),
            pltpu.SMEM(doc_lengths.shape, jnp.int32),
            dma,
            dma,
            dma,
            dma,
            dma((far,)),
            dma((far, dp_count)),
            dma((far,)),
            dma((far, dp_count)),
            dma,
            dma((2,)),
            dma,
            dma((dp_count - 1, 2)),
            dma,
            dma((dp_count - 1, 2)),
            dma,
            dma,
            dma,
            dma((blocks,)),
            dma,
            dma((2,)),
            dma,
            dma,
            dma((4,)),
            dma,
            dma,
            dma((2,)),
        ],
        compiler_params=pltpu.CompilerParams(
            collective_id=0, has_side_effects=True, vmem_limit_bytes=54 * 1024 * 1024
        ),
        name="exchange",
    )(grad_out[0], out_weight, query_act[0], rotated_keys[0], value_input[0], doc_lengths)
    query_grad, key_grad, value_grad, weight_grad = finish(
        query_grad, key_grad, value_grad, weight_grad
    )
    return (query_grad[None], key_grad[None, None], value_grad[None, None], weight_grad)


def solution(mesh):
    placed = (
        P("dp", None, "tensor"),
        P("dp", None, None),
        P("dp", None, None),
        P("dp", "tensor", None),
        P("tensor", "dp"),
        P("dp", None),
    )
    return jax.shard_map(
        shards,
        mesh=mesh,
        in_specs=placed,
        out_specs=(
            P("dp", None, "tensor"),
            P("dp", "tensor", None, None),
            P("dp", "tensor", None, None),
            P("tensor", "dp"),
        ),
        check_vma=False,
    )
```

```python
import functools

import jax
import jax.numpy as jnp
from jax import lax
from jax.experimental import pallas as pl
from jax.experimental.pallas import tpu as pltpu
from jax.sharding import PartitionSpec as P

HEAD_SIZE = 128


MESH = pl.DeviceIdType.MESH


def block_sizes(seq_len, tensor_count):
    rows = seq_len // tensor_count
    forward_rows = min(256, seq_len)
    part_rows = rows // max(1, rows // 128)
    block_rows = max(part_rows, min(128, 2 * rows))
    return forward_rows, part_rows, block_rows, seq_len // 2 + forward_rows


def exchange_kernel(
    dp_count,
    tensor_count,
    grad_ref,
    weight_ref,
    query_full,
    key_full,
    value_full,
    lengths_full,
    query_grad_out,
    key_grad_out,
    value_grad_out,
    weight_grad_out,
    grads,
    weights,
    sums_out,
    sums_in,
    cross_out,
    cross_in,
    accum,
    query_ref,
    key_ref,
    value_ref,
    query_grad_ref,
    weight_grad_ref,
    probs,
    probs_t,
    outs,
    outs_own,
    outs_t,
    share_out,
    share_in,
    turn_out,
    out_grad,
    back_out,
    back_in,
    kv_grads,
    kv_in,
    kv_done,
    lengths_ref,
    own_sem,
    near_send,
    near_recv,
    far_send,
    far_recv,
    pass_send,
    pass_recv,
    line_send,
    line_recv,
    total_recv,
    wing_send,
    wing_recv,
    cross_send,
    cross_recv,
    outs_send,
    outs_recv,
    share_send,
    share_recv,
    turn_send,
    turn_recv,
    back_send,
    back_recv,
    kv_send,
    kv_recv,
    load_sem,
    query_sem,
    put_sem,
    kv_sem,
):
    dp_index = lax.axis_index("dp")
    tensor_index = lax.axis_index("tensor")
    chip_count = tensor_count // 2
    pairs = chip_count // 2
    spots = dp_count // 2
    chip, core = tensor_index // 2, tensor_index % 2
    pair, parity = chip // 2, chip % 2
    mate = (pair * 2 + 1 - parity) * 2 + core
    partner = chip * 2 + 1 - core
    spot, lane = dp_index // 2, dp_index % 2
    twin = spot * 2 + 1 - lane
    rows = grad_ref.shape[0]
    depth, width = weight_ref.shape
    half = width // 2
    seq_len = query_full.shape[0]
    heads = depth // HEAD_SIZE
    half_rows = seq_len // 2
    score_scale = HEAD_SIZE ** (-0.5)
    forward_rows, part_rows, back_rows, window = block_sizes(seq_len, tensor_count)
    kv_columns = pl.ds(pl.multiple_of(tensor_index // 2 * HEAD_SIZE, HEAD_SIZE), HEAD_SIZE)
    slots = (slice(0, depth), slice(depth, 2 * depth))
    sides = (slice(0, half), slice(half, width))
    chunks = ((0, 0), (0, 1), (1, 0))
    ways = (1, -1)
    routes = [(away, whose) for whose in (1, 0) for away in range(pairs) if away or whose]
    fars = len(routes)
    pieces = rows // part_rows

    def exists(way):
        return spot <= spots - 2 if way > 0 else spot >= 1

    def reaches(way, far):
        return spot + far <= spots - 1 if way > 0 else spot >= far

    def local_rows(whose, which_pair, which_core):
        start = ((whose * pairs + which_pair) * 2 + which_core) * rows
        return pl.ds(pl.multiple_of(start, rows), rows)

    def columns(which_lane, block, side):
        start = (2 * block + which_lane) * width + side * half
        return pl.ds(pl.multiple_of(start, half), half)

    def remote(source, target, send, recv, dp_to, tensor_to):
        return pltpu.make_async_remote_copy(
            source, target, send, recv, device_id=(dp_to, tensor_to), device_id_type=MESH
        )

    def drain(ref, sem):
        pltpu.make_async_copy(ref, ref, sem).wait()

    def own_copy(side, block):
        return pltpu.make_async_copy(
            grad_ref.at[:, columns(lane, block, side)],
            grads.at[side, block, local_rows(0, pair, core)],
            own_sem.at[0],
        )

    def own_weight(side):
        return pltpu.make_async_copy(
            weight_ref.at[:, sides[side]], weights.at[side, spot, slots[0]], own_sem.at[1]
        )

    def near_copy(side, block):
        return remote(
            grad_ref.at[:, columns(lane, block, side)],
            grads.at[side, block, local_rows(0, pair, core)],
            near_send,
            near_recv,
            dp_index,
            partner,
        )

    def far_copy(route, side, block):
        away, whose = routes[route]
        return remote(
            grad_ref.at[:, columns(1 - lane if whose else lane, block, side)],
            grads.at[side, block, local_rows(whose, pair, core)],
            far_send.at[route],
            far_recv.at[route, block],
            twin if whose else dp_index,
            ((pair + away) % pairs * 2 + parity) * 2 + core,
        )

    def source_rows(route, which_core):
        away, whose = routes[route]
        return local_rows(whose, (pair + pairs - away) % pairs, which_core)

    def pass_copy(route, side, block):
        piece = grads.at[side, block, source_rows(route, core)]
        return remote(
            piece, piece, pass_send.at[route], pass_recv.at[route, block], dp_index, partner
        )

    def piece_rows(rows_slice, piece):
        return pl.ds(
            pl.multiple_of(rows_slice.start + piece * part_rows, part_rows), part_rows
        )

    def last_copy(route, piece):
        away, whose = routes[route]
        return remote(
            grad_ref.at[
                slice(piece * part_rows, (piece + 1) * part_rows),
                columns(1 - lane if whose else lane, spot, 0),
            ],
            grads.at[0, spot, piece_rows(local_rows(whose, pair, core), piece)],
            far_send.at[route],
            far_recv.at[route, spots + piece],
            twin if whose else dp_index,
            ((pair + away) % pairs * 2 + parity) * 2 + core,
        )

    def last_pass_copy(route, piece):
        here = grads.at[0, spot, piece_rows(source_rows(route, core), piece)]
        return remote(
            here,
            here,
            pass_send.at[route],
            pass_recv.at[route, spots + piece],
            dp_index,
            partner,
        )

    def line_copy(way, far, chunk):
        side, slot = chunks[chunk]
        block = spot - way * far
        if far == 0 and slot == 0:
            source = weight_ref.at[:, sides[side]]
        else:
            source = weights.at[side, block, slots[slot]]
        return remote(
            source,
            weights.at[side, block, slots[slot]],
            line_send.at[(1 - way) // 2],
            line_recv.at[chunk, block],
            dp_index + 2 * way,
            tensor_index,
        )

    def wing_copy(block, side=1, own=False):
        return remote(
            weight_ref.at[:, sides[side]] if own else weights.at[side, block, slots[0]],
            weights.at[side, block, slots[1]],
            wing_send,
            wing_recv.at[block if side else spots],
            dp_index,
            mate,
        )

    def total_copy(way, far, chunk):
        owner = spot + way * far
        index = spots if way < 0 and far == 1 else owner
        return remote(
            sums_out.at[chunk, owner],
            sums_in.at[chunk, index],
            line_send.at[(1 - way) // 2],
            total_recv.at[chunk, index],
            dp_index + 2 * way,
            tensor_index,
        )

    def cross_copy(block):
        return remote(
            cross_out.at[block],
            cross_in.at[block],
            cross_send,
            cross_recv.at[block],
            dp_index,
            mate,
        )

    def chip_lanes(which_pair, which_parity):
        start = (2 * which_pair + which_parity) * 2 * rows
        return pl.ds(pl.multiple_of(start, 2 * rows), 2 * rows)

    def outs_copy(kind, which_pair):
        here = slice(which_pair * 2 * rows, (which_pair + 1) * 2 * rows)
        there = slice(half_rows + which_pair * 2 * rows, half_rows + (which_pair + 1) * 2 * rows)
        own = outs_own.at[:, chip_lanes(which_pair, parity)]
        if kind == 0:
            return pltpu.make_async_copy(own, outs_t.at[0, :, here], own_sem.at[2])
        if kind == 1:
            other = outs_own.at[:, chip_lanes(which_pair, 1 - parity)]
            return remote(
                other, outs_t.at[1, :, here], outs_send.at[0], outs_recv.at[0], dp_index, mate
            )
        if kind == 2:
            return remote(
                own, outs_t.at[0, :, there], outs_send.at[1], outs_recv.at[1], twin, tensor_index
            )
        return remote(
            outs_t.at[1, :, here],
            outs_t.at[1, :, there],
            outs_send.at[2],
            outs_recv.at[2],
            twin,
            tensor_index,
        )

    parts = [
        (which_pair, which_core, piece)
        for piece in range(rows // part_rows)
        for which_pair in range(pairs)
        for which_core in (0, 1)
    ]

    def part_start(part):
        which_pair, which_core, piece = parts[part]
        return (which_pair * 2 + which_core) * rows + piece * part_rows

    def part_slice(part):
        return slice(part_start(part), part_start(part) + part_rows)

    def share_copy(part):
        here = part_slice(part)
        return remote(
            share_out.at[here],
            share_in.at[here],
            share_send,
            share_recv.at[part],
            twin,
            tensor_index,
        )

    def turn_copy(part):
        here = part_slice(part)
        return remote(
            turn_out.at[here], out_grad.at[1, here], turn_send, turn_recv.at[part], dp_index, mate
        )

    def back_copy(part):
        here = slice(part * (depth // len(parts)), (part + 1) * (depth // len(parts)))
        return remote(back_out.at[here], back_in.at[here], back_send, back_recv, dp_index, mate)

    kv_copy = remote(
        kv_grads.at[:, pl.ds(pl.multiple_of((1 - core) * half_rows, half_rows), half_rows)],
        kv_in,
        kv_send,
        kv_recv,
        dp_index,
        partner,
    )

    targets = [(dp_index, partner), (dp_index, mate), (twin, tensor_index)]
    for away in range(1, pairs):
        other = ((pair + away) % pairs * 2 + parity) * 2 + core
        targets += [(dp_index, other), (twin, other)]
    barrier = pltpu.get_barrier_semaphore()
    for target in targets:
        pl.semaphore_signal(barrier, inc=1, device_id=target, device_id_type=MESH)
    for way in ways:

        @pl.when(exists(way))
        def _():
            pl.semaphore_signal(
                barrier,
                inc=1,
                device_id=(dp_index + 2 * way, tensor_index),
                device_id_type=MESH,
            )

    loads = [
        pltpu.make_async_copy(query_full, query_ref, load_sem.at[0]),
        pltpu.make_async_copy(key_full.at[:, kv_columns], key_ref, load_sem.at[1]),
        pltpu.make_async_copy(value_full.at[:, kv_columns], value_ref, load_sem.at[2]),
        pltpu.make_async_copy(lengths_full, lengths_ref, load_sem.at[3]),
    ]
    for load in loads:
        load.start()
    beside = (spot + spots - 2) // (spots - 1) + (2 * spots - 3 - spot) // (spots - 1)
    pl.semaphore_wait(barrier, len(targets) + beside)

    upper = (2 * spot) // spots
    first_block = (1 - upper) * (spots - 1)

    def far_start(block):
        for side in (0, 1):
            for route in range(fars):
                far_copy(route, side, block).start()

    def line_start(chunk):
        for way in ways:

            @pl.when(exists(way))
            def _():
                line_copy(way, 0, chunk).start()

    line_start(2)
    wing_copy(spot, 0, True).start()
    far_start(first_block)
    line_start(0)
    nt = (((1,), (1,)), ((), ()))
    tn = (((0,), (0,)), ((), ()))

    def dot(left, right, dims):
        return lax.dot_general(left, right, dims, preferred_element_type=jnp.float32)

    def window_start(index):
        skip, total = half_rows // forward_rows, seq_len // forward_rows
        past = (index + total - skip) // total
        return past * (index - skip) * forward_rows

    def window_keys(index):
        return pl.ds(pl.multiple_of(window_start(index), forward_rows), window)

    def forward(index):
        here = pl.ds(pl.multiple_of(index * forward_rows, forward_rows), forward_rows)
        query_places = index * forward_rows + lax.broadcasted_iota(jnp.int32, (forward_rows, 1), 0)
        key_places = window_start(index) + lax.broadcasted_iota(
            jnp.int32, (forward_rows, window), 1
        )
        doc_start = jnp.zeros((forward_rows, 1), jnp.int32)
        doc_end = jnp.int32(0)
        for doc in range(lengths_ref.shape[1]):
            doc_end = doc_end + lengths_ref[0, doc]
            doc_start = jnp.where(query_places >= doc_end, doc_end, doc_start)
        allowed = (key_places >= doc_start) & (key_places <= query_places)
        keys, values = key_ref[window_keys(index)], value_ref[window_keys(index)]
        for head in range(heads):
            lanes = slice(head * HEAD_SIZE, (head + 1) * HEAD_SIZE)
            scores = dot(query_ref[here, lanes], keys, nt) * score_scale
            scores = jnp.where(allowed, scores, -jnp.inf)
            row_max = jnp.max(scores, axis=1, keepdims=True)
            total = jnp.sum(jnp.exp(scores - row_max), axis=1, keepdims=True)
            prob = jnp.exp(scores - (row_max + jnp.log(total)))
            probs[head, here] = prob
            out = jnp.dot(prob.astype(jnp.bfloat16), values, preferred_element_type=jnp.float32)
            outs[here, lanes] = out.astype(jnp.bfloat16)
            outs_own[lanes, here] = out.T.astype(jnp.bfloat16)
            for part in range(forward_rows // back_rows):
                piece = prob[part * back_rows : (part + 1) * back_rows]
                block = index * (forward_rows // back_rows) + part
                probs_t[head, block] = piece.T.astype(jnp.bfloat16)

    def backward(which, start):
        whose = parity if which == 0 else 1 - parity
        place = start // (2 * rows) * 4 * rows + start % (2 * rows)
        block = place // back_rows + whose * (2 * rows // back_rows)
        here = pl.ds(pl.multiple_of(block * back_rows, back_rows), back_rows)
        seen = window_keys(block // (forward_rows // back_rows))
        keys, values = key_ref[seen], value_ref[seen]
        key_total, value_total = kv_grads[0, seen], kv_grads[1, seen]
        for head in range(heads):
            lanes = slice(head * HEAD_SIZE, (head + 1) * HEAD_SIZE)
            grad = out_grad[which, start : start + back_rows, lanes]
            delta = jnp.sum(
                grad.astype(jnp.float32) * outs[here, lanes].astype(jnp.float32), axis=1, keepdims=True
            )
            dscore = probs[head, here] * (dot(grad, values, nt) - delta) * score_scale
            dscore = dscore.astype(jnp.bfloat16)
            query_grad_ref[here, lanes] = jnp.dot(
                dscore, keys, preferred_element_type=jnp.float32
            ).astype(jnp.bfloat16)
            key_total += dot(dscore, query_ref[here, lanes], tn)
            value_total += jnp.dot(probs_t[head, block], grad, preferred_element_type=jnp.float32)
        kv_grads[0, seen] = key_total
        kv_grads[1, seen] = value_total
        pltpu.make_async_copy(
            query_grad_ref.at[here], query_grad_out.at[here], query_sem
        ).start()

    def project(block, whose, which=(0, 1), piece=None):
        if piece is None:
            areas = [slice(whose * half_rows, (whose + 1) * half_rows)]
        else:
            areas = [
                slice(half_rows + part_start(part), half_rows + part_start(part) + part_rows)
                for part in range(len(parts))
                if parts[part][2] == piece
            ]
        for here in areas:
            total = accum[here]
            for side in which:
                total += dot(grads[side, block, here], weights[side, block], nt)
            accum[here] = total

    def line_hop(far, chunk):
        side, slot = chunks[chunk]
        for way in ways:

            @pl.when(reaches(-way, far))
            def _():
                block = spot - way * far
                drain(weights.at[side, block, slots[slot]], line_recv.at[chunk, block])

                @pl.when(exists(way))
                def _():
                    line_copy(way, far, chunk).start()

                if chunk == 2:
                    wing_copy(block).start()

    def wing_wait(block, side=1):
        drain(weights.at[side, block, slots[1]], wing_recv.at[block if side else spots])

    def hop_project(far):
        for way in ways:

            @pl.when(reaches(-way, far))
            def _():
                wing_wait(spot - way * far)
                project(spot - way * far, 0)

    def far_pass(block, which=(0, 1)):
        for route in range(fars):
            for side in which[:1] if len(which) == 1 else ():
                drain(grads.at[side, block, source_rows(route, core)], far_recv.at[route, block])
            if len(which) == 2:
                drain(grads.at[:, block, source_rows(route, core)], far_recv.at[route, block])
            for side in which:
                pass_copy(route, side, block).start()

    def pass_wait(block, which=(0, 1)):
        for route in range(fars):
            there = source_rows(route, 1 - core)
            if len(which) == 2:
                drain(grads.at[:, block, there], pass_recv.at[route, block])
            else:
                drain(grads.at[which[0], block, there], pass_recv.at[route, block])

    def last_pass(piece):
        for route in range(fars):
            here = piece_rows(source_rows(route, core), piece)
            drain(grads.at[0, spot, here], far_recv.at[route, spots + piece])
            last_pass_copy(route, piece).start()

    def last_wait(piece):
        for route in range(fars):
            here = piece_rows(source_rows(route, 1 - core), piece)
            drain(grads.at[0, spot, here], pass_recv.at[route, spots + piece])

    def sum_part(slot, side, block):
        return jnp.dot(outs_t[slot], grads[side, block], preferred_element_type=jnp.float32)

    def cross(block):
        cross_out[block] = sum_part(1, 1, block).astype(jnp.bfloat16)
        cross_copy(block).start()

    def owner_do(far, work):
        for way in ways:

            @pl.when(reaches(way, far))
            def _():
                work(way, spot + way * far)

    def total_sum(chunk, owner):
        side, slot = chunks[chunk]
        part = sum_part(slot, side, owner) + sums_in[chunk, owner].astype(jnp.float32)
        if side:
            drain(cross_in.at[owner], cross_recv.at[owner])
            part = part + cross_in[owner].astype(jnp.float32)
        sums_out[chunk, owner] = part.astype(jnp.bfloat16)

    def total_step(far, chunk):
        def work(way, owner):
            @pl.when(owner != first_block)
            def _():
                @pl.when(exists(-way))
                def _():
                    drain(sums_in.at[chunk, owner], total_recv.at[chunk, owner])

                total_sum(chunk, owner)
                total_copy(way, far, chunk).start()

        owner_do(far, work)

    def total_first(chunk, at_end):
        edge = spot % (spots - 1)

        @pl.when(edge == 0 if at_end else edge != 0)
        def _():
            if not at_end:
                drain(sums_in.at[chunk, first_block], total_recv.at[chunk, first_block])
            total_sum(chunk, first_block)
            remote(
                sums_out.at[chunk, first_block],
                sums_in.at[chunk, first_block],
                line_send.at[upper],
                total_recv.at[chunk, first_block],
                dp_index + 2 - 4 * upper,
                tensor_index,
            ).start()

    def total_final(chunk):
        side, slot = chunks[chunk]
        part = sum_part(slot, side, spot)
        if side:
            drain(cross_in.at[spot], cross_recv.at[spot])
            part = part + cross_in[spot].astype(jnp.float32)
        for way, index in ((-1, spot), (1, spots)):

            @pl.when(exists(way))
            def _():
                drain(sums_in.at[chunk, index], total_recv.at[chunk, index])

            part = part + sums_in[chunk, index].astype(jnp.float32)
        return part

    def weight_put(side):
        return pltpu.make_async_copy(
            weight_grad_ref.at[side], weight_grad_out.at[:, sides[side]], put_sem
        )

    def share(piece):
        for part in range(len(parts)):
            if parts[part][2] == piece:
                here = part_slice(part)
                there = slice(half_rows + here.start, half_rows + here.stop)
                share_out[here] = accum[there].astype(jnp.bfloat16)
                share_copy(part).start()

    def settle(part):
        here = part_slice(part)
        share_copy(part).wait_recv()
        both = (accum[here] + share_in[here].astype(jnp.float32)).astype(jnp.bfloat16)
        turn_out[here] = both[:, slots[1]]
        turn_copy(part).start()
        out_grad[0, here] = both[:, slots[0]]

    def finished(part):
        start = part_start(part)
        if back_rows == part_rows:
            return start
        return start - rows if parts[part][1] == 1 else None

    for load in loads:
        load.wait()
    blocks = seq_len // forward_rows
    forward(0)

    @pl.loop(0, spots)
    def _(block):
        for side in (0, 1):
            near_copy(side, block).start()
            own_copy(side, block).start()

    for side in (0, 1):
        own_weight(side).start()
    for index in range(1, blocks):
        forward(index)
    for which_pair in range(pairs):
        outs_copy(1, which_pair).start()
        outs_copy(2, which_pair).start()
        outs_copy(0, which_pair).start()
    wing_copy(spot, 1, True).start()
    line_hop(1, 2)
    wing_wait(spot, 0)
    line_start(1)
    line_hop(1, 0)

    accum[...] = jnp.zeros_like(accum)
    kv_grads[...] = jnp.zeros_like(kv_grads)
    for way in ways:

        @pl.when(reaches(way, spots - 1))
        def _():
            for chunk in range(3):
                for index in range(spots + 1):
                    if index != (spots if way > 0 else spots - 1):
                        sums_in[chunk, index] = jnp.zeros_like(sums_in[chunk, index])

    drain(grads.at[:, :, local_rows(0, pair, core)], own_sem.at[0])
    drain(weights.at[:, spot, slots[0]], own_sem.at[1])
    drain(outs_t.at[0, :, slice(0, half_rows)], own_sem.at[2])
    drain(grads.at[:, :, local_rows(0, pair, 1 - core)], near_recv)
    def pass_rest(far):
        def work(way, owner):
            @pl.when(owner != first_block)
            def _():
                far_pass(owner)

        owner_do(far, work)

    drain(outs_t.at[1, :, slice(0, half_rows)], outs_recv.at[0])
    for which_pair in range(pairs):
        outs_copy(3, which_pair).start()

    def rest_start(far):
        def work(way, owner):
            if far > 1 or spots == 2:

                @pl.when(owner != first_block)
                def _():
                    far_start(owner)

            else:
                far_start(owner)

        owner_do(far, work)

    for far in range(spots - 1, 0, -1):
        rest_start(far)
    for route in range(fars):
        far_copy(route, 1, spot).start()
    for piece in range(pieces):
        for route in range(fars):
            last_copy(route, piece).start()
    def rest_do(far, work):
        def inner(way, owner):
            @pl.when(owner != first_block)
            def _():
                work(owner)

        owner_do(far, inner)

    def both_project(far):
        owner_do(far, lambda way, owner: project(owner, 1))

    far_pass(first_block)
    drain(outs_t.at[0, :, slice(half_rows, seq_len)], outs_recv.at[1])
    pass_wait(first_block)
    total_first(0, True)
    line_hop(1, 1)
    drain(outs_t.at[1, :, slice(half_rows, seq_len)], outs_recv.at[2])
    cross(first_block)
    total_first(1, True)
    line_hop(2, 2)
    line_hop(2, 0)
    total_first(0, False)
    wing_wait(spot)
    project(spot, 0)
    total_first(2, True)
    total_first(1, False)
    line_hop(2, 1)
    hop_project(1)
    for far in range(spots - 2, 0, -1):
        hop = spots - far + 1
        pass_rest(far)
        rest_do(far, pass_wait)
        rest_do(far, cross)
        total_step(far, 1)
        total_step(far, 0)
        if far == spots - 2:
            total_first(2, False)
            hop_project(2)
        if far <= spots // 2:
            both_project(far)
        if far == 1:
            far_pass(spot, (1,))
            line_hop(spots - 1, 1)
            hop_project(spots - 1)
            both_project(spots - 1)
            pass_wait(spot, (1,))
            cross(spot)
            project(spot, 1, (1,))
            last_pass(0)
        if hop < spots:
            line_hop(hop, 2)
            line_hop(hop, 0)
        if far > 1:
            total_step(far, 2)
        if hop < spots - 1:
            line_hop(hop, 1)
            hop_project(hop)
            if hop > spots // 2:
                both_project(hop)
    for piece in range(pieces):
        last_wait(piece)
        project(spot, 1, (0,), piece)
        share(piece)
        if piece + 1 < pieces:
            last_pass(piece + 1)

    total_step(1, 2)
    back_out[...] = total_final(1).astype(jnp.bfloat16)
    later = []
    for part in range(len(parts)):
        settle(part)
        back_copy(part).start()
        if finished(part) is not None:
            backward(0, finished(part))
        if part == len(parts) - 2:
            weight_grad_ref[0] = total_final(0)
        for earlier in later:
            turn_copy(earlier).wait_recv()
            if finished(earlier) is not None:
                backward(1, finished(earlier))
        later = [part]
    weight_grad_ref[1] = total_final(2)
    weight_put(1).start()
    turn_copy(later[0]).wait_recv()
    backward(1, finished(later[0]))
    kv_copy.start()
    drain(back_in, back_recv)
    weight_grad_ref[0] = weight_grad_ref[0] + back_in[...].astype(jnp.float32)
    weight_put(0).start()
    mine = pl.ds(pl.multiple_of(core * half_rows, half_rows), half_rows)
    kv_copy.wait()
    kv_done[...] = (kv_grads[:, mine] + kv_in[...]).astype(jnp.bfloat16)
    kv_puts = [
        pltpu.make_async_copy(kv_done.at[which], to, kv_sem.at[which])
        for which, to in enumerate((key_grad_out, value_grad_out))
    ]
    for put in kv_puts:
        put.start()

    drain(grads.at[:, :, local_rows(0, pair, core)], near_send)
    for route in range(fars):
        drain(grads.at[:, :, local_rows(0, pair, core)], far_send.at[route])
        drain(grads.at[:, :, local_rows(0, pair, core)], pass_send.at[route])
    for index in range(3):
        drain(outs_t.at[0, :, slice(0, half_rows)], outs_send.at[index])
    drain(share_out, share_send)
    drain(turn_out, turn_send)
    drain(query_grad_ref, query_sem)
    for put in kv_puts:
        put.wait()
    drain(sums_in.at[0], wing_send)
    drain(cross_out, cross_send)
    drain(back_out, back_send)
    for way in ways:

        @pl.when(exists(way))
        def _():
            drain(grads.at[0, :, slice(0, 3 * depth)], line_send.at[(1 - way) // 2])

    drain(weight_grad_ref, put_sem)


def finish_kernel(*refs):
    count = (len(refs) - 1) // 2
    puts = [
        pltpu.make_async_copy(refs[i], refs[count + i], refs[2 * count].at[i]) for i in range(count)
    ]
    for put in puts:
        put.start()
    for put in puts:
        put.wait()


def finish(*values):
    anywhere = pl.BlockSpec(memory_space=pl.ANY)
    return pl.pallas_call(
        finish_kernel,
        out_shape=tuple(pltpu.HBM(value.shape, value.dtype) for value in values),
        in_specs=[anywhere] * len(values),
        out_specs=(anywhere,) * len(values),
        scratch_shapes=[pltpu.SemaphoreType.DMA((len(values),))],
        compiler_params=pltpu.CompilerParams(vmem_limit_bytes=8 * 1024 * 1024),
        name="finish",
    )(*values)


def shards(query_act, rotated_keys, value_input, grad_out, out_weight, doc_lengths):
    dp_count, tensor_count = lax.axis_size("dp"), lax.axis_size("tensor")
    spots = dp_count // 2
    fars = tensor_count // 2 - 1
    seq_len = query_act.shape[1]
    depth, width = out_weight.shape
    half = width // 2
    heads = depth // HEAD_SIZE
    forward_rows, part_rows, back_rows, window = block_sizes(seq_len, tensor_count)
    parts = seq_len // 2 // part_rows
    pieces = seq_len // tensor_count // part_rows
    dma = pltpu.SemaphoreType.DMA
    anywhere = pl.BlockSpec(memory_space=pl.ANY)
    low, full = jnp.bfloat16, jnp.float32
    kv_shape = pltpu.VMEM((seq_len // 2, HEAD_SIZE), low)
    query_grad, key_grad, value_grad, weight_grad = pl.pallas_call(
        functools.partial(exchange_kernel, dp_count, tensor_count),
        out_shape=(
            pltpu.VMEM((seq_len, depth), low),
            kv_shape,
            kv_shape,
            pltpu.VMEM((depth, width), full),
        ),
        in_specs=[pl.BlockSpec(memory_space=pltpu.HBM)] * 6,
        out_specs=(anywhere,) * 4,
        scratch_shapes=[
            pltpu.VMEM((2, spots, seq_len, half), low),
            pltpu.VMEM((2, spots, 2 * depth, half), low),
            pltpu.VMEM((3, spots, depth, half), low),
            pltpu.VMEM((3, spots + 1, depth, half), low),
            pltpu.VMEM((spots, depth, half), low),
            pltpu.VMEM((spots, depth, half), low),
            pltpu.VMEM((seq_len, 2 * depth), full),
            pltpu.VMEM((seq_len, depth), low),
            pltpu.VMEM((seq_len, HEAD_SIZE), low),
            pltpu.VMEM((seq_len, HEAD_SIZE), low),
            pltpu.VMEM((seq_len, depth), low),
            pltpu.VMEM((2, depth, half), full),
            pltpu.VMEM((heads, seq_len, window), full),
            pltpu.VMEM((heads, seq_len // back_rows, window, back_rows), low),
            pltpu.VMEM((seq_len, depth), low),
            pltpu.VMEM((depth, seq_len), low),
            pltpu.VMEM((2, depth, seq_len), low),
            pltpu.VMEM((seq_len // 2, 2 * depth), low),
            pltpu.VMEM((seq_len // 2, 2 * depth), low),
            pltpu.VMEM((seq_len // 2, depth), low),
            pltpu.VMEM((2, seq_len // 2, depth), low),
            pltpu.VMEM((depth, half), low),
            pltpu.VMEM((depth, half), low),
            pltpu.VMEM((2, seq_len, HEAD_SIZE), full),
            pltpu.VMEM((2, seq_len // 2, HEAD_SIZE), full),
            pltpu.VMEM((2, seq_len // 2, HEAD_SIZE), low),
            pltpu.SMEM(doc_lengths.shape, jnp.int32),
            dma((3,)),
            dma,
            dma,
            dma((fars,)),
            dma((fars, spots + pieces)),
            dma((fars,)),
            dma((fars, spots + pieces)),
            dma((2,)),
            dma((3, spots)),
            dma((3, spots + 1)),
            dma,
            dma((spots + 1,)),
            dma,
            dma((spots,)),
            dma((3,)),
            dma((3,)),
            dma,
            dma((parts,)),
            dma,
            dma((parts,)),
            dma,
            dma,
            dma,
            dma,
            dma((4,)),
            dma,
            dma,
            dma((2,)),
        ],
        compiler_params=pltpu.CompilerParams(
            collective_id=0, has_side_effects=True, vmem_limit_bytes=56 * 1024 * 1024
        ),
        name="exchange",
    )(grad_out[0], out_weight, query_act[0], rotated_keys[0], value_input[0], doc_lengths)
    query_grad, key_grad, value_grad, weight_grad = finish(
        query_grad, key_grad, value_grad, weight_grad
    )
    return (query_grad[None], key_grad[None, None], value_grad[None, None], weight_grad)


def solution(mesh):
    placed = (
        P("dp", None, "tensor"),
        P("dp", None, None),
        P("dp", None, None),
        P("dp", "tensor", None),
        P("tensor", "dp"),
        P("dp", None),
    )
    return jax.shard_map(
        shards,
        mesh=mesh,
        in_specs=placed,
        out_specs=(
            P("dp", None, "tensor"),
            P("dp", "tensor", None, None),
            P("dp", "tensor", None, None),
            P("tensor", "dp"),
        ),
        check_vma=False,
    )
```

```python
import functools

import jax
import jax.numpy as jnp
from jax import lax
from jax.experimental import pallas as pl
from jax.experimental.pallas import tpu as pltpu
from jax.sharding import PartitionSpec as P

HEAD_SIZE = 128


MESH = pl.DeviceIdType.MESH


def block_sizes(seq_len, tensor_count):
    rows = seq_len // tensor_count
    forward_rows = min(256, seq_len)
    part_rows = rows // max(1, rows // 128)
    block_rows = max(part_rows, min(128, 2 * rows))
    return forward_rows, part_rows, block_rows, seq_len // 2 + forward_rows


def exchange_kernel(
    dp_count,
    tensor_count,
    grad_ref,
    weight_ref,
    query_full,
    key_full,
    value_full,
    lengths_full,
    query_grad_out,
    key_grad_out,
    value_grad_out,
    weight_grad_out,
    grads,
    weights,
    sums_out,
    sums_in,
    cross_out,
    cross_in,
    accum,
    query_ref,
    key_ref,
    value_ref,
    query_grad_ref,
    weight_grad_ref,
    probs,
    probs_t,
    outs,
    outs_own,
    outs_t,
    share_out,
    share_in,
    turn_out,
    out_grad,
    back_out,
    back_in,
    kv_grads,
    kv_in,
    kv_done,
    lengths_ref,
    own_sem,
    near_send,
    near_recv,
    far_send,
    far_recv,
    pass_send,
    pass_recv,
    line_send,
    line_recv,
    total_recv,
    wing_send,
    wing_recv,
    cross_send,
    cross_recv,
    outs_send,
    outs_recv,
    share_send,
    share_recv,
    turn_send,
    turn_recv,
    back_send,
    back_recv,
    kv_send,
    kv_recv,
    load_sem,
    query_sem,
    put_sem,
    kv_sem,
):
    dp_index = lax.axis_index("dp")
    tensor_index = lax.axis_index("tensor")
    chip_count = tensor_count // 2
    pairs = chip_count // 2
    spots = dp_count // 2
    chip, core = tensor_index // 2, tensor_index % 2
    pair, parity = chip // 2, chip % 2
    mate = (pair * 2 + 1 - parity) * 2 + core
    partner = chip * 2 + 1 - core
    spot, lane = dp_index // 2, dp_index % 2
    twin = spot * 2 + 1 - lane
    rows = grad_ref.shape[0]
    depth, width = weight_ref.shape
    half = width // 2
    seq_len = query_full.shape[0]
    heads = depth // HEAD_SIZE
    half_rows = seq_len // 2
    score_scale = HEAD_SIZE ** (-0.5)
    forward_rows, part_rows, back_rows, window = block_sizes(seq_len, tensor_count)
    kv_columns = pl.ds(pl.multiple_of(tensor_index // 2 * HEAD_SIZE, HEAD_SIZE), HEAD_SIZE)
    slots = (slice(0, depth), slice(depth, 2 * depth))
    sides = (slice(0, half), slice(half, width))
    chunks = ((0, 0), (0, 1), (1, 0))
    ways = (1, -1)
    routes = [(away, whose) for whose in (1, 0) for away in range(pairs) if away or whose]
    fars = len(routes)
    pieces = rows // part_rows

    def exists(way):
        return spot <= spots - 2 if way > 0 else spot >= 1

    def reaches(way, far):
        return spot + far <= spots - 1 if way > 0 else spot >= far

    def local_rows(whose, which_pair, which_core):
        start = ((whose * pairs + which_pair) * 2 + which_core) * rows
        return pl.ds(pl.multiple_of(start, rows), rows)

    def columns(which_lane, block, side):
        start = (2 * block + which_lane) * width + side * half
        return pl.ds(pl.multiple_of(start, half), half)

    def remote(source, target, send, recv, dp_to, tensor_to):
        return pltpu.make_async_remote_copy(
            source, target, send, recv, device_id=(dp_to, tensor_to), device_id_type=MESH
        )

    def drain(ref, sem):
        pltpu.make_async_copy(ref, ref, sem).wait()

    def own_copy(side, block):
        return pltpu.make_async_copy(
            grad_ref.at[:, columns(lane, block, side)],
            grads.at[side, block, local_rows(0, pair, core)],
            own_sem.at[0],
        )

    def own_weight(side):
        return pltpu.make_async_copy(
            weight_ref.at[:, sides[side]], weights.at[side, spot, slots[0]], own_sem.at[1]
        )

    def near_copy(side, block):
        return remote(
            grad_ref.at[:, columns(lane, block, side)],
            grads.at[side, block, local_rows(0, pair, core)],
            near_send,
            near_recv,
            dp_index,
            partner,
        )

    def far_copy(route, side, block):
        away, whose = routes[route]
        return remote(
            grad_ref.at[:, columns(1 - lane if whose else lane, block, side)],
            grads.at[side, block, local_rows(whose, pair, core)],
            far_send.at[route],
            far_recv.at[route, block],
            twin if whose else dp_index,
            ((pair + away) % pairs * 2 + parity) * 2 + core,
        )

    def source_rows(route, which_core):
        away, whose = routes[route]
        return local_rows(whose, (pair + pairs - away) % pairs, which_core)

    def pass_copy(route, side, block):
        piece = grads.at[side, block, source_rows(route, core)]
        return remote(
            piece, piece, pass_send.at[route], pass_recv.at[route, block], dp_index, partner
        )

    def piece_rows(rows_slice, piece):
        return pl.ds(
            pl.multiple_of(rows_slice.start + piece * part_rows, part_rows), part_rows
        )

    def last_copy(route, piece):
        away, whose = routes[route]
        return remote(
            grad_ref.at[
                slice(piece * part_rows, (piece + 1) * part_rows),
                columns(1 - lane if whose else lane, spot, 0),
            ],
            grads.at[0, spot, piece_rows(local_rows(whose, pair, core), piece)],
            far_send.at[route],
            far_recv.at[route, spots + piece],
            twin if whose else dp_index,
            ((pair + away) % pairs * 2 + parity) * 2 + core,
        )

    def last_pass_copy(route, piece):
        here = grads.at[0, spot, piece_rows(source_rows(route, core), piece)]
        return remote(
            here,
            here,
            pass_send.at[route],
            pass_recv.at[route, spots + piece],
            dp_index,
            partner,
        )

    def line_copy(way, far, chunk):
        side, slot = chunks[chunk]
        block = spot - way * far
        if far == 0 and slot == 0:
            source = weight_ref.at[:, sides[side]]
        else:
            source = weights.at[side, block, slots[slot]]
        return remote(
            source,
            weights.at[side, block, slots[slot]],
            line_send.at[(1 - way) // 2],
            line_recv.at[chunk, block],
            dp_index + 2 * way,
            tensor_index,
        )

    def wing_copy(block, side=1, own=False):
        return remote(
            weight_ref.at[:, sides[side]] if own else weights.at[side, block, slots[0]],
            weights.at[side, block, slots[1]],
            wing_send,
            wing_recv.at[block if side else spots],
            dp_index,
            mate,
        )

    def total_copy(way, far, chunk):
        owner = spot + way * far
        index = spots if way < 0 and far == 1 else owner
        return remote(
            sums_out.at[chunk, owner],
            sums_in.at[chunk, index],
            line_send.at[(1 - way) // 2],
            total_recv.at[chunk, index],
            dp_index + 2 * way,
            tensor_index,
        )

    def cross_copy(block):
        return remote(
            cross_out.at[block],
            cross_in.at[block],
            cross_send,
            cross_recv.at[block],
            dp_index,
            mate,
        )

    def chip_lanes(which_pair, which_parity):
        start = (2 * which_pair + which_parity) * 2 * rows
        return pl.ds(pl.multiple_of(start, 2 * rows), 2 * rows)

    def outs_copy(kind, which_pair):
        here = slice(which_pair * 2 * rows, (which_pair + 1) * 2 * rows)
        there = slice(half_rows + which_pair * 2 * rows, half_rows + (which_pair + 1) * 2 * rows)
        own = outs_own.at[:, chip_lanes(which_pair, parity)]
        if kind == 0:
            return pltpu.make_async_copy(own, outs_t.at[0, :, here], own_sem.at[2])
        if kind == 1:
            other = outs_own.at[:, chip_lanes(which_pair, 1 - parity)]
            return remote(
                other, outs_t.at[1, :, here], outs_send.at[0], outs_recv.at[0], dp_index, mate
            )
        if kind == 2:
            return remote(
                own, outs_t.at[0, :, there], outs_send.at[1], outs_recv.at[1], twin, tensor_index
            )
        return remote(
            outs_t.at[1, :, here],
            outs_t.at[1, :, there],
            outs_send.at[2],
            outs_recv.at[2],
            twin,
            tensor_index,
        )

    parts = [
        (which_pair, which_core, piece)
        for piece in range(rows // part_rows)
        for which_pair in range(pairs)
        for which_core in (0, 1)
    ]

    def part_start(part):
        which_pair, which_core, piece = parts[part]
        return (which_pair * 2 + which_core) * rows + piece * part_rows

    def part_slice(part):
        return slice(part_start(part), part_start(part) + part_rows)

    def share_copy(part, slot):
        here = part_slice(part)
        return remote(
            share_out.at[here, slots[slot]],
            share_in.at[here, slots[slot]],
            share_send,
            share_recv.at[part, slot],
            twin,
            tensor_index,
        )

    def turn_copy(part):
        here = part_slice(part)
        return remote(
            turn_out.at[here], out_grad.at[1, here], turn_send, turn_recv.at[part], dp_index, mate
        )

    def back_copy(part):
        here = slice(part * (depth // len(parts)), (part + 1) * (depth // len(parts)))
        return remote(back_out.at[here], back_in.at[here], back_send, back_recv, dp_index, mate)

    kv_copy = remote(
        kv_grads.at[:, pl.ds(pl.multiple_of((1 - core) * half_rows, half_rows), half_rows)],
        kv_in,
        kv_send,
        kv_recv,
        dp_index,
        partner,
    )

    targets = [(dp_index, partner), (dp_index, mate), (twin, tensor_index)]
    for away in range(1, pairs):
        other = ((pair + away) % pairs * 2 + parity) * 2 + core
        targets += [(dp_index, other), (twin, other)]
    barrier = pltpu.get_barrier_semaphore()
    for target in targets:
        pl.semaphore_signal(barrier, inc=1, device_id=target, device_id_type=MESH)
    for way in ways:

        @pl.when(exists(way))
        def _():
            pl.semaphore_signal(
                barrier,
                inc=1,
                device_id=(dp_index + 2 * way, tensor_index),
                device_id_type=MESH,
            )

    loads = [
        pltpu.make_async_copy(query_full, query_ref, load_sem.at[0]),
        pltpu.make_async_copy(key_full.at[:, kv_columns], key_ref, load_sem.at[1]),
        pltpu.make_async_copy(value_full.at[:, kv_columns], value_ref, load_sem.at[2]),
        pltpu.make_async_copy(lengths_full, lengths_ref, load_sem.at[3]),
    ]
    for load in loads:
        load.start()
    beside = (spot + spots - 2) // (spots - 1) + (2 * spots - 3 - spot) // (spots - 1)
    pl.semaphore_wait(barrier, len(targets) + beside)

    upper = (2 * spot) // spots
    first_block = (1 - upper) * (spots - 1)

    def far_start(block):
        for side in (0, 1):
            for route in range(fars):
                far_copy(route, side, block).start()

    def line_start(chunk):
        for way in ways:

            @pl.when(exists(way))
            def _():
                line_copy(way, 0, chunk).start()

    line_start(2)
    wing_copy(spot, 0, True).start()
    far_start(first_block)
    line_start(0)
    nt = (((1,), (1,)), ((), ()))
    tn = (((0,), (0,)), ((), ()))

    def dot(left, right, dims):
        return lax.dot_general(left, right, dims, preferred_element_type=jnp.float32)

    def window_start(index):
        skip, total = half_rows // forward_rows, seq_len // forward_rows
        past = (index + total - skip) // total
        return past * (index - skip) * forward_rows

    def window_keys(index):
        return pl.ds(pl.multiple_of(window_start(index), forward_rows), window)

    def forward(index):
        here = pl.ds(pl.multiple_of(index * forward_rows, forward_rows), forward_rows)
        query_places = index * forward_rows + lax.broadcasted_iota(jnp.int32, (forward_rows, 1), 0)
        key_places = window_start(index) + lax.broadcasted_iota(
            jnp.int32, (forward_rows, window), 1
        )
        doc_start = jnp.zeros((forward_rows, 1), jnp.int32)
        doc_end = jnp.int32(0)
        for doc in range(lengths_ref.shape[1]):
            doc_end = doc_end + lengths_ref[0, doc]
            doc_start = jnp.where(query_places >= doc_end, doc_end, doc_start)
        allowed = (key_places >= doc_start) & (key_places <= query_places)
        keys, values = key_ref[window_keys(index)], value_ref[window_keys(index)]
        for head in range(heads):
            lanes = slice(head * HEAD_SIZE, (head + 1) * HEAD_SIZE)
            scores = dot(query_ref[here, lanes], keys, nt) * score_scale
            scores = jnp.where(allowed, scores, -jnp.inf)
            row_max = jnp.max(scores, axis=1, keepdims=True)
            total = jnp.sum(jnp.exp(scores - row_max), axis=1, keepdims=True)
            prob = jnp.exp(scores - (row_max + jnp.log(total)))
            probs[head, here] = prob
            out = jnp.dot(prob.astype(jnp.bfloat16), values, preferred_element_type=jnp.float32)
            outs[here, lanes] = out.astype(jnp.bfloat16)
            outs_own[lanes, here] = out.T.astype(jnp.bfloat16)
            for part in range(forward_rows // back_rows):
                piece = prob[part * back_rows : (part + 1) * back_rows]
                block = index * (forward_rows // back_rows) + part
                probs_t[head, block] = piece.T.astype(jnp.bfloat16)

    def backward(which, start):
        whose = parity if which == 0 else 1 - parity
        place = start // (2 * rows) * 4 * rows + start % (2 * rows)
        block = place // back_rows + whose * (2 * rows // back_rows)
        here = pl.ds(pl.multiple_of(block * back_rows, back_rows), back_rows)
        seen = window_keys(block // (forward_rows // back_rows))
        keys, values = key_ref[seen], value_ref[seen]
        key_total, value_total = kv_grads[0, seen], kv_grads[1, seen]
        for head in range(heads):
            lanes = slice(head * HEAD_SIZE, (head + 1) * HEAD_SIZE)
            grad = out_grad[which, start : start + back_rows, lanes]
            delta = jnp.sum(
                grad.astype(jnp.float32) * outs[here, lanes].astype(jnp.float32), axis=1, keepdims=True
            )
            dscore = probs[head, here] * (dot(grad, values, nt) - delta) * score_scale
            dscore = dscore.astype(jnp.bfloat16)
            query_grad_ref[here, lanes] = jnp.dot(
                dscore, keys, preferred_element_type=jnp.float32
            ).astype(jnp.bfloat16)
            key_total += dot(dscore, query_ref[here, lanes], tn)
            value_total += jnp.dot(probs_t[head, block], grad, preferred_element_type=jnp.float32)
        kv_grads[0, seen] = key_total
        kv_grads[1, seen] = value_total
        pltpu.make_async_copy(
            query_grad_ref.at[here], query_grad_out.at[here], query_sem
        ).start()

    def project(block, whose, which=(0, 1), piece=None):
        if piece is None:
            areas = [slice(whose * half_rows, (whose + 1) * half_rows)]
        else:
            areas = [
                slice(half_rows + part_start(part), half_rows + part_start(part) + part_rows)
                for part in range(len(parts))
                if parts[part][2] == piece
            ]
        for here in areas:
            total = accum[here]
            for side in which:
                total += dot(grads[side, block, here], weights[side, block], nt)
            accum[here] = total

    def line_hop(far, chunk):
        side, slot = chunks[chunk]
        for way in ways:

            @pl.when(reaches(-way, far))
            def _():
                block = spot - way * far
                drain(weights.at[side, block, slots[slot]], line_recv.at[chunk, block])

                @pl.when(exists(way))
                def _():
                    line_copy(way, far, chunk).start()

                if chunk == 2:
                    wing_copy(block).start()

    def wing_wait(block, side=1):
        drain(weights.at[side, block, slots[1]], wing_recv.at[block if side else spots])

    def hop_project(far):
        for way in ways:

            @pl.when(reaches(-way, far))
            def _():
                wing_wait(spot - way * far)
                project(spot - way * far, 0)

    def far_pass(block, which=(0, 1)):
        for route in range(fars):
            for side in which[:1] if len(which) == 1 else ():
                drain(grads.at[side, block, source_rows(route, core)], far_recv.at[route, block])
            if len(which) == 2:
                drain(grads.at[:, block, source_rows(route, core)], far_recv.at[route, block])
            for side in which:
                pass_copy(route, side, block).start()

    def pass_wait(block, which=(0, 1)):
        for route in range(fars):
            there = source_rows(route, 1 - core)
            if len(which) == 2:
                drain(grads.at[:, block, there], pass_recv.at[route, block])
            else:
                drain(grads.at[which[0], block, there], pass_recv.at[route, block])

    def last_pass(piece):
        for route in range(fars):
            here = piece_rows(source_rows(route, core), piece)
            drain(grads.at[0, spot, here], far_recv.at[route, spots + piece])
            last_pass_copy(route, piece).start()

    def last_wait(piece):
        for route in range(fars):
            here = piece_rows(source_rows(route, 1 - core), piece)
            drain(grads.at[0, spot, here], pass_recv.at[route, spots + piece])

    def sum_part(slot, side, block):
        return jnp.dot(outs_t[slot], grads[side, block], preferred_element_type=jnp.float32)

    def cross(block):
        cross_out[block] = sum_part(1, 1, block).astype(jnp.bfloat16)
        cross_copy(block).start()

    def owner_do(far, work):
        for way in ways:

            @pl.when(reaches(way, far))
            def _():
                work(way, spot + way * far)

    def total_sum(chunk, owner):
        side, slot = chunks[chunk]
        part = sum_part(slot, side, owner) + sums_in[chunk, owner].astype(jnp.float32)
        if side:
            drain(cross_in.at[owner], cross_recv.at[owner])
            part = part + cross_in[owner].astype(jnp.float32)
        sums_out[chunk, owner] = part.astype(jnp.bfloat16)

    def total_step(far, chunk):
        def work(way, owner):
            @pl.when(owner != first_block)
            def _():
                @pl.when(exists(-way))
                def _():
                    drain(sums_in.at[chunk, owner], total_recv.at[chunk, owner])

                total_sum(chunk, owner)
                total_copy(way, far, chunk).start()

        owner_do(far, work)

    def total_first(chunk, at_end):
        edge = spot % (spots - 1)

        @pl.when(edge == 0 if at_end else edge != 0)
        def _():
            if not at_end:
                drain(sums_in.at[chunk, first_block], total_recv.at[chunk, first_block])
            total_sum(chunk, first_block)
            remote(
                sums_out.at[chunk, first_block],
                sums_in.at[chunk, first_block],
                line_send.at[upper],
                total_recv.at[chunk, first_block],
                dp_index + 2 - 4 * upper,
                tensor_index,
            ).start()

    def total_final(chunk):
        side, slot = chunks[chunk]
        part = sum_part(slot, side, spot)
        if side:
            drain(cross_in.at[spot], cross_recv.at[spot])
            part = part + cross_in[spot].astype(jnp.float32)
        for way, index in ((-1, spot), (1, spots)):

            @pl.when(exists(way))
            def _():
                drain(sums_in.at[chunk, index], total_recv.at[chunk, index])

            part = part + sums_in[chunk, index].astype(jnp.float32)
        return part

    def weight_put(side):
        return pltpu.make_async_copy(
            weight_grad_ref.at[side], weight_grad_out.at[:, sides[side]], put_sem
        )

    def share(piece):
        for slot in (1, 0):
            for part in range(len(parts)):
                if parts[part][2] == piece:
                    here = part_slice(part)
                    there = slice(half_rows + here.start, half_rows + here.stop)
                    share_out[here, slots[slot]] = accum[there, slots[slot]].astype(jnp.bfloat16)
                    share_copy(part, slot).start()

    def settle(part, slot):
        here = part_slice(part)
        share_copy(part, slot).wait_recv()
        both = accum[here, slots[slot]] + share_in[here, slots[slot]].astype(jnp.float32)
        if slot:
            turn_out[here] = both.astype(jnp.bfloat16)
            turn_copy(part).start()
        else:
            out_grad[0, here] = both.astype(jnp.bfloat16)

    def finished(part):
        start = part_start(part)
        if back_rows == part_rows:
            return start
        return start - rows if parts[part][1] == 1 else None

    for load in loads:
        load.wait()
    blocks = seq_len // forward_rows
    forward(0)

    @pl.loop(0, spots)
    def _(block):
        for side in (0, 1):
            near_copy(side, block).start()
            own_copy(side, block).start()

    for side in (0, 1):
        own_weight(side).start()
    for index in range(1, blocks):
        forward(index)
    for which_pair in range(pairs):
        outs_copy(1, which_pair).start()
        outs_copy(2, which_pair).start()
        outs_copy(0, which_pair).start()
    wing_copy(spot, 1, True).start()
    line_hop(1, 2)
    wing_wait(spot, 0)
    line_start(1)
    line_hop(1, 0)

    accum[...] = jnp.zeros_like(accum)
    kv_grads[...] = jnp.zeros_like(kv_grads)
    for way in ways:

        @pl.when(reaches(way, spots - 1))
        def _():
            for chunk in range(3):
                for index in range(spots + 1):
                    if index != (spots if way > 0 else spots - 1):
                        sums_in[chunk, index] = jnp.zeros_like(sums_in[chunk, index])

    drain(grads.at[:, :, local_rows(0, pair, core)], own_sem.at[0])
    drain(weights.at[:, spot, slots[0]], own_sem.at[1])
    drain(outs_t.at[0, :, slice(0, half_rows)], own_sem.at[2])
    drain(grads.at[:, :, local_rows(0, pair, 1 - core)], near_recv)
    drain(outs_t.at[1, :, slice(0, half_rows)], outs_recv.at[0])
    for which_pair in range(pairs):
        outs_copy(3, which_pair).start()

    def rest_start(far):
        def work(way, owner):
            if far > 1 or spots == 2:

                @pl.when(owner != first_block)
                def _():
                    far_start(owner)

            else:
                far_start(owner)

        owner_do(far, work)

    for far in range(spots - 1, 0, -1):
        rest_start(far)
    for route in range(fars):
        far_copy(route, 1, spot).start()
    for piece in range(pieces):
        for route in range(fars):
            last_copy(route, piece).start()
    def stage(far, way, where):
        owner = spot + way * far

        @pl.when(reaches(way, far))
        def _():
            @pl.when(owner != first_block)
            def _():
                @pl.when(where)
                def _():
                    far_pass(owner)
                    pass_wait(owner)
                    cross(owner)

    inside = spot % (spots - 1) != 0
    early = spots == 4

    def both_project(far):
        owner_do(far, lambda way, owner: project(owner, 1))

    far_pass(first_block)
    drain(outs_t.at[0, :, slice(half_rows, seq_len)], outs_recv.at[1])
    pass_wait(first_block)
    total_first(0, True)
    line_hop(1, 1)
    drain(outs_t.at[1, :, slice(half_rows, seq_len)], outs_recv.at[2])
    cross(first_block)
    total_first(1, True)
    line_hop(2, 2)
    line_hop(2, 0)
    total_first(0, False)
    wing_wait(spot)
    project(spot, 0)
    total_first(2, True)
    total_first(1, False)
    line_hop(2, 1)
    hop_project(1)
    for far in range(spots - 2, 0, -1):
        hop = spots - far + 1
        for way in ways:
            if early and far == 1 and way > 0:
                stage(far, way, spot % (spots - 1) == 0)
            else:
                stage(far, way, spot >= 0)
        total_step(far, 1)
        total_step(far, 0)
        if far == spots - 2:
            total_first(2, False)
            if early:
                stage(1, 1, inside)
            hop_project(2)
        if far <= spots // 2:
            both_project(far)
        if far == 1:
            far_pass(spot, (1,))
            line_hop(spots - 1, 1)
            hop_project(spots - 1)
            both_project(spots - 1)
            pass_wait(spot, (1,))
            cross(spot)
            project(spot, 1, (1,))
            last_pass(0)
        if hop < spots:
            line_hop(hop, 2)
            line_hop(hop, 0)
        if far > 1:
            total_step(far, 2)
        if hop < spots - 1:
            line_hop(hop, 1)
            hop_project(hop)
            if hop > spots // 2:
                both_project(hop)
    for piece in range(pieces):
        last_wait(piece)
        project(spot, 1, (0,), piece)
        share(piece)
        if piece + 1 < pieces:
            last_pass(piece + 1)

    def turned(part):
        turn_copy(part).wait_recv()
        if finished(part) is not None:
            backward(1, finished(part))

    def settled(part):
        settle(part, 0)
        if finished(part) is not None:
            backward(0, finished(part))

    def back_start(piece):
        for part in range(len(parts)):
            if parts[part][2] == piece:
                back_copy(part).start()

    groups = [
        [part for part in range(len(parts)) if parts[part][2] == piece] for piece in range(pieces)
    ]
    for piece, group in enumerate(groups):
        before = groups[piece - 1] if piece else []
        for number, part in enumerate(group):
            settle(part, 1)
            if piece == 0 and number == 0:
                total_step(1, 2)
            if number < len(before):
                turned(before[number])
        for part in before[len(group) :]:
            turned(part)
        if piece == 0:
            back_out[...] = total_final(1).astype(jnp.bfloat16)
        back_start(piece)
        for part in group:
            settled(part)
    for part in groups[-1]:
        turned(part)
    kv_copy.start()
    weight_grad_ref[1] = total_final(2)
    weight_put(1).start()
    part = total_final(0)
    drain(back_in, back_recv)
    weight_grad_ref[0] = part + back_in[...].astype(jnp.float32)
    weight_put(0).start()
    drain(grads.at[:, :, local_rows(0, pair, core)], near_send)
    for route in range(fars):
        drain(grads.at[:, :, local_rows(0, pair, core)], far_send.at[route])
        drain(grads.at[:, :, local_rows(0, pair, core)], pass_send.at[route])
    for index in range(3):
        drain(outs_t.at[0, :, slice(0, half_rows)], outs_send.at[index])
    drain(share_out, share_send)
    drain(turn_out, turn_send)
    drain(query_grad_ref, query_sem)
    drain(sums_in.at[0], wing_send)
    drain(cross_out, cross_send)
    drain(back_out, back_send)
    for way in ways:

        @pl.when(exists(way))
        def _():
            drain(grads.at[0, :, slice(0, 3 * depth)], line_send.at[(1 - way) // 2])

    mine = pl.ds(pl.multiple_of(core * half_rows, half_rows), half_rows)
    kv_copy.wait()
    kv_done[...] = (kv_grads[:, mine] + kv_in[...]).astype(jnp.bfloat16)
    kv_puts = [
        pltpu.make_async_copy(kv_done.at[which], to, kv_sem.at[which])
        for which, to in enumerate((key_grad_out, value_grad_out))
    ]
    for put in kv_puts:
        put.start()
    drain(weight_grad_ref, put_sem)
    for put in kv_puts:
        put.wait()


def finish_kernel(*refs):
    count = (len(refs) - 1) // 2
    puts = [
        pltpu.make_async_copy(refs[i], refs[count + i], refs[2 * count].at[i]) for i in range(count)
    ]
    for put in puts:
        put.start()
    for put in puts:
        put.wait()


def finish(*values):
    anywhere = pl.BlockSpec(memory_space=pl.ANY)
    return pl.pallas_call(
        finish_kernel,
        out_shape=tuple(pltpu.HBM(value.shape, value.dtype) for value in values),
        in_specs=[anywhere] * len(values),
        out_specs=(anywhere,) * len(values),
        scratch_shapes=[pltpu.SemaphoreType.DMA((len(values),))],
        compiler_params=pltpu.CompilerParams(vmem_limit_bytes=8 * 1024 * 1024),
        name="finish",
    )(*values)


def shards(query_act, rotated_keys, value_input, grad_out, out_weight, doc_lengths):
    dp_count, tensor_count = lax.axis_size("dp"), lax.axis_size("tensor")
    spots = dp_count // 2
    fars = tensor_count // 2 - 1
    seq_len = query_act.shape[1]
    depth, width = out_weight.shape
    half = width // 2
    heads = depth // HEAD_SIZE
    forward_rows, part_rows, back_rows, window = block_sizes(seq_len, tensor_count)
    parts = seq_len // 2 // part_rows
    pieces = seq_len // tensor_count // part_rows
    dma = pltpu.SemaphoreType.DMA
    anywhere = pl.BlockSpec(memory_space=pl.ANY)
    low, full = jnp.bfloat16, jnp.float32
    kv_shape = pltpu.VMEM((seq_len // 2, HEAD_SIZE), low)
    query_grad, key_grad, value_grad, weight_grad = pl.pallas_call(
        functools.partial(exchange_kernel, dp_count, tensor_count),
        out_shape=(
            pltpu.VMEM((seq_len, depth), low),
            kv_shape,
            kv_shape,
            pltpu.VMEM((depth, width), full),
        ),
        in_specs=[pl.BlockSpec(memory_space=pltpu.HBM)] * 6,
        out_specs=(anywhere,) * 4,
        scratch_shapes=[
            pltpu.VMEM((2, spots, seq_len, half), low),
            pltpu.VMEM((2, spots, 2 * depth, half), low),
            pltpu.VMEM((3, spots, depth, half), low),
            pltpu.VMEM((3, spots + 1, depth, half), low),
            pltpu.VMEM((spots, depth, half), low),
            pltpu.VMEM((spots, depth, half), low),
            pltpu.VMEM((seq_len, 2 * depth), full),
            pltpu.VMEM((seq_len, depth), low),
            pltpu.VMEM((seq_len, HEAD_SIZE), low),
            pltpu.VMEM((seq_len, HEAD_SIZE), low),
            pltpu.VMEM((seq_len, depth), low),
            pltpu.VMEM((2, depth, half), full),
            pltpu.VMEM((heads, seq_len, window), full),
            pltpu.VMEM((heads, seq_len // back_rows, window, back_rows), low),
            pltpu.VMEM((seq_len, depth), low),
            pltpu.VMEM((depth, seq_len), low),
            pltpu.VMEM((2, depth, seq_len), low),
            pltpu.VMEM((seq_len // 2, 2 * depth), low),
            pltpu.VMEM((seq_len // 2, 2 * depth), low),
            pltpu.VMEM((seq_len // 2, depth), low),
            pltpu.VMEM((2, seq_len // 2, depth), low),
            pltpu.VMEM((depth, half), low),
            pltpu.VMEM((depth, half), low),
            pltpu.VMEM((2, seq_len, HEAD_SIZE), full),
            pltpu.VMEM((2, seq_len // 2, HEAD_SIZE), full),
            pltpu.VMEM((2, seq_len // 2, HEAD_SIZE), low),
            pltpu.SMEM(doc_lengths.shape, jnp.int32),
            dma((3,)),
            dma,
            dma,
            dma((fars,)),
            dma((fars, spots + pieces)),
            dma((fars,)),
            dma((fars, spots + pieces)),
            dma((2,)),
            dma((3, spots)),
            dma((3, spots + 1)),
            dma,
            dma((spots + 1,)),
            dma,
            dma((spots,)),
            dma((3,)),
            dma((3,)),
            dma,
            dma((parts, 2)),
            dma,
            dma((parts,)),
            dma,
            dma,
            dma,
            dma,
            dma((4,)),
            dma,
            dma,
            dma((2,)),
        ],
        compiler_params=pltpu.CompilerParams(
            collective_id=0, has_side_effects=True, vmem_limit_bytes=56 * 1024 * 1024
        ),
        name="exchange",
    )(grad_out[0], out_weight, query_act[0], rotated_keys[0], value_input[0], doc_lengths)
    query_grad, key_grad, value_grad, weight_grad = finish(
        query_grad, key_grad, value_grad, weight_grad
    )
    return (query_grad[None], key_grad[None, None], value_grad[None, None], weight_grad)


def solution(mesh):
    placed = (
        P("dp", None, "tensor"),
        P("dp", None, None),
        P("dp", None, None),
        P("dp", "tensor", None),
        P("tensor", "dp"),
        P("dp", None),
    )
    return jax.shard_map(
        shards,
        mesh=mesh,
        in_specs=placed,
        out_specs=(
            P("dp", None, "tensor"),
            P("dp", "tensor", None, None),
            P("dp", "tensor", None, None),
            P("tensor", "dp"),
        ),
        check_vma=False,
    )
```

```python
import functools

import jax
import jax.numpy as jnp
from jax import lax
from jax.experimental import pallas as pl
from jax.experimental.pallas import tpu as pltpu
from jax.sharding import PartitionSpec as P

HEAD_SIZE = 128


MESH = pl.DeviceIdType.MESH


def block_sizes(seq_len, tensor_count):
    rows = seq_len // tensor_count
    forward_rows = min(256, seq_len)
    part_rows = rows // max(1, rows // 128)
    block_rows = max(part_rows, min(128, 2 * rows))
    return forward_rows, part_rows, block_rows, seq_len // 2 + forward_rows, seq_len // 2 + block_rows


def exchange_kernel(
    dp_count,
    tensor_count,
    grad_ref,
    weight_ref,
    query_full,
    key_full,
    value_full,
    lengths_full,
    query_grad_out,
    key_grad_out,
    value_grad_out,
    weight_grad_out,
    grads,
    weights,
    sums_out,
    sums_in,
    cross_out,
    cross_in,
    accum,
    query_ref,
    key_ref,
    value_ref,
    query_grad_ref,
    weight_grad_ref,
    probs,
    probs_t,
    outs,
    outs_own,
    outs_t,
    share_out,
    share_in,
    turn_out,
    out_grad,
    back_out,
    back_in,
    kv_grads,
    kv_in,
    kv_done,
    lengths_ref,
    own_sem,
    near_send,
    near_recv,
    far_send,
    far_recv,
    pass_send,
    pass_recv,
    line_send,
    line_recv,
    total_recv,
    wing_send,
    wing_recv,
    cross_send,
    cross_recv,
    outs_send,
    outs_recv,
    share_send,
    share_recv,
    turn_send,
    turn_recv,
    back_send,
    back_recv,
    kv_send,
    kv_recv,
    load_sem,
    query_sem,
    put_sem,
    kv_sem,
):
    dp_index = lax.axis_index("dp")
    tensor_index = lax.axis_index("tensor")
    chip_count = tensor_count // 2
    pairs = chip_count // 2
    spots = dp_count // 2
    chip, core = tensor_index // 2, tensor_index % 2
    pair, parity = chip // 2, chip % 2
    mate = (pair * 2 + 1 - parity) * 2 + core
    partner = chip * 2 + 1 - core
    spot, lane = dp_index // 2, dp_index % 2
    twin = spot * 2 + 1 - lane
    rows = grad_ref.shape[0]
    depth, width = weight_ref.shape
    half = width // 2
    seq_len = query_full.shape[0]
    heads = depth // HEAD_SIZE
    half_rows = seq_len // 2
    score_scale = HEAD_SIZE ** (-0.5)
    forward_rows, part_rows, back_rows, window, narrow = block_sizes(seq_len, tensor_count)
    kv_columns = pl.ds(pl.multiple_of(tensor_index // 2 * HEAD_SIZE, HEAD_SIZE), HEAD_SIZE)
    slots = (slice(0, depth), slice(depth, 2 * depth))
    sides = (slice(0, half), slice(half, width))
    chunks = ((0, 0), (0, 1), (1, 0))
    ways = (1, -1)
    routes = [(away, whose) for whose in (1, 0) for away in range(pairs) if away or whose]
    fars = len(routes)
    pieces = rows // part_rows

    def exists(way):
        return spot <= spots - 2 if way > 0 else spot >= 1

    def reaches(way, far):
        return spot + far <= spots - 1 if way > 0 else spot >= far

    def local_rows(whose, which_pair, which_core):
        start = ((whose * pairs + which_pair) * 2 + which_core) * rows
        return pl.ds(pl.multiple_of(start, rows), rows)

    def columns(which_lane, block, side):
        start = (2 * block + which_lane) * width + side * half
        return pl.ds(pl.multiple_of(start, half), half)

    def remote(source, target, send, recv, dp_to, tensor_to):
        return pltpu.make_async_remote_copy(
            source, target, send, recv, device_id=(dp_to, tensor_to), device_id_type=MESH
        )

    def drain(ref, sem):
        pltpu.make_async_copy(ref, ref, sem).wait()

    def own_copy(side, block):
        return pltpu.make_async_copy(
            grad_ref.at[:, columns(lane, block, side)],
            grads.at[side, block, local_rows(0, pair, core)],
            own_sem.at[0],
        )

    def own_weight(side):
        return pltpu.make_async_copy(
            weight_ref.at[:, sides[side]], weights.at[side, spot, slots[0]], own_sem.at[1]
        )

    def near_copy(side, block):
        return remote(
            grad_ref.at[:, columns(lane, block, side)],
            grads.at[side, block, local_rows(0, pair, core)],
            near_send,
            near_recv,
            dp_index,
            partner,
        )

    def far_copy(route, side, block):
        away, whose = routes[route]
        return remote(
            grad_ref.at[:, columns(1 - lane if whose else lane, block, side)],
            grads.at[side, block, local_rows(whose, pair, core)],
            far_send.at[route],
            far_recv.at[route, block],
            twin if whose else dp_index,
            ((pair + away) % pairs * 2 + parity) * 2 + core,
        )

    def source_rows(route, which_core):
        away, whose = routes[route]
        return local_rows(whose, (pair + pairs - away) % pairs, which_core)

    def pass_copy(route, side, block):
        piece = grads.at[side, block, source_rows(route, core)]
        return remote(
            piece, piece, pass_send.at[route], pass_recv.at[route, block], dp_index, partner
        )

    def piece_rows(rows_slice, piece):
        return pl.ds(
            pl.multiple_of(rows_slice.start + piece * part_rows, part_rows), part_rows
        )

    def last_copy(route, piece):
        away, whose = routes[route]
        return remote(
            grad_ref.at[
                slice(piece * part_rows, (piece + 1) * part_rows),
                columns(1 - lane if whose else lane, spot, 0),
            ],
            grads.at[0, spot, piece_rows(local_rows(whose, pair, core), piece)],
            far_send.at[route],
            far_recv.at[route, spots + piece],
            twin if whose else dp_index,
            ((pair + away) % pairs * 2 + parity) * 2 + core,
        )

    def last_pass_copy(route, piece):
        here = grads.at[0, spot, piece_rows(source_rows(route, core), piece)]
        return remote(
            here,
            here,
            pass_send.at[route],
            pass_recv.at[route, spots + piece],
            dp_index,
            partner,
        )

    def line_copy(way, far, chunk):
        side, slot = chunks[chunk]
        block = spot - way * far
        if far == 0 and slot == 0:
            source = weight_ref.at[:, sides[side]]
        else:
            source = weights.at[side, block, slots[slot]]
        return remote(
            source,
            weights.at[side, block, slots[slot]],
            line_send.at[(1 - way) // 2],
            line_recv.at[chunk, block],
            dp_index + 2 * way,
            tensor_index,
        )

    def wing_copy(block, side=1, own=False):
        return remote(
            weight_ref.at[:, sides[side]] if own else weights.at[side, block, slots[0]],
            weights.at[side, block, slots[1]],
            wing_send,
            wing_recv.at[block if side else spots],
            dp_index,
            mate,
        )

    def total_copy(way, far, chunk):
        owner = spot + way * far
        index = spots if way < 0 and far == 1 else owner
        return remote(
            sums_out.at[chunk, owner],
            sums_in.at[chunk, index],
            line_send.at[(1 - way) // 2],
            total_recv.at[chunk, index],
            dp_index + 2 * way,
            tensor_index,
        )

    def cross_copy(block):
        return remote(
            cross_out.at[block],
            cross_in.at[block],
            cross_send,
            cross_recv.at[block],
            dp_index,
            mate,
        )

    def chip_lanes(which_pair, which_parity):
        start = (2 * which_pair + which_parity) * 2 * rows
        return pl.ds(pl.multiple_of(start, 2 * rows), 2 * rows)

    def outs_copy(kind, which_pair):
        here = slice(which_pair * 2 * rows, (which_pair + 1) * 2 * rows)
        there = slice(half_rows + which_pair * 2 * rows, half_rows + (which_pair + 1) * 2 * rows)
        own = outs_own.at[:, chip_lanes(which_pair, parity)]
        if kind == 0:
            return pltpu.make_async_copy(own, outs_t.at[0, :, here], own_sem.at[2])
        if kind == 1:
            other = outs_own.at[:, chip_lanes(which_pair, 1 - parity)]
            return remote(
                other, outs_t.at[1, :, here], outs_send.at[0], outs_recv.at[0], dp_index, mate
            )
        if kind == 2:
            return remote(
                own, outs_t.at[0, :, there], outs_send.at[1], outs_recv.at[1], twin, tensor_index
            )
        return remote(
            outs_t.at[1, :, here],
            outs_t.at[1, :, there],
            outs_send.at[2],
            outs_recv.at[2],
            twin,
            tensor_index,
        )

    parts = [
        (which_pair, which_core, piece)
        for piece in range(rows // part_rows)
        for which_pair in range(pairs)
        for which_core in (0, 1)
    ]

    def part_start(part):
        which_pair, which_core, piece = parts[part]
        return (which_pair * 2 + which_core) * rows + piece * part_rows

    def part_slice(part):
        return slice(part_start(part), part_start(part) + part_rows)

    def share_copy(part, slot):
        here = part_slice(part)
        return remote(
            share_out.at[here, slots[slot]],
            share_in.at[here, slots[slot]],
            share_send,
            share_recv.at[part, slot],
            twin,
            tensor_index,
        )

    def turn_copy(part):
        here = part_slice(part)
        return remote(
            turn_out.at[here], out_grad.at[1, here], turn_send, turn_recv.at[part], dp_index, mate
        )

    def back_copy(part):
        here = slice(part * (depth // len(parts)), (part + 1) * (depth // len(parts)))
        return remote(back_out.at[here], back_in.at[here], back_send, back_recv, dp_index, mate)

    kv_copy = remote(
        kv_grads.at[:, pl.ds(pl.multiple_of((1 - core) * half_rows, half_rows), half_rows)],
        kv_in,
        kv_send,
        kv_recv,
        dp_index,
        partner,
    )

    targets = [(dp_index, partner), (dp_index, mate), (twin, tensor_index)]
    for away in range(1, pairs):
        other = ((pair + away) % pairs * 2 + parity) * 2 + core
        targets += [(dp_index, other), (twin, other)]
    barrier = pltpu.get_barrier_semaphore()
    for target in targets:
        pl.semaphore_signal(barrier, inc=1, device_id=target, device_id_type=MESH)
    for way in ways:

        @pl.when(exists(way))
        def _():
            pl.semaphore_signal(
                barrier,
                inc=1,
                device_id=(dp_index + 2 * way, tensor_index),
                device_id_type=MESH,
            )

    loads = [
        pltpu.make_async_copy(query_full, query_ref, load_sem.at[0]),
        pltpu.make_async_copy(key_full.at[:, kv_columns], key_ref, load_sem.at[1]),
        pltpu.make_async_copy(value_full.at[:, kv_columns], value_ref, load_sem.at[2]),
        pltpu.make_async_copy(lengths_full, lengths_ref, load_sem.at[3]),
    ]
    for load in loads:
        load.start()
    beside = (spot + spots - 2) // (spots - 1) + (2 * spots - 3 - spot) // (spots - 1)
    pl.semaphore_wait(barrier, len(targets) + beside)

    upper = (2 * spot) // spots
    first_block = (1 - upper) * (spots - 1)

    def far_start(block):
        for side in (0, 1):
            for route in range(fars):
                far_copy(route, side, block).start()

    def line_start(chunk):
        for way in ways:

            @pl.when(exists(way))
            def _():
                line_copy(way, 0, chunk).start()

    line_start(2)
    wing_copy(spot, 0, True).start()
    far_start(first_block)
    line_start(0)
    nt = (((1,), (1,)), ((), ()))
    tn = (((0,), (0,)), ((), ()))

    def dot(left, right, dims):
        return lax.dot_general(left, right, dims, preferred_element_type=jnp.float32)

    def first_key(block, block_rows):
        skip, total = half_rows // block_rows, seq_len // block_rows
        past = (block + total - skip) // total
        return past * (block - skip) * block_rows

    def window_keys(index):
        return pl.ds(first_key(index, forward_rows), window)

    def forward(index):
        here = pl.ds(pl.multiple_of(index * forward_rows, forward_rows), forward_rows)
        query_places = index * forward_rows + lax.broadcasted_iota(jnp.int32, (forward_rows, 1), 0)
        key_places = first_key(index, forward_rows) + lax.broadcasted_iota(
            jnp.int32, (forward_rows, window), 1
        )
        doc_start = jnp.zeros((forward_rows, 1), jnp.int32)
        doc_end = jnp.int32(0)
        for doc in range(lengths_ref.shape[1]):
            doc_end = doc_end + lengths_ref[0, doc]
            doc_start = jnp.where(query_places >= doc_end, doc_end, doc_start)
        allowed = (key_places >= doc_start) & (key_places <= query_places)
        keys, values = key_ref[window_keys(index)], value_ref[window_keys(index)]
        for head in range(heads):
            lanes = slice(head * HEAD_SIZE, (head + 1) * HEAD_SIZE)
            scores = dot(query_ref[here, lanes], keys, nt) * score_scale
            scores = jnp.where(allowed, scores, -jnp.inf)
            row_max = jnp.max(scores, axis=1, keepdims=True)
            total = jnp.sum(jnp.exp(scores - row_max), axis=1, keepdims=True)
            prob = jnp.exp(scores - (row_max + jnp.log(total)))
            out = jnp.dot(prob.astype(jnp.bfloat16), values, preferred_element_type=jnp.float32)
            outs[here, lanes] = out.astype(jnp.bfloat16)
            outs_own[lanes, here] = out.T.astype(jnp.bfloat16)
            for part in range(forward_rows // back_rows):
                block = index * (forward_rows // back_rows) + part
                skip = first_key(block, back_rows) - first_key(index, forward_rows)
                piece = prob[part * back_rows : (part + 1) * back_rows, skip : skip + narrow]
                probs[head, block * back_rows : (block + 1) * back_rows] = piece
                probs_t[head, block] = piece.T.astype(jnp.bfloat16)

    def backward(which, start):
        whose = parity if which == 0 else 1 - parity
        place = start // (2 * rows) * 4 * rows + start % (2 * rows)
        block = place // back_rows + whose * (2 * rows // back_rows)
        here = pl.ds(pl.multiple_of(block * back_rows, back_rows), back_rows)
        seen = pl.ds(pl.multiple_of(first_key(block, back_rows), back_rows), narrow)
        keys, values = key_ref[seen], value_ref[seen]
        grads_low, products, deltas, dscores = [], [], [], []
        for head in range(heads):
            lanes = slice(head * HEAD_SIZE, (head + 1) * HEAD_SIZE)
            grad = out_grad[which, start : start + back_rows, lanes]
            grads_low.append(grad)
            products.append(dot(grad, values, nt))
            deltas.append(
                jnp.sum(
                    grad.astype(jnp.float32) * outs[here, lanes].astype(jnp.float32),
                    axis=1,
                    keepdims=True,
                )
            )
        value_total = kv_grads[1, seen]
        for head in range(heads):
            value_total += jnp.dot(
                probs_t[head, block], grads_low[head], preferred_element_type=jnp.float32
            )
        kv_grads[1, seen] = value_total
        for head in range(heads):
            dscore = probs[head, here] * (products[head] - deltas[head]) * score_scale
            dscores.append(dscore.astype(jnp.bfloat16))
        key_total = kv_grads[0, seen]
        for head in range(heads):
            lanes = slice(head * HEAD_SIZE, (head + 1) * HEAD_SIZE)
            key_total += dot(dscores[head], query_ref[here, lanes], tn)
            query_grad_ref[here, lanes] = jnp.dot(
                dscores[head], keys, preferred_element_type=jnp.float32
            ).astype(jnp.bfloat16)
        kv_grads[0, seen] = key_total
        pltpu.make_async_copy(
            query_grad_ref.at[here], query_grad_out.at[here], query_sem
        ).start()

    def project(block, whose, which=(0, 1), piece=None):
        if piece is None:
            areas = [slice(whose * half_rows, (whose + 1) * half_rows)]
        else:
            areas = [
                slice(half_rows + part_start(part), half_rows + part_start(part) + part_rows)
                for part in range(len(parts))
                if parts[part][2] == piece
            ]
        for here in areas:
            total = accum[here]
            for side in which:
                total += dot(grads[side, block, here], weights[side, block], nt)
            accum[here] = total

    def line_hop(far, chunk):
        side, slot = chunks[chunk]
        for way in ways:

            @pl.when(reaches(-way, far))
            def _():
                block = spot - way * far
                drain(weights.at[side, block, slots[slot]], line_recv.at[chunk, block])

                @pl.when(exists(way))
                def _():
                    line_copy(way, far, chunk).start()

                if chunk == 2:
                    wing_copy(block).start()

    def wing_wait(block, side=1):
        drain(weights.at[side, block, slots[1]], wing_recv.at[block if side else spots])

    def hop_project(far):
        for way in ways:

            @pl.when(reaches(-way, far))
            def _():
                wing_wait(spot - way * far)
                project(spot - way * far, 0)

    def far_pass(block, which=(0, 1)):
        for route in range(fars):
            for side in which[:1] if len(which) == 1 else ():
                drain(grads.at[side, block, source_rows(route, core)], far_recv.at[route, block])
            if len(which) == 2:
                drain(grads.at[:, block, source_rows(route, core)], far_recv.at[route, block])
            for side in which:
                pass_copy(route, side, block).start()

    def pass_wait(block, which=(0, 1)):
        for route in range(fars):
            there = source_rows(route, 1 - core)
            if len(which) == 2:
                drain(grads.at[:, block, there], pass_recv.at[route, block])
            else:
                drain(grads.at[which[0], block, there], pass_recv.at[route, block])

    def last_pass(piece):
        for route in range(fars):
            here = piece_rows(source_rows(route, core), piece)
            drain(grads.at[0, spot, here], far_recv.at[route, spots + piece])
            last_pass_copy(route, piece).start()

    def last_wait(piece):
        for route in range(fars):
            here = piece_rows(source_rows(route, 1 - core), piece)
            drain(grads.at[0, spot, here], pass_recv.at[route, spots + piece])

    def sum_part(slot, side, block):
        return jnp.dot(outs_t[slot], grads[side, block], preferred_element_type=jnp.float32)

    def cross(block):
        cross_out[block] = sum_part(1, 1, block).astype(jnp.bfloat16)
        cross_copy(block).start()

    def owner_do(far, work):
        for way in ways:

            @pl.when(reaches(way, far))
            def _():
                work(way, spot + way * far)

    def total_sum(chunk, owner):
        side, slot = chunks[chunk]
        part = sum_part(slot, side, owner) + sums_in[chunk, owner].astype(jnp.float32)
        if side:
            drain(cross_in.at[owner], cross_recv.at[owner])
            part = part + cross_in[owner].astype(jnp.float32)
        sums_out[chunk, owner] = part.astype(jnp.bfloat16)

    def total_step(far, chunk):
        def work(way, owner):
            @pl.when(owner != first_block)
            def _():
                @pl.when(exists(-way))
                def _():
                    drain(sums_in.at[chunk, owner], total_recv.at[chunk, owner])

                total_sum(chunk, owner)
                total_copy(way, far, chunk).start()

        owner_do(far, work)

    def total_first(chunk, at_end):
        edge = spot % (spots - 1)

        @pl.when(edge == 0 if at_end else edge != 0)
        def _():
            if not at_end:
                drain(sums_in.at[chunk, first_block], total_recv.at[chunk, first_block])
            total_sum(chunk, first_block)
            remote(
                sums_out.at[chunk, first_block],
                sums_in.at[chunk, first_block],
                line_send.at[upper],
                total_recv.at[chunk, first_block],
                dp_index + 2 - 4 * upper,
                tensor_index,
            ).start()

    def total_final(chunk, part):
        if chunks[chunk][0]:
            drain(cross_in.at[spot], cross_recv.at[spot])
            part = part + cross_in[spot].astype(jnp.float32)
        for way, index in ((-1, spot), (1, spots)):

            @pl.when(exists(way))
            def _():
                drain(sums_in.at[chunk, index], total_recv.at[chunk, index])

            part = part + sums_in[chunk, index].astype(jnp.float32)
        return part

    def weight_put(side):
        return pltpu.make_async_copy(
            weight_grad_ref.at[side], weight_grad_out.at[:, sides[side]], put_sem
        )

    def share(piece):
        for slot in (1, 0):
            for part in range(len(parts)):
                if parts[part][2] == piece:
                    here = part_slice(part)
                    there = slice(half_rows + here.start, half_rows + here.stop)
                    share_out[here, slots[slot]] = accum[there, slots[slot]].astype(jnp.bfloat16)
                    share_copy(part, slot).start()

    def settle(part, slot):
        here = part_slice(part)
        share_copy(part, slot).wait_recv()
        both = accum[here, slots[slot]] + share_in[here, slots[slot]].astype(jnp.float32)
        if slot:
            turn_out[here] = both.astype(jnp.bfloat16)
            turn_copy(part).start()
        else:
            out_grad[0, here] = both.astype(jnp.bfloat16)

    def finished(part):
        start = part_start(part)
        if back_rows == part_rows:
            return start
        return start - rows if parts[part][1] == 1 else None

    for load in loads:
        load.wait()
    blocks = seq_len // forward_rows
    forward(0)

    @pl.loop(0, spots)
    def _(block):
        for side in (0, 1):
            near_copy(side, block).start()
            own_copy(side, block).start()

    for side in (0, 1):
        own_weight(side).start()
    for index in range(1, blocks):
        forward(index)
    for which_pair in range(pairs):
        outs_copy(1, which_pair).start()
        outs_copy(2, which_pair).start()
        outs_copy(0, which_pair).start()
    wing_copy(spot, 1, True).start()
    line_hop(1, 2)
    wing_wait(spot, 0)
    line_start(1)
    line_hop(1, 0)

    accum[...] = jnp.zeros_like(accum)
    kv_grads[...] = jnp.zeros_like(kv_grads)
    for way in ways:

        @pl.when(reaches(way, spots - 1))
        def _():
            for chunk in range(3):
                for index in range(spots + 1):
                    if index != (spots if way > 0 else spots - 1):
                        sums_in[chunk, index] = jnp.zeros_like(sums_in[chunk, index])

    drain(grads.at[:, :, local_rows(0, pair, core)], own_sem.at[0])
    drain(weights.at[:, spot, slots[0]], own_sem.at[1])
    drain(outs_t.at[0, :, slice(0, half_rows)], own_sem.at[2])
    drain(grads.at[:, :, local_rows(0, pair, 1 - core)], near_recv)
    drain(outs_t.at[1, :, slice(0, half_rows)], outs_recv.at[0])
    for which_pair in range(pairs):
        outs_copy(3, which_pair).start()

    def rest_start(far):
        def work(way, owner):
            if far > 1 or spots == 2:

                @pl.when(owner != first_block)
                def _():
                    far_start(owner)

            else:
                far_start(owner)

        owner_do(far, work)

    for far in range(spots - 1, 0, -1):
        rest_start(far)
    for route in range(fars):
        far_copy(route, 1, spot).start()
    for piece in range(pieces):
        for route in range(fars):
            last_copy(route, piece).start()
    def stage(far, way, where):
        owner = spot + way * far

        @pl.when(reaches(way, far))
        def _():
            @pl.when(owner != first_block)
            def _():
                @pl.when(where)
                def _():
                    far_pass(owner)
                    pass_wait(owner)
                    cross(owner)

    inside = spot % (spots - 1) != 0
    early = spots == 4

    def both_project(far):
        owner_do(far, lambda way, owner: project(owner, 1))

    far_pass(first_block)
    drain(outs_t.at[0, :, slice(half_rows, seq_len)], outs_recv.at[1])
    pass_wait(first_block)
    total_first(0, True)
    line_hop(1, 1)
    drain(outs_t.at[1, :, slice(half_rows, seq_len)], outs_recv.at[2])
    cross(first_block)
    total_first(1, True)
    line_hop(2, 2)
    line_hop(2, 0)
    total_first(0, False)
    wing_wait(spot)
    project(spot, 0)
    total_first(2, True)
    total_first(1, False)
    line_hop(2, 1)
    hop_project(1)
    for far in range(spots - 2, 0, -1):
        hop = spots - far + 1
        for way in ways:
            if early and far == 1 and way > 0:
                stage(far, way, spot % (spots - 1) == 0)
            else:
                stage(far, way, spot >= 0)
        total_step(far, 1)
        total_step(far, 0)
        if far == spots - 2:
            total_first(2, False)
            if early:
                stage(1, 1, inside)
            hop_project(2)
        if far <= spots // 2:
            both_project(far)
        if far == 1:
            far_pass(spot, (1,))
            line_hop(spots - 1, 1)
            hop_project(spots - 1)
            both_project(spots - 1)
            pass_wait(spot, (1,))
            cross(spot)
            project(spot, 1, (1,))
            last_pass(0)
        if hop < spots:
            line_hop(hop, 2)
            line_hop(hop, 0)
        if far > 1:
            total_step(far, 2)
        if hop < spots - 1:
            line_hop(hop, 1)
            hop_project(hop)
            if hop > spots // 2:
                both_project(hop)
    for piece in range(pieces):
        last_wait(piece)
        project(spot, 1, (0,), piece)
        share(piece)
        if piece + 1 < pieces:
            last_pass(piece + 1)

    def turned(part):
        turn_copy(part).wait_recv()
        if finished(part) is not None:
            backward(1, finished(part))

    def settled(part):
        settle(part, 0)
        if finished(part) is not None:
            backward(0, finished(part))

    def back_start(piece):
        for part in range(len(parts)):
            if parts[part][2] == piece:
                back_copy(part).start()

    groups = [
        [part for part in range(len(parts)) if parts[part][2] == piece] for piece in range(pieces)
    ]
    for piece, group in enumerate(groups):
        before = groups[piece - 1] if piece else []
        for number, part in enumerate(group):
            settle(part, 1)
            if piece == 0 and number == 0:
                total_step(1, 2)
            if number < len(before):
                turned(before[number])
        for part in before[len(group) :]:
            turned(part)
        if piece == 0:
            back_out[...] = total_final(1, sum_part(1, 0, spot)).astype(jnp.bfloat16)
        back_start(piece)
        for number, part in enumerate(group):
            settled(part)
            if piece == 0 and number < 2:
                weight_grad_ref[number] = sum_part(0, number, spot)
            if piece == pieces - 1 and number == len(group) - 2:
                weight_grad_ref[0] = total_final(0, weight_grad_ref[0])
    for part in groups[-1]:
        turned(part)
    kv_copy.start()
    weight_grad_ref[1] = total_final(2, weight_grad_ref[1])
    weight_put(1).start()
    drain(grads.at[:, :, local_rows(0, pair, core)], near_send)
    for route in range(fars):
        drain(grads.at[:, :, local_rows(0, pair, core)], far_send.at[route])
        drain(grads.at[:, :, local_rows(0, pair, core)], pass_send.at[route])
    for index in range(3):
        drain(outs_t.at[0, :, slice(0, half_rows)], outs_send.at[index])
    drain(share_out, share_send)
    drain(turn_out, turn_send)
    drain(query_grad_ref, query_sem)
    drain(sums_in.at[0], wing_send)
    drain(cross_out, cross_send)
    drain(back_out, back_send)
    for way in ways:

        @pl.when(exists(way))
        def _():
            drain(grads.at[0, :, slice(0, 3 * depth)], line_send.at[(1 - way) // 2])

    drain(back_in, back_recv)
    weight_grad_ref[0] = weight_grad_ref[0] + back_in[...].astype(jnp.float32)
    weight_put(0).start()
    mine = pl.ds(pl.multiple_of(core * half_rows, half_rows), half_rows)
    kv_copy.wait_recv()
    kv_puts = []
    for which, to in enumerate((key_grad_out, value_grad_out)):
        kv_done[which] = (kv_grads[which, mine] + kv_in[which]).astype(jnp.bfloat16)
        kv_puts.append(pltpu.make_async_copy(kv_done.at[which], to, kv_sem.at[which]))
        kv_puts[which].start()
    kv_copy.wait_send()
    drain(weight_grad_ref, put_sem)
    for put in kv_puts:
        put.wait()


def finish_kernel(*refs):
    count = (len(refs) - 1) // 2
    puts = [
        pltpu.make_async_copy(refs[i], refs[count + i], refs[2 * count].at[i]) for i in range(count)
    ]
    for put in puts:
        put.start()
    for put in puts:
        put.wait()


def finish(*values):
    anywhere = pl.BlockSpec(memory_space=pl.ANY)
    return pl.pallas_call(
        finish_kernel,
        out_shape=tuple(pltpu.HBM(value.shape, value.dtype) for value in values),
        in_specs=[anywhere] * len(values),
        out_specs=(anywhere,) * len(values),
        scratch_shapes=[pltpu.SemaphoreType.DMA((len(values),))],
        compiler_params=pltpu.CompilerParams(vmem_limit_bytes=8 * 1024 * 1024),
        name="finish",
    )(*values)


def shards(query_act, rotated_keys, value_input, grad_out, out_weight, doc_lengths):
    dp_count, tensor_count = lax.axis_size("dp"), lax.axis_size("tensor")
    spots = dp_count // 2
    fars = tensor_count // 2 - 1
    seq_len = query_act.shape[1]
    depth, width = out_weight.shape
    half = width // 2
    heads = depth // HEAD_SIZE
    forward_rows, part_rows, back_rows, window, narrow = block_sizes(seq_len, tensor_count)
    parts = seq_len // 2 // part_rows
    pieces = seq_len // tensor_count // part_rows
    dma = pltpu.SemaphoreType.DMA
    anywhere = pl.BlockSpec(memory_space=pl.ANY)
    low, full = jnp.bfloat16, jnp.float32
    kv_shape = pltpu.VMEM((seq_len // 2, HEAD_SIZE), low)
    query_grad, key_grad, value_grad, weight_grad = pl.pallas_call(
        functools.partial(exchange_kernel, dp_count, tensor_count),
        out_shape=(
            pltpu.VMEM((seq_len, depth), low),
            kv_shape,
            kv_shape,
            pltpu.VMEM((depth, width), full),
        ),
        in_specs=[pl.BlockSpec(memory_space=pltpu.HBM)] * 6,
        out_specs=(anywhere,) * 4,
        scratch_shapes=[
            pltpu.VMEM((2, spots, seq_len, half), low),
            pltpu.VMEM((2, spots, 2 * depth, half), low),
            pltpu.VMEM((3, spots, depth, half), low),
            pltpu.VMEM((3, spots + 1, depth, half), low),
            pltpu.VMEM((spots, depth, half), low),
            pltpu.VMEM((spots, depth, half), low),
            pltpu.VMEM((seq_len, 2 * depth), full),
            pltpu.VMEM((seq_len, depth), low),
            pltpu.VMEM((seq_len, HEAD_SIZE), low),
            pltpu.VMEM((seq_len, HEAD_SIZE), low),
            pltpu.VMEM((seq_len, depth), low),
            pltpu.VMEM((2, depth, half), full),
            pltpu.VMEM((heads, seq_len, narrow), full),
            pltpu.VMEM((heads, seq_len // back_rows, narrow, back_rows), low),
            pltpu.VMEM((seq_len, depth), low),
            pltpu.VMEM((depth, seq_len), low),
            pltpu.VMEM((2, depth, seq_len), low),
            pltpu.VMEM((seq_len // 2, 2 * depth), low),
            pltpu.VMEM((seq_len // 2, 2 * depth), low),
            pltpu.VMEM((seq_len // 2, depth), low),
            pltpu.VMEM((2, seq_len // 2, depth), low),
            pltpu.VMEM((depth, half), low),
            pltpu.VMEM((depth, half), low),
            pltpu.VMEM((2, seq_len, HEAD_SIZE), full),
            pltpu.VMEM((2, seq_len // 2, HEAD_SIZE), full),
            pltpu.VMEM((2, seq_len // 2, HEAD_SIZE), low),
            pltpu.SMEM(doc_lengths.shape, jnp.int32),
            dma((3,)),
            dma,
            dma,
            dma((fars,)),
            dma((fars, spots + pieces)),
            dma((fars,)),
            dma((fars, spots + pieces)),
            dma((2,)),
            dma((3, spots)),
            dma((3, spots + 1)),
            dma,
            dma((spots + 1,)),
            dma,
            dma((spots,)),
            dma((3,)),
            dma((3,)),
            dma,
            dma((parts, 2)),
            dma,
            dma((parts,)),
            dma,
            dma,
            dma,
            dma,
            dma((4,)),
            dma,
            dma,
            dma((2,)),
        ],
        compiler_params=pltpu.CompilerParams(
            collective_id=0, has_side_effects=True, vmem_limit_bytes=56 * 1024 * 1024
        ),
        name="exchange",
    )(grad_out[0], out_weight, query_act[0], rotated_keys[0], value_input[0], doc_lengths)
    query_grad, key_grad, value_grad, weight_grad = finish(
        query_grad, key_grad, value_grad, weight_grad
    )
    return (query_grad[None], key_grad[None, None], value_grad[None, None], weight_grad)


def solution(mesh):
    placed = (
        P("dp", None, "tensor"),
        P("dp", None, None),
        P("dp", None, None),
        P("dp", "tensor", None),
        P("tensor", "dp"),
        P("dp", None),
    )
    return jax.shard_map(
        shards,
        mesh=mesh,
        in_specs=placed,
        out_specs=(
            P("dp", None, "tensor"),
            P("dp", "tensor", None, None),
            P("dp", "tensor", None, None),
            P("tensor", "dp"),
        ),
        check_vma=False,
    )
```

```python
import functools

import jax
import jax.numpy as jnp
from jax import lax
from jax.experimental import pallas as pl
from jax.experimental.pallas import tpu as pltpu
from jax.sharding import PartitionSpec as P

HEAD_SIZE = 128


MESH = pl.DeviceIdType.MESH


def block_sizes(seq_len, tensor_count):
    rows = seq_len // tensor_count
    forward_rows = min(256, seq_len)
    part_rows = rows // max(1, rows // 128)
    block_rows = max(part_rows, min(128, 2 * rows))
    return forward_rows, part_rows, block_rows, seq_len // 2 + forward_rows, seq_len // 2 + block_rows


def exchange_kernel(
    dp_count,
    tensor_count,
    grad_ref,
    weight_ref,
    query_full,
    key_full,
    value_full,
    lengths_full,
    query_grad_out,
    key_grad_out,
    value_grad_out,
    weight_grad_out,
    grads,
    weights,
    sums_out,
    sums_in,
    cross_out,
    cross_in,
    accum,
    query_ref,
    key_ref,
    value_ref,
    query_grad_ref,
    weight_grad_ref,
    probs,
    probs_t,
    outs,
    outs_own,
    outs_t,
    share_out,
    share_in,
    turn_out,
    out_grad,
    back_out,
    back_in,
    kv_grads,
    kv_in,
    kv_done,
    lengths_ref,
    own_sem,
    near_send,
    near_recv,
    far_send,
    far_recv,
    pass_send,
    pass_recv,
    line_send,
    line_recv,
    total_recv,
    wing_send,
    wing_recv,
    cross_send,
    cross_recv,
    outs_send,
    outs_recv,
    share_send,
    share_recv,
    turn_send,
    turn_recv,
    back_send,
    back_recv,
    kv_send,
    kv_recv,
    load_sem,
    query_sem,
    put_sem,
    kv_sem,
):
    dp_index = lax.axis_index("dp")
    tensor_index = lax.axis_index("tensor")
    chip_count = tensor_count // 2
    pairs = chip_count // 2
    spots = dp_count // 2
    chip, core = tensor_index // 2, tensor_index % 2
    pair, parity = chip // 2, chip % 2
    mate = (pair * 2 + 1 - parity) * 2 + core
    partner = chip * 2 + 1 - core
    spot, lane = dp_index // 2, dp_index % 2
    twin = spot * 2 + 1 - lane
    rows = grad_ref.shape[0]
    depth, width = weight_ref.shape
    half = width // 2
    seq_len = query_full.shape[0]
    heads = depth // HEAD_SIZE
    half_rows = seq_len // 2
    score_scale = HEAD_SIZE ** (-0.5)
    forward_rows, part_rows, back_rows, window, narrow = block_sizes(seq_len, tensor_count)
    kv_columns = pl.ds(pl.multiple_of(tensor_index // 2 * HEAD_SIZE, HEAD_SIZE), HEAD_SIZE)
    slots = (slice(0, depth), slice(depth, 2 * depth))
    sides = (slice(0, half), slice(half, width))
    chunks = ((0, 0), (0, 1), (1, 0))
    ways = (1, -1)
    routes = [(away, whose) for whose in (1, 0) for away in range(pairs) if away or whose]
    fars = len(routes)
    pieces = rows // part_rows

    def exists(way):
        return spot <= spots - 2 if way > 0 else spot >= 1

    def reaches(way, far):
        return spot + far <= spots - 1 if way > 0 else spot >= far

    def local_rows(whose, which_pair, which_core):
        start = ((whose * pairs + which_pair) * 2 + which_core) * rows
        return pl.ds(pl.multiple_of(start, rows), rows)

    def columns(which_lane, block, side):
        start = (2 * block + which_lane) * width + side * half
        return pl.ds(pl.multiple_of(start, half), half)

    def remote(source, target, send, recv, dp_to, tensor_to):
        return pltpu.make_async_remote_copy(
            source, target, send, recv, device_id=(dp_to, tensor_to), device_id_type=MESH
        )

    def drain(ref, sem):
        pltpu.make_async_copy(ref, ref, sem).wait()

    def own_copy(side, block):
        return pltpu.make_async_copy(
            grad_ref.at[:, columns(lane, block, side)],
            grads.at[side, block, local_rows(0, pair, core)],
            own_sem.at[0],
        )

    def own_weight(side):
        return pltpu.make_async_copy(
            weight_ref.at[:, sides[side]], weights.at[side, spot, slots[0]], own_sem.at[1]
        )

    def near_copy(side, block):
        return remote(
            grad_ref.at[:, columns(lane, block, side)],
            grads.at[side, block, local_rows(0, pair, core)],
            near_send,
            near_recv,
            dp_index,
            partner,
        )

    def far_copy(route, side, block):
        away, whose = routes[route]
        return remote(
            grad_ref.at[:, columns(1 - lane if whose else lane, block, side)],
            grads.at[side, block, local_rows(whose, pair, core)],
            far_send.at[route],
            far_recv.at[route, block],
            twin if whose else dp_index,
            ((pair + away) % pairs * 2 + parity) * 2 + core,
        )

    def source_rows(route, which_core):
        away, whose = routes[route]
        return local_rows(whose, (pair + pairs - away) % pairs, which_core)

    def pass_copy(route, side, block):
        piece = grads.at[side, block, source_rows(route, core)]
        return remote(
            piece, piece, pass_send.at[route], pass_recv.at[route, block], dp_index, partner
        )

    def piece_rows(rows_slice, piece):
        return pl.ds(
            pl.multiple_of(rows_slice.start + piece * part_rows, part_rows), part_rows
        )

    def last_copy(route, piece):
        away, whose = routes[route]
        return remote(
            grad_ref.at[
                slice(piece * part_rows, (piece + 1) * part_rows),
                columns(1 - lane if whose else lane, spot, 0),
            ],
            grads.at[0, spot, piece_rows(local_rows(whose, pair, core), piece)],
            far_send.at[route],
            far_recv.at[route, spots + piece],
            twin if whose else dp_index,
            ((pair + away) % pairs * 2 + parity) * 2 + core,
        )

    def last_pass_copy(route, piece):
        here = grads.at[0, spot, piece_rows(source_rows(route, core), piece)]
        return remote(
            here,
            here,
            pass_send.at[route],
            pass_recv.at[route, spots + piece],
            dp_index,
            partner,
        )

    def line_copy(way, far, chunk):
        side, slot = chunks[chunk]
        block = spot - way * far
        if far == 0 and slot == 0:
            source = weight_ref.at[:, sides[side]]
        else:
            source = weights.at[side, block, slots[slot]]
        return remote(
            source,
            weights.at[side, block, slots[slot]],
            line_send.at[(1 - way) // 2],
            line_recv.at[chunk, block],
            dp_index + 2 * way,
            tensor_index,
        )

    def wing_copy(block, side=1, own=False):
        return remote(
            weight_ref.at[:, sides[side]] if own else weights.at[side, block, slots[0]],
            weights.at[side, block, slots[1]],
            wing_send,
            wing_recv.at[block if side else spots],
            dp_index,
            mate,
        )

    def total_copy(way, far, chunk):
        owner = spot + way * far
        index = spots if way < 0 and far == 1 else owner
        return remote(
            sums_out.at[chunk, owner],
            sums_in.at[chunk, index],
            line_send.at[(1 - way) // 2],
            total_recv.at[chunk, index],
            dp_index + 2 * way,
            tensor_index,
        )

    def cross_copy(block):
        return remote(
            cross_out.at[block],
            cross_in.at[block],
            cross_send,
            cross_recv.at[block],
            dp_index,
            mate,
        )

    def chip_lanes(which_pair, which_parity):
        start = (2 * which_pair + which_parity) * 2 * rows
        return pl.ds(pl.multiple_of(start, 2 * rows), 2 * rows)

    def outs_copy(kind, which_pair):
        here = slice(which_pair * 2 * rows, (which_pair + 1) * 2 * rows)
        there = slice(half_rows + which_pair * 2 * rows, half_rows + (which_pair + 1) * 2 * rows)
        own = outs_own.at[:, chip_lanes(which_pair, parity)]
        if kind == 0:
            return pltpu.make_async_copy(own, outs_t.at[0, :, here], own_sem.at[2])
        if kind == 1:
            other = outs_own.at[:, chip_lanes(which_pair, 1 - parity)]
            return remote(
                other, outs_t.at[1, :, here], outs_send.at[0], outs_recv.at[0], dp_index, mate
            )
        if kind == 2:
            return remote(
                own, outs_t.at[0, :, there], outs_send.at[1], outs_recv.at[1], twin, tensor_index
            )
        return remote(
            outs_t.at[1, :, here],
            outs_t.at[1, :, there],
            outs_send.at[2],
            outs_recv.at[2],
            twin,
            tensor_index,
        )

    parts = [
        (which_pair, which_core, piece)
        for piece in range(rows // part_rows)
        for which_pair in range(pairs)
        for which_core in (0, 1)
    ]

    def part_start(part):
        which_pair, which_core, piece = parts[part]
        return (which_pair * 2 + which_core) * rows + piece * part_rows

    def part_slice(part):
        return slice(part_start(part), part_start(part) + part_rows)

    def share_copy(part, slot):
        here = part_slice(part)
        return remote(
            share_out.at[here, slots[slot]],
            share_in.at[here, slots[slot]],
            share_send,
            share_recv.at[part, slot],
            twin,
            tensor_index,
        )

    def turn_copy(part):
        here = part_slice(part)
        return remote(
            turn_out.at[here], out_grad.at[1, here], turn_send, turn_recv.at[part], dp_index, mate
        )

    def back_copy(part):
        here = slice(part * (depth // len(parts)), (part + 1) * (depth // len(parts)))
        return remote(back_out.at[here], back_in.at[here], back_send, back_recv, dp_index, mate)

    kv_copy = remote(
        kv_grads.at[:, pl.ds(pl.multiple_of((1 - core) * half_rows, half_rows), half_rows)],
        kv_in,
        kv_send,
        kv_recv,
        dp_index,
        partner,
    )

    targets = [(dp_index, partner), (dp_index, mate), (twin, tensor_index)]
    for away in range(1, pairs):
        other = ((pair + away) % pairs * 2 + parity) * 2 + core
        targets += [(dp_index, other), (twin, other)]
    barrier = pltpu.get_barrier_semaphore()
    for target in targets:
        pl.semaphore_signal(barrier, inc=1, device_id=target, device_id_type=MESH)
    for way in ways:

        @pl.when(exists(way))
        def _():
            pl.semaphore_signal(
                barrier,
                inc=1,
                device_id=(dp_index + 2 * way, tensor_index),
                device_id_type=MESH,
            )

    loads = [
        pltpu.make_async_copy(query_full, query_ref, load_sem.at[0]),
        pltpu.make_async_copy(key_full.at[:, kv_columns], key_ref, load_sem.at[1]),
        pltpu.make_async_copy(value_full.at[:, kv_columns], value_ref, load_sem.at[2]),
        pltpu.make_async_copy(lengths_full, lengths_ref, load_sem.at[3]),
    ]
    for load in loads:
        load.start()
    beside = (spot + spots - 2) // (spots - 1) + (2 * spots - 3 - spot) // (spots - 1)
    pl.semaphore_wait(barrier, len(targets) + beside)

    upper = (2 * spot) // spots
    first_block = (1 - upper) * (spots - 1)

    def far_start(block):
        for side in (0, 1):
            for route in range(fars):
                far_copy(route, side, block).start()

    def line_start(chunk):
        for way in ways:

            @pl.when(exists(way))
            def _():
                line_copy(way, 0, chunk).start()

    line_start(2)
    wing_copy(spot, 0, True).start()
    far_start(first_block)
    line_start(0)
    nt = (((1,), (1,)), ((), ()))
    tn = (((0,), (0,)), ((), ()))

    def dot(left, right, dims):
        return lax.dot_general(left, right, dims, preferred_element_type=jnp.float32)

    def first_key(block, block_rows):
        skip, total = half_rows // block_rows, seq_len // block_rows
        past = (block + total - skip) // total
        return past * (block - skip) * block_rows

    def window_keys(index):
        return pl.ds(first_key(index, forward_rows), window)

    def forward(index):
        here = pl.ds(pl.multiple_of(index * forward_rows, forward_rows), forward_rows)
        query_places = index * forward_rows + lax.broadcasted_iota(jnp.int32, (forward_rows, 1), 0)
        key_places = first_key(index, forward_rows) + lax.broadcasted_iota(
            jnp.int32, (forward_rows, window), 1
        )
        doc_start = jnp.zeros((forward_rows, 1), jnp.int32)
        doc_end = jnp.int32(0)
        for doc in range(lengths_ref.shape[1]):
            doc_end = doc_end + lengths_ref[0, doc]
            doc_start = jnp.where(query_places >= doc_end, doc_end, doc_start)
        allowed = (key_places >= doc_start) & (key_places <= query_places)
        keys, values = key_ref[window_keys(index)], value_ref[window_keys(index)]
        for head in range(heads):
            lanes = slice(head * HEAD_SIZE, (head + 1) * HEAD_SIZE)
            scores = dot(query_ref[here, lanes], keys, nt) * score_scale
            scores = jnp.where(allowed, scores, -jnp.inf)
            row_max = jnp.max(scores, axis=1, keepdims=True)
            total = jnp.sum(jnp.exp(scores - row_max), axis=1, keepdims=True)
            prob = jnp.exp(scores - (row_max + jnp.log(total)))
            out = jnp.dot(prob.astype(jnp.bfloat16), values, preferred_element_type=jnp.float32)
            outs[here, lanes] = out.astype(jnp.bfloat16)
            outs_own[lanes, here] = out.T.astype(jnp.bfloat16)
            for part in range(forward_rows // back_rows):
                block = index * (forward_rows // back_rows) + part
                skip = first_key(block, back_rows) - first_key(index, forward_rows)
                piece = prob[part * back_rows : (part + 1) * back_rows, skip : skip + narrow]
                probs[head, block * back_rows : (block + 1) * back_rows] = piece
                probs_t[head, block] = piece.T.astype(jnp.bfloat16)

    def backward(which, start):
        whose = parity if which == 0 else 1 - parity
        place = start // (2 * rows) * 4 * rows + start % (2 * rows)
        block = place // back_rows + whose * (2 * rows // back_rows)
        here = pl.ds(pl.multiple_of(block * back_rows, back_rows), back_rows)
        seen = pl.ds(pl.multiple_of(first_key(block, back_rows), back_rows), narrow)
        keys, values = key_ref[seen], value_ref[seen]
        grads_low, products, deltas, dscores = [], [], [], []
        for head in range(heads):
            lanes = slice(head * HEAD_SIZE, (head + 1) * HEAD_SIZE)
            grad = out_grad[which, start : start + back_rows, lanes]
            grads_low.append(grad)
            products.append(dot(grad, values, nt))
            deltas.append(
                jnp.sum(
                    grad.astype(jnp.float32) * outs[here, lanes].astype(jnp.float32),
                    axis=1,
                    keepdims=True,
                )
            )
        value_total = kv_grads[1, seen]
        for head in range(heads):
            value_total += jnp.dot(
                probs_t[head, block], grads_low[head], preferred_element_type=jnp.float32
            )
        kv_grads[1, seen] = value_total
        for head in range(heads):
            dscore = probs[head, here] * (products[head] - deltas[head]) * score_scale
            dscores.append(dscore.astype(jnp.bfloat16))
        key_total = kv_grads[0, seen]
        for head in range(heads):
            lanes = slice(head * HEAD_SIZE, (head + 1) * HEAD_SIZE)
            key_total += dot(dscores[head], query_ref[here, lanes], tn)
            query_grad_ref[here, lanes] = jnp.dot(
                dscores[head], keys, preferred_element_type=jnp.float32
            ).astype(jnp.bfloat16)
        kv_grads[0, seen] = key_total
        pltpu.make_async_copy(
            query_grad_ref.at[here], query_grad_out.at[here], query_sem
        ).start()

    def project(block, whose, which=(0, 1), piece=None):
        if piece is None:
            areas = [slice(whose * half_rows, (whose + 1) * half_rows)]
        else:
            areas = [
                slice(half_rows + part_start(part), half_rows + part_start(part) + part_rows)
                for part in range(len(parts))
                if parts[part][2] == piece
            ]
        for here in areas:
            total = accum[here]
            for side in which:
                total += dot(grads[side, block, here], weights[side, block], nt)
            accum[here] = total

    def line_hop(far, chunk):
        side, slot = chunks[chunk]
        for way in ways:

            @pl.when(reaches(-way, far))
            def _():
                block = spot - way * far
                drain(weights.at[side, block, slots[slot]], line_recv.at[chunk, block])

                @pl.when(exists(way))
                def _():
                    line_copy(way, far, chunk).start()

                if chunk == 2:
                    wing_copy(block).start()

    def wing_wait(block, side=1):
        drain(weights.at[side, block, slots[1]], wing_recv.at[block if side else spots])

    def hop_project(far):
        for way in ways:

            @pl.when(reaches(-way, far))
            def _():
                wing_wait(spot - way * far)
                project(spot - way * far, 0)

    def far_pass(block, which=(0, 1)):
        for route in range(fars):
            for side in which[:1] if len(which) == 1 else ():
                drain(grads.at[side, block, source_rows(route, core)], far_recv.at[route, block])
            if len(which) == 2:
                drain(grads.at[:, block, source_rows(route, core)], far_recv.at[route, block])
            for side in which:
                pass_copy(route, side, block).start()

    def pass_wait(block, which=(0, 1)):
        for route in range(fars):
            there = source_rows(route, 1 - core)
            if len(which) == 2:
                drain(grads.at[:, block, there], pass_recv.at[route, block])
            else:
                drain(grads.at[which[0], block, there], pass_recv.at[route, block])

    def last_pass(piece):
        for route in range(fars):
            here = piece_rows(source_rows(route, core), piece)
            drain(grads.at[0, spot, here], far_recv.at[route, spots + piece])
            last_pass_copy(route, piece).start()

    def last_wait(piece):
        for route in range(fars):
            here = piece_rows(source_rows(route, 1 - core), piece)
            drain(grads.at[0, spot, here], pass_recv.at[route, spots + piece])

    def sum_part(slot, side, block):
        return jnp.dot(outs_t[slot], grads[side, block], preferred_element_type=jnp.float32)

    def cross(block):
        cross_out[block] = sum_part(1, 1, block).astype(jnp.bfloat16)
        cross_copy(block).start()

    def owner_do(far, work):
        for way in ways:

            @pl.when(reaches(way, far))
            def _():
                work(way, spot + way * far)

    def total_sum(chunk, owner):
        side, slot = chunks[chunk]
        part = sum_part(slot, side, owner) + sums_in[chunk, owner].astype(jnp.float32)
        if side:
            drain(cross_in.at[owner], cross_recv.at[owner])
            part = part + cross_in[owner].astype(jnp.float32)
        sums_out[chunk, owner] = part.astype(jnp.bfloat16)

    def total_step(far, chunk):
        def work(way, owner):
            @pl.when(owner != first_block)
            def _():
                @pl.when(exists(-way))
                def _():
                    drain(sums_in.at[chunk, owner], total_recv.at[chunk, owner])

                total_sum(chunk, owner)
                total_copy(way, far, chunk).start()

        owner_do(far, work)

    def total_first(chunk, at_end):
        edge = spot % (spots - 1)

        @pl.when(edge == 0 if at_end else edge != 0)
        def _():
            if not at_end:
                drain(sums_in.at[chunk, first_block], total_recv.at[chunk, first_block])
            total_sum(chunk, first_block)
            remote(
                sums_out.at[chunk, first_block],
                sums_in.at[chunk, first_block],
                line_send.at[upper],
                total_recv.at[chunk, first_block],
                dp_index + 2 - 4 * upper,
                tensor_index,
            ).start()

    def total_final(chunk, part):
        if chunks[chunk][0]:
            drain(cross_in.at[spot], cross_recv.at[spot])
            part = part + cross_in[spot].astype(jnp.float32)
        for way, index in ((-1, spot), (1, spots)):

            @pl.when(exists(way))
            def _():
                drain(sums_in.at[chunk, index], total_recv.at[chunk, index])

            part = part + sums_in[chunk, index].astype(jnp.float32)
        return part

    def weight_put(side):
        return pltpu.make_async_copy(
            weight_grad_ref.at[side], weight_grad_out.at[:, sides[side]], put_sem
        )

    def share(piece):
        for slot in (1, 0):
            for part in range(len(parts)):
                if parts[part][2] == piece:
                    here = part_slice(part)
                    there = slice(half_rows + here.start, half_rows + here.stop)
                    share_out[here, slots[slot]] = accum[there, slots[slot]].astype(jnp.bfloat16)
                    share_copy(part, slot).start()

    def settle(part, slot):
        here = part_slice(part)
        share_copy(part, slot).wait_recv()
        both = accum[here, slots[slot]] + share_in[here, slots[slot]].astype(jnp.float32)
        if slot:
            turn_out[here] = both.astype(jnp.bfloat16)
            turn_copy(part).start()
        else:
            out_grad[0, here] = both.astype(jnp.bfloat16)

    def finished(part):
        start = part_start(part)
        if back_rows == part_rows:
            return start
        return start - rows if parts[part][1] == 1 else None

    for load in loads:
        load.wait()
    blocks = seq_len // forward_rows
    forward(0)

    @pl.loop(0, spots)
    def _(block):
        for side in (0, 1):
            near_copy(side, block).start()
            own_copy(side, block).start()

    for side in (0, 1):
        own_weight(side).start()
    for index in range(1, blocks):
        forward(index)
    for which_pair in range(pairs):
        outs_copy(1, which_pair).start()
        outs_copy(2, which_pair).start()
        outs_copy(0, which_pair).start()
    wing_copy(spot, 1, True).start()
    line_hop(1, 2)
    wing_wait(spot, 0)
    line_start(1)
    line_hop(1, 0)

    accum[...] = jnp.zeros_like(accum)
    kv_grads[...] = jnp.zeros_like(kv_grads)
    for way in ways:

        @pl.when(reaches(way, spots - 1))
        def _():
            for chunk in range(3):
                for index in range(spots + 1):
                    if index != (spots if way > 0 else spots - 1):
                        sums_in[chunk, index] = jnp.zeros_like(sums_in[chunk, index])

    drain(grads.at[:, :, local_rows(0, pair, core)], own_sem.at[0])
    drain(weights.at[:, spot, slots[0]], own_sem.at[1])
    drain(outs_t.at[0, :, slice(0, half_rows)], own_sem.at[2])
    drain(grads.at[:, :, local_rows(0, pair, 1 - core)], near_recv)
    drain(outs_t.at[1, :, slice(0, half_rows)], outs_recv.at[0])
    for which_pair in range(pairs):
        outs_copy(3, which_pair).start()

    def rest_start(far):
        def work(way, owner):
            if far > 1 or spots == 2:

                @pl.when(owner != first_block)
                def _():
                    far_start(owner)

            else:
                far_start(owner)

        owner_do(far, work)

    for far in range(spots - 1, 0, -1):
        rest_start(far)
    for route in range(fars):
        far_copy(route, 1, spot).start()
    for piece in range(pieces):
        for route in range(fars):
            last_copy(route, piece).start()
    def stage(far, way, where):
        owner = spot + way * far

        @pl.when(reaches(way, far))
        def _():
            @pl.when(owner != first_block)
            def _():
                @pl.when(where)
                def _():
                    far_pass(owner)
                    pass_wait(owner)
                    cross(owner)

    inside = spot % (spots - 1) != 0
    early = spots == 4

    def both_project(far):
        owner_do(far, lambda way, owner: project(owner, 1))

    far_pass(first_block)
    drain(outs_t.at[0, :, slice(half_rows, seq_len)], outs_recv.at[1])
    pass_wait(first_block)
    total_first(0, True)
    line_hop(1, 1)
    drain(outs_t.at[1, :, slice(half_rows, seq_len)], outs_recv.at[2])
    cross(first_block)
    total_first(1, True)
    line_hop(2, 2)
    line_hop(2, 0)
    total_first(0, False)
    wing_wait(spot)
    project(spot, 0)
    total_first(2, True)
    total_first(1, False)
    line_hop(2, 1)
    hop_project(1)
    for far in range(spots - 2, 0, -1):
        hop = spots - far + 1
        for way in ways:
            if early and far == 1 and way > 0:
                stage(far, way, spot % (spots - 1) == 0)
            else:
                stage(far, way, spot >= 0)
        total_step(far, 1)
        total_step(far, 0)
        if far == spots - 2:
            total_first(2, False)
            if early:
                stage(1, 1, inside)
            hop_project(2)
        if far <= spots // 2:
            both_project(far)
        if far == 1:
            far_pass(spot, (1,))
            line_hop(spots - 1, 1)
            hop_project(spots - 1)
            both_project(spots - 1)
            pass_wait(spot, (1,))
            cross(spot)
            project(spot, 1, (1,))
            last_pass(0)
        if hop < spots:
            line_hop(hop, 2)
            line_hop(hop, 0)
        if far > 1:
            total_step(far, 2)
        if hop < spots - 1:
            line_hop(hop, 1)
            hop_project(hop)
            if hop > spots // 2:
                both_project(hop)
    for piece in range(pieces):
        last_wait(piece)
        project(spot, 1, (0,), piece)
        share(piece)
        if piece + 1 < pieces:
            last_pass(piece + 1)

    def turned(part):
        turn_copy(part).wait_recv()
        if finished(part) is not None:
            backward(1, finished(part))

    def settled(part):
        settle(part, 0)
        if finished(part) is not None:
            backward(0, finished(part))

    def back_start(piece):
        for part in range(len(parts)):
            if parts[part][2] == piece:
                back_copy(part).start()

    groups = [
        [part for part in range(len(parts)) if parts[part][2] == piece] for piece in range(pieces)
    ]
    for piece, group in enumerate(groups):
        before = groups[piece - 1] if piece else []
        for number, part in enumerate(group):
            settle(part, 1)
            if piece == 0 and number == 0:
                total_step(1, 2)
            if number < len(before):
                turned(before[number])
        for part in before[len(group) :]:
            turned(part)
        if piece == 0:
            back_out[...] = total_final(1, sum_part(1, 0, spot)).astype(jnp.bfloat16)
        back_start(piece)
        for number, part in enumerate(group):
            settled(part)
            if piece == 0 and number < 2:
                weight_grad_ref[number] = sum_part(0, number, spot)
            if piece == pieces - 1 and number == len(group) - 2:
                weight_grad_ref[0] = total_final(0, weight_grad_ref[0])
    for part in groups[-1]:
        turned(part)
    kv_copy.start()
    weight_grad_ref[1] = total_final(2, weight_grad_ref[1])
    weight_put(1).start()
    drain(grads.at[:, :, local_rows(0, pair, core)], near_send)
    for route in range(fars):
        drain(grads.at[:, :, local_rows(0, pair, core)], far_send.at[route])
        drain(grads.at[:, :, local_rows(0, pair, core)], pass_send.at[route])
    for index in range(3):
        drain(outs_t.at[0, :, slice(0, half_rows)], outs_send.at[index])
    drain(share_out, share_send)
    drain(turn_out, turn_send)
    drain(query_grad_ref, query_sem)
    drain(sums_in.at[0], wing_send)
    drain(cross_out, cross_send)
    drain(back_out, back_send)
    for way in ways:

        @pl.when(exists(way))
        def _():
            drain(grads.at[0, :, slice(0, 3 * depth)], line_send.at[(1 - way) // 2])

    mine = pl.ds(pl.multiple_of(core * half_rows, half_rows), half_rows)
    kv_copy.wait_recv()
    kv_puts = []
    for which, to in enumerate((key_grad_out, value_grad_out)):
        kv_done[which] = (kv_grads[which, mine] + kv_in[which]).astype(jnp.bfloat16)
        kv_puts.append(pltpu.make_async_copy(kv_done.at[which], to, kv_sem.at[which]))
        kv_puts[which].start()
    drain(back_in, back_recv)
    weight_grad_ref[0] = weight_grad_ref[0] + back_in[...].astype(jnp.float32)
    weight_put(0).start()
    kv_copy.wait_send()
    drain(weight_grad_ref, put_sem)
    for put in kv_puts:
        put.wait()


def finish_kernel(*refs):
    count = (len(refs) - 1) // 2
    puts = [
        pltpu.make_async_copy(refs[i], refs[count + i], refs[2 * count].at[i]) for i in range(count)
    ]
    for put in puts:
        put.start()
    for put in puts:
        put.wait()


def finish(*values):
    anywhere = pl.BlockSpec(memory_space=pl.ANY)
    return pl.pallas_call(
        finish_kernel,
        out_shape=tuple(pltpu.HBM(value.shape, value.dtype) for value in values),
        in_specs=[anywhere] * len(values),
        out_specs=(anywhere,) * len(values),
        scratch_shapes=[pltpu.SemaphoreType.DMA((len(values),))],
        compiler_params=pltpu.CompilerParams(vmem_limit_bytes=8 * 1024 * 1024),
        name="finish",
    )(*values)


def shards(query_act, rotated_keys, value_input, grad_out, out_weight, doc_lengths):
    dp_count, tensor_count = lax.axis_size("dp"), lax.axis_size("tensor")
    spots = dp_count // 2
    fars = tensor_count // 2 - 1
    seq_len = query_act.shape[1]
    depth, width = out_weight.shape
    half = width // 2
    heads = depth // HEAD_SIZE
    forward_rows, part_rows, back_rows, window, narrow = block_sizes(seq_len, tensor_count)
    parts = seq_len // 2 // part_rows
    pieces = seq_len // tensor_count // part_rows
    dma = pltpu.SemaphoreType.DMA
    anywhere = pl.BlockSpec(memory_space=pl.ANY)
    low, full = jnp.bfloat16, jnp.float32
    kv_shape = pltpu.VMEM((seq_len // 2, HEAD_SIZE), low)
    query_grad, key_grad, value_grad, weight_grad = pl.pallas_call(
        functools.partial(exchange_kernel, dp_count, tensor_count),
        out_shape=(
            pltpu.VMEM((seq_len, depth), low),
            kv_shape,
            kv_shape,
            pltpu.VMEM((depth, width), full),
        ),
        in_specs=[pl.BlockSpec(memory_space=pltpu.HBM)] * 6,
        out_specs=(anywhere,) * 4,
        scratch_shapes=[
            pltpu.VMEM((2, spots, seq_len, half), low),
            pltpu.VMEM((2, spots, 2 * depth, half), low),
            pltpu.VMEM((3, spots, depth, half), low),
            pltpu.VMEM((3, spots + 1, depth, half), low),
            pltpu.VMEM((spots, depth, half), low),
            pltpu.VMEM((spots, depth, half), low),
            pltpu.VMEM((seq_len, 2 * depth), full),
            pltpu.VMEM((seq_len, depth), low),
            pltpu.VMEM((seq_len, HEAD_SIZE), low),
            pltpu.VMEM((seq_len, HEAD_SIZE), low),
            pltpu.VMEM((seq_len, depth), low),
            pltpu.VMEM((2, depth, half), full),
            pltpu.VMEM((heads, seq_len, narrow), full),
            pltpu.VMEM((heads, seq_len // back_rows, narrow, back_rows), low),
            pltpu.VMEM((seq_len, depth), low),
            pltpu.VMEM((depth, seq_len), low),
            pltpu.VMEM((2, depth, seq_len), low),
            pltpu.VMEM((seq_len // 2, 2 * depth), low),
            pltpu.VMEM((seq_len // 2, 2 * depth), low),
            pltpu.VMEM((seq_len // 2, depth), low),
            pltpu.VMEM((2, seq_len // 2, depth), low),
            pltpu.VMEM((depth, half), low),
            pltpu.VMEM((depth, half), low),
            pltpu.VMEM((2, seq_len, HEAD_SIZE), full),
            pltpu.VMEM((2, seq_len // 2, HEAD_SIZE), full),
            pltpu.VMEM((2, seq_len // 2, HEAD_SIZE), low),
            pltpu.SMEM(doc_lengths.shape, jnp.int32),
            dma((3,)),
            dma,
            dma,
            dma((fars,)),
            dma((fars, spots + pieces)),
            dma((fars,)),
            dma((fars, spots + pieces)),
            dma((2,)),
            dma((3, spots)),
            dma((3, spots + 1)),
            dma,
            dma((spots + 1,)),
            dma,
            dma((spots,)),
            dma((3,)),
            dma((3,)),
            dma,
            dma((parts, 2)),
            dma,
            dma((parts,)),
            dma,
            dma,
            dma,
            dma,
            dma((4,)),
            dma,
            dma,
            dma((2,)),
        ],
        compiler_params=pltpu.CompilerParams(
            collective_id=0, has_side_effects=True, vmem_limit_bytes=56 * 1024 * 1024
        ),
        name="exchange",
    )(grad_out[0], out_weight, query_act[0], rotated_keys[0], value_input[0], doc_lengths)
    query_grad, key_grad, value_grad, weight_grad = finish(
        query_grad, key_grad, value_grad, weight_grad
    )
    return (query_grad[None], key_grad[None, None], value_grad[None, None], weight_grad)


def solution(mesh):
    placed = (
        P("dp", None, "tensor"),
        P("dp", None, None),
        P("dp", None, None),
        P("dp", "tensor", None),
        P("tensor", "dp"),
        P("dp", None),
    )
    return jax.shard_map(
        shards,
        mesh=mesh,
        in_specs=placed,
        out_specs=(
            P("dp", None, "tensor"),
            P("dp", "tensor", None, None),
            P("dp", "tensor", None, None),
            P("tensor", "dp"),
        ),
        check_vma=False,
    )
```
